32 devices in a mesh: seq: 16 (over z, x, core), rep: 2 (over y).
Axes of the slice: x: 2, y: 2, z: 4, core: 2. Of those that a mesh axis runs over, the one named last changes fastest.
Arguments:
- tokens: bfloat16 [2, 4096, 1024], P(None, 'seq'), may hold values from -6 to 6
- cotangent: bfloat16 [2, 4096, 1024], P(None, 'seq'), may hold values from -6 to 6
- domain_ids: int32 [2, 4096], P(None, 'seq'), may hold values from 0 to 7
- domain_counts: int32 [8], replicated, may hold values from 512 to 2047
- domain_weights: float32 [8], replicated, may hold values from 0.5 to 2
- seq_cuts: int32 [2], replicated, may hold values from 1024 to 4096, as said below
- attn_gain: float32 [2, 1024], replicated, may hold values from 0.1 to 1.9
- query_weight: bfloat16 [2, 1024, 1024], replicated, may hold values from -0.1875 to 0.1875
- latent_weight: bfloat16 [2, 1024, 512], replicated, may hold values from -0.1875 to 0.1875
- latent_up: bfloat16 [2, 256, 2048], replicated, may hold values from -0.375 to 0.375
- out_weight: bfloat16 [2, 1024, 1024], replicated, may hold values from -1.5 to 1.5
- out_bias: float32 [2, 1024], replicated, may hold values from -3 to 3
- mlp_gain: float32 [2, 1024], replicated, may hold values from 0.1 to 1.9
- gate_up_matrix: bfloat16 [2, 1024, 5632], replicated, may hold values from -0.1875 to 0.1875
- down_matrix: bfloat16 [2, 2816, 1024], replicated, may hold values from -0.109375 to 0.109375
Outputs:
- output: bfloat16 [2, 4096, 1024], P(None, 'seq')
- input_grad: bfloat16 [2, 4096, 1024], P(None, 'seq')
- attn_gain_grad: float32 [2, 1024], P(None, ('seq', 'rep'))
- query_weight_grad: float32 [2, 1024, 1024], P(None, ('seq', 'rep'))
- latent_weight_grad: float32 [2, 1024, 512], P(None, ('seq', 'rep'))
- latent_up_grad: float32 [2, 256, 2048], P(None, None, ('seq', 'rep'))
- out_weight_grad: float32 [2, 1024, 1024], P(None, None, ('seq', 'rep'))
- out_bias_grad: float32 [2, 1024], P(None, ('seq', 'rep'))
- mlp_gain_grad: float32 [2, 1024], P(None, ('seq', 'rep'))
- gate_up_grad: float32 [2, 1024, 5632], P(None, ('seq', 'rep'))
- down_weight_grad: float32 [2, 2816, 1024], P(None, None, ('seq', 'rep'))
The draws below stay inside these ranges and needn't reach their ends.
Inputs may be any that keep to these rules, and one draw needn't show every extreme that they name: `seq_cuts`: each row holds one sequence before its cut and one from it on; in one row, drawn from the seed, the cut is 4096, so that row is a single sequence.
All inputs are finite; a program needn't handle non-finite values.
Results may differ from the reference program's by a relative error of at most 0.024.
Values may be sent and summed in bfloat16 or wider, within the bound.
No kernel may reach another device: no remote copies, remote signals or barrier semaphores. Data moves between devices by JAX's collectives and lax.ppermute only.
A program may use at most 320 MiB of HBM per device.

```python
import math
import jax
import jax.numpy as jnp
import numpy as np
from jax import lax

D = 1024
HEADS = 16
HD = 64
GROUPS = 2
R = 256
FF = 2816
LAYERS = 2
DOMAINS = 8
LEN = 4096
SEQS = 2
TOKENS = 8192
HH = 1024


def draw_seq_cuts(key, part):
    first_key, second_key = jax.random.split(jax.random.fold_in(key, 17))
    inner_cuts = jax.random.randint(first_key, (SEQS,), LEN // 4, 3 * LEN // 4 + 1)
    whole_row = jax.random.randint(second_key, (), 0, SEQS)
    return jnp.where(jnp.arange(SEQS) == whole_row, LEN, inner_cuts).astype(jnp.int32)


def plant(result, stream_key, low, largest):
    longest = result.shape.index(max(result.shape))
    spots = []
    for shift in (0, 1):
        where = [jax.random.randint(jax.random.fold_in(stream_key, axis), (), 0, length) for axis, length in enumerate(result.shape)]
        where[longest] = (where[longest] + shift) % result.shape[longest]
        spots.append(tuple(where))
    return result.at[spots[0]].set(low).at[spots[1]].set(largest)


def strengthened(values, key, source, target, shards_of, factor):
    def block_of(axis_at):
        return (jnp.arange(values.shape[axis_at]) // (values.shape[axis_at] // shards_of)).reshape((-1,) + (1,) * (values.ndim - 1 - axis_at))

    one_side = jax.random.permutation(key, shards_of)[block_of(target)]
    second = (block_of(target) + shards_of // 2) % shards_of
    return jnp.where((block_of(source) == one_side) | (block_of(source) == second), factor * values, values)


def level_of(own_key, extent, cuts, least, largest):
    gain, own = 1.0, jax.random.fold_in(own_key, 6)
    for position, parts in cuts:
        heights = jnp.exp(jax.random.uniform(jax.random.fold_in(own, position), (parts,), jnp.float32, least / len(cuts), largest / len(cuts)))
        gain = gain * jnp.repeat(heights, extent[position] // parts).reshape([-1 if axis == position else 1 for axis in range(len(extent))])
    return gain


def cumulative_ranks(count, slope):
    portions = [(1 << 20) // math.isqrt(grade ** slope) + 1 for grade in range(1, count + 1)]
    deviation = 1 + sum(portions) // (1 << 30)
    return np.cumsum(np.array([max(1, weight // deviation) for weight in portions]))


def ranked(key, dims, number_of, lean):
    grid = cumulative_ranks(number_of, lean)
    lot = jax.random.randint(jax.random.fold_in(key, 1), dims, 0, int(grid[number_of - 1]))
    rank = jnp.searchsorted(jnp.asarray(grid, jnp.int32), lot, side="right")
    return jax.random.permutation(jax.random.fold_in(key, 2), number_of)[rank].astype(jnp.int32)


def gaussian(stream_key, dims, width, most, cuts=(), held_as=jnp.bfloat16):
    loudness = level_of(stream_key, dims, cuts, -0.22, 0.18) if cuts else 1.0
    drawn = jax.random.normal(stream_key, dims, jnp.float32) * width * loudness
    return jnp.minimum(jnp.maximum(drawn, -most), most).astype(held_as)


def bell_draw_with(stream_key, dims, width, bound, shards, heavy, kind=jnp.bfloat16):
    result = width * jax.random.normal(stream_key, dims, jnp.float32)
    if shards:
        result = result * level_of(stream_key, dims, shards, -0.22, 0.18)
    return jnp.clip(strengthened(result, jax.random.fold_in(stream_key, 3), *heavy), -bound, bound).astype(kind)


def setup_inputs(seed: int = 0) -> dict:
    keys = jax.random.split(jax.random.key(seed), 16)
    return {
        "tokens": gaussian(keys[0], (SEQS, LEN, D), 1.0, 6.0, ((1, 16),)),
        "cotangent": bell_draw_with(keys[1], (SEQS, LEN, D), 1.0, 6.0, ((1, 16),), (1, 2, 16, 2.0)),
        "domain_ids": plant(ranked(keys[2], (SEQS, LEN), DOMAINS, 2), jax.random.fold_in(keys[2], 3), 0, DOMAINS - 1).astype(jnp.int32),
        "domain_counts": plant(jax.random.randint(keys[3], (DOMAINS,), SEQS * LEN // DOMAINS // 2, 2 * SEQS * LEN // DOMAINS), jax.random.fold_in(keys[3], 1), SEQS * LEN // DOMAINS // 2, (2 * SEQS * LEN // DOMAINS) - 1).astype(jnp.int32),
        "domain_weights": jnp.clip(jnp.exp(jax.random.uniform(keys[4], (DOMAINS,), jnp.float32, math.log(0.5), math.log(2.0))), 0.5, 2.0),
        "seq_cuts": draw_seq_cuts(jax.random.fold_in(keys[15], 71), 0),
        "attn_gain": jnp.clip(1.0 + 0.18 * jax.random.normal(keys[6], (LAYERS, D), jnp.float32), 0.1, 1.9),
        "query_weight": gaussian(keys[7], (LAYERS, D, HH), D ** -0.5, 0.1875),
        "latent_weight": gaussian(keys[8], (LAYERS, D, GROUPS * R), D ** -0.5, 0.1875),
        "latent_up": gaussian(keys[9], (LAYERS, R, 2 * HH), R ** -0.5, 0.375),
        "out_weight": gaussian(keys[10], (LAYERS, HH, D), (HD // 4) ** -0.5, 1.5),
        "out_bias": gaussian(keys[11], (LAYERS, D), 0.3, 3.0, (), jnp.float32),
        "mlp_gain": jnp.clip(1.0 + 0.18 * jax.random.normal(keys[12], (LAYERS, D), jnp.float32), 0.1, 1.9),
        "gate_up_matrix": gaussian(keys[13], (LAYERS, D, 2 * FF), D ** -0.5, 0.1875),
        "down_matrix": gaussian(keys[14], (LAYERS, FF, D), FF ** -0.5, 0.109375),
    }


@jax.custom_vjp
def low(v):
    return lax.optimization_barrier(v.astype(jnp.bfloat16)).astype(jnp.float32)

@jax.custom_vjp
def low_back(v):
    return v

def low_keep(v):
    return (low(v), None)

def low_pass(kept, grad):
    return (grad,)

def back_keep(v):
    return (v, None)

def back_low(kept, grad):
    return (low(grad),)
low.defvjp(low_keep, low_pass)
low_back.defvjp(back_keep, back_low)
HIGH_PRECISION = lax.Precision.HIGHEST
NEG_FILL = -1e+30

def rms_scale(value_rows):
    return lax.rsqrt(lax.optimization_barrier(jnp.mean(value_rows * value_rows, axis=-1, keepdims=True)) + 1e-06)

def project(value_rows, weight_factor):
    return jnp.einsum('wnj,jg->wng', value_rows, weight_factor, precision=HIGH_PRECISION)

def attend_sequence(seq_args):
    q_seq, k_seq, v_seq, cut_here = seq_args
    block_rows = min(512, LEN)
    block_count = LEN // block_rows
    col_index = jnp.arange(LEN, dtype=jnp.int32)

    def one_block(block_args):
        q_block, first_row = block_args
        row_index = first_row + jnp.arange(block_rows, dtype=jnp.int32)
        causal_ok = col_index[None, :] <= row_index[:, None]
        same_doc = (row_index[:, None] < cut_here) == (col_index[None, :] < cut_here)
        scores = low_back(jnp.einsum('qhd,khd->hqk', q_block, k_seq, precision=HIGH_PRECISION) * HD ** (-0.5))
        scores = jnp.where((causal_ok & same_doc)[None], scores, NEG_FILL)
        row_max = lax.optimization_barrier(jnp.max(scores, axis=-1, keepdims=True))
        exp_scores = jnp.exp(scores - row_max)
        probs = exp_scores / lax.optimization_barrier(jnp.sum(exp_scores, axis=-1, keepdims=True))
        return jnp.einsum('hqk,khd->qhd', low(probs), v_seq, precision=HIGH_PRECISION)
    block_firsts = jnp.arange(block_count, dtype=jnp.int32) * block_rows
    blocks = lax.map(jax.checkpoint(one_block), (q_seq.reshape(block_count, block_rows, HEADS, HD), block_firsts))
    return blocks.reshape(LEN, HEADS * HD)

def layer_forward(residual_in, attn_gain, query_weight, latent_weight, latent_up, out_weight, out_bias, mlp_gain, gate_up_matrix, down_matrix, seq_cuts):
    normed_attn = low(residual_in * rms_scale(residual_in) * attn_gain)
    queries = low_back(low(project(normed_attn, query_weight)))
    latents = low_back(low(project(normed_attn, latent_weight)))
    lat_groups = latents.reshape(SEQS, LEN, GROUPS, R)
    up_split = latent_up.reshape(R, 2, GROUPS, HEADS // GROUPS * HD)
    keys_all = low_back(low(jnp.einsum('slgr,rgf->slgf', lat_groups, up_split[:, 0], precision=HIGH_PRECISION)))
    vals_all = low_back(low(jnp.einsum('slgr,rgf->slgf', lat_groups, up_split[:, 1], precision=HIGH_PRECISION)))
    heads_raw = lax.map(jax.checkpoint(attend_sequence), (queries.reshape(SEQS, LEN, HEADS, HD), keys_all.reshape(SEQS, LEN, HEADS, HD), vals_all.reshape(SEQS, LEN, HEADS, HD), seq_cuts))
    heads_out = low_back(low(heads_raw))
    attn_branch = low_back(project(heads_out, out_weight) + out_bias)
    hidden_in = residual_in + attn_branch
    normed_mlp = low(hidden_in * rms_scale(hidden_in) * mlp_gain)
    gate_both = project(normed_mlp, gate_up_matrix)
    gate_part = low_back(gate_both[..., :FF])
    up_part = low_back(gate_both[..., FF:])
    hidden_act = low(jax.nn.silu(gate_part) * up_part)
    return hidden_in + low_back(project(hidden_act, down_matrix))

def reference(tokens, cotangent, domain_ids, domain_counts, domain_weights, seq_cuts, attn_gain, query_weight, latent_weight, latent_up, out_weight, out_bias, mlp_gain, gate_up_matrix, down_matrix):

    def forward(residual_in, gains_attn, w_query, w_latent, w_up, w_out, b_out, gains_mlp, w_gate_up, w_down):
        for layer_index in range(LAYERS):
            residual_in = layer_forward(residual_in, gains_attn[layer_index], w_query[layer_index], w_latent[layer_index], w_up[layer_index], w_out[layer_index], b_out[layer_index], gains_mlp[layer_index], w_gate_up[layer_index], w_down[layer_index], seq_cuts)
        return residual_in
    final_state, pullback = jax.vjp(forward, tokens.astype(jnp.float32), attn_gain, query_weight.astype(jnp.float32), latent_weight.astype(jnp.float32), latent_up.astype(jnp.float32), out_weight.astype(jnp.float32), out_bias, mlp_gain, gate_up_matrix.astype(jnp.float32), down_matrix.astype(jnp.float32))
    one_hot = (domain_ids[..., None] == jnp.arange(DOMAINS, dtype=jnp.int32)).astype(jnp.float32)
    per_domain = domain_weights * (TOKENS / DOMAINS) / domain_counts.astype(jnp.float32)
    row_scale = lax.optimization_barrier(jnp.sum(one_hot * per_domain, axis=-1))
    grads = pullback(cotangent.astype(jnp.float32) * row_scale[..., None])
    return (final_state.astype(jnp.bfloat16), grads[0].astype(jnp.bfloat16), grads[1], grads[2], grads[3], grads[4], grads[5], grads[6], grads[7], grads[8], grads[9])
```

```python
import jax
import jax.numpy as jnp
from jax import lax
from jax.sharding import PartitionSpec as P

HD = 64
LAYERS = 2


NEG_FILL = -1e30


def rms_scale(value_rows):
    return lax.rsqrt(jnp.mean(value_rows * value_rows, axis=-1, keepdims=True) + 1e-06)


def norm_back(grad_in, value_rows, scale_rows, gain_vec):
    normed = value_rows * scale_rows
    upstream = grad_in * gain_vec
    return (
        scale_rows * (upstream - normed * jnp.mean(upstream * normed, axis=-1, keepdims=True)),
        grad_in * normed,
    )


def to_heads(value_rows, heads_per):
    seq_rows, loc_len, col_count = value_rows.shape
    head_size = col_count // heads_per
    return (
        value_rows.reshape(seq_rows, loc_len, heads_per, head_size)
        .transpose(0, 2, 1, 3)
        .reshape(seq_rows * heads_per, loc_len, head_size)
    )


def from_heads(value_rows, heads_per):
    piece_count, loc_len, head_size = value_rows.shape
    seq_rows = piece_count // heads_per
    return (
        value_rows.reshape(seq_rows, heads_per, loc_len, head_size)
        .transpose(0, 2, 1, 3)
        .reshape(seq_rows, loc_len, heads_per * head_size)
    )


def shards(
    tokens,
    cotangent,
    domain_ids,
    domain_counts,
    domain_weights,
    seq_cuts,
    attn_gain,
    query_weight,
    latent_weight,
    latent_up,
    out_weight,
    out_bias,
    mlp_gain,
    gate_up_matrix,
    down_matrix,
):
    seq_count = lax.axis_size("seq")
    rep_count = lax.axis_size("rep")
    seq_place = lax.axis_index("seq")
    own_group = lax.axis_index("rep")
    seq_rows, loc_len, width = tokens.shape
    full_len = loc_len * seq_count
    tok_rows = seq_rows * loc_len
    half_rows = tok_rows // rep_count
    half_first = own_group * half_rows
    heads_dim = query_weight.shape[2]
    group_cols = heads_dim // rep_count
    heads_per = group_cols // HD
    latent_size = latent_up.shape[1]
    hidden_size = down_matrix.shape[1]
    att_scale = HD ** (-0.5)
    block_rows = min(512, full_len)
    block_count = full_len // block_rows
    head_global = own_group * heads_per + seq_place % heads_per
    cut_here = seq_cuts[seq_place // heads_per]
    block_firsts = jnp.arange(block_count, dtype=jnp.int32) * block_rows
    col_index = jnp.arange(full_len, dtype=jnp.int32)

    def allowed_rows(first_row):
        row_index = first_row + jnp.arange(block_rows, dtype=jnp.int32)
        causal_ok = col_index[None, :] <= row_index[:, None]
        same_doc = (row_index[:, None] < cut_here) == (col_index[None, :] < cut_here)
        return causal_ok & same_doc

    def flat_all(value_rows):
        return value_rows.reshape(tok_rows, value_rows.shape[-1])

    def own_blocks(value_rows):
        flat = flat_all(value_rows)
        cols = flat.shape[1]
        kept_cols = cols // rep_count
        block = cols // (seq_count * rep_count)
        kept_at = jnp.arange(kept_cols, dtype=jnp.int32)
        source = (kept_at // block * rep_count + own_group) * block + kept_at % block
        pick = (jnp.arange(cols, dtype=jnp.int32)[:, None] == source[None, :]).astype(flat.dtype)
        return jnp.dot(flat, pick, preferred_element_type=jnp.float32).astype(flat.dtype)

    def seq_sum(value_rows):
        return lax.psum_scatter(
            value_rows.astype(jnp.bfloat16), "seq", scatter_dimension=0, tiled=True
        ).astype(jnp.float32)

    def own_half(value_rows):
        both = lax.all_gather(value_rows, "rep", axis=1, tiled=True)
        rows = both.shape[0] // rep_count
        return lax.dynamic_slice_in_dim(both, own_group * rows, rows, 0)

    device_count = seq_count * rep_count
    up_moves = []
    for seq_at in range(seq_count):
        for rep_at in range(rep_count):
            side, inner = divmod(seq_at, seq_count // 2)
            up_moves.append(
                (
                    seq_at * rep_count + rep_at,
                    side * (device_count // 2) + rep_at * (seq_count // 2) + inner,
                )
            )

    def own_rows(value_rows):
        return lax.dynamic_slice_in_dim(flat_all(value_rows), half_first, half_rows, 0)

    domain_total = domain_counts.shape[0]
    all_tokens = seq_rows * full_len
    per_domain = domain_weights * (all_tokens / domain_total) / domain_counts.astype(jnp.float32)
    one_hot = (domain_ids[..., None] == jnp.arange(domain_total, dtype=jnp.int32)).astype(
        jnp.float32
    )
    row_scale = jnp.sum(one_hot * per_domain, axis=-1)
    current = tokens.astype(jnp.float32)
    kept = []
    for layer_index in range(LAYERS):
        r_one = rms_scale(current)
        normed_attn = (current * r_one * attn_gain[layer_index]).astype(jnp.bfloat16)
        query_columns = lax.dynamic_slice_in_dim(
            query_weight[layer_index], own_group * group_cols, group_cols, 1
        )
        latent_columns = lax.dynamic_slice_in_dim(
            latent_weight[layer_index], own_group * latent_size, latent_size, 1
        )
        up_layer = latent_up[layer_index]
        key_cols = lax.dynamic_slice_in_dim(up_layer, own_group * group_cols, group_cols, 1)
        val_cols = lax.dynamic_slice_in_dim(
            up_layer, heads_dim + own_group * group_cols, group_cols, 1
        )
        queries = jnp.dot(normed_attn, query_columns, preferred_element_type=jnp.float32).astype(
            jnp.bfloat16
        )
        latents = jnp.dot(normed_attn, latent_columns, preferred_element_type=jnp.float32).astype(
            jnp.bfloat16
        )
        spread_lat = jnp.broadcast_to(
            latents[:, None], (seq_rows, heads_per, loc_len, latent_size)
        ).reshape(seq_rows * heads_per, loc_len, latent_size)
        q_recv, lat_recv = (
            lax.all_to_all(
                to_heads(queries, heads_per), "seq", split_axis=0, concat_axis=1, tiled=True
            ),
            lax.all_to_all(spread_lat, "seq", split_axis=0, concat_axis=1, tiled=True),
        )
        q_seq = q_recv[0]
        head_keys = lax.dynamic_slice_in_dim(up_layer, head_global * HD, HD, 1)
        head_vals = lax.dynamic_slice_in_dim(up_layer, heads_dim + head_global * HD, HD, 1)
        k_seq = jnp.dot(lat_recv[0], head_keys, preferred_element_type=jnp.float32).astype(
            jnp.bfloat16
        )
        v_seq = jnp.dot(lat_recv[0], head_vals, preferred_element_type=jnp.float32).astype(
            jnp.bfloat16
        )

        def forward_block(block_args, k_seq=k_seq, v_seq=v_seq):
            q_block, first_row = block_args
            scores = (
                jnp.einsum("qd,kd->qk", q_block, k_seq, preferred_element_type=jnp.float32)
                * att_scale
            )
            scores = jnp.where(allowed_rows(first_row), scores, NEG_FILL)
            row_max = jnp.max(scores, axis=-1, keepdims=True)
            exp_scores = jnp.exp(scores - row_max)
            row_sum = jnp.sum(exp_scores, axis=-1, keepdims=True)
            probs_low = (exp_scores / row_sum).astype(jnp.bfloat16)
            head_block = jnp.dot(probs_low, v_seq, preferred_element_type=jnp.float32).astype(
                jnp.bfloat16
            )
            return (head_block, (row_max + jnp.log(row_sum))[:, 0])

        q_blocks = q_seq.reshape(block_count, block_rows, HD)
        head_blocks, log_blocks = lax.map(forward_block, (q_blocks, block_firsts))
        head_seq = head_blocks.reshape(full_len, HD)
        back_heads = lax.all_to_all(head_seq[None], "seq", split_axis=1, concat_axis=0, tiled=True)
        own_heads = from_heads(back_heads, heads_per)
        heads_out = lax.all_gather(own_heads, "rep", axis=2, tiled=True)
        attn_branch = (
            jnp.dot(heads_out, out_weight[layer_index], preferred_element_type=jnp.float32)
            + out_bias[layer_index]
        )
        hidden_in = current + attn_branch
        r_two = rms_scale(hidden_in)
        normed_mlp = (hidden_in * r_two * mlp_gain[layer_index]).astype(jnp.bfloat16)
        gate_both = jnp.dot(
            normed_mlp, gate_up_matrix[layer_index], preferred_element_type=jnp.float32
        )
        gate_part = gate_both[..., :hidden_size]
        up_part = gate_both[..., hidden_size:]
        hidden_act = (jax.nn.silu(gate_part) * up_part).astype(jnp.bfloat16)
        next_state = hidden_in + jnp.dot(
            hidden_act, down_matrix[layer_index], preferred_element_type=jnp.float32
        )
        kept.append(
            (
                current,
                r_one,
                normed_attn,
                latents,
                query_columns,
                latent_columns,
                key_cols,
                val_cols,
                q_blocks,
                k_seq,
                v_seq,
                log_blocks,
                heads_out,
                hidden_in,
                r_two,
                normed_mlp,
                gate_part,
                up_part,
                hidden_act,
            )
        )
        current = next_state
    output = current.astype(jnp.bfloat16)
    grad_state = cotangent.astype(jnp.float32) * row_scale[..., None]
    layer_grads = []
    for layer_index in reversed(range(LAYERS)):
        (
            state_in,
            r_one,
            normed_attn,
            latents,
            query_columns,
            latent_columns,
            key_cols,
            val_cols,
            q_blocks,
            k_seq,
            v_seq,
            log_blocks,
            heads_out,
            hidden_in,
            r_two,
            normed_mlp,
            gate_part,
            up_part,
            hidden_act,
        ) = kept[layer_index]
        feedforward_grad = grad_state.astype(jnp.bfloat16)
        g_down = jnp.einsum(
            "td,tf->df",
            own_blocks(feedforward_grad),
            flat_all(hidden_act),
            preferred_element_type=jnp.float32,
        )
        d_hidden = jnp.einsum(
            "kqm,zm->kqz",
            feedforward_grad,
            down_matrix[layer_index],
            preferred_element_type=jnp.float32,
        )
        sig_gate = jax.nn.sigmoid(gate_part)
        d_gate = (d_hidden * up_part * sig_gate * (1.0 + gate_part * (1.0 - sig_gate))).astype(
            jnp.bfloat16
        )
        d_up = (d_hidden * gate_part * sig_gate).astype(jnp.bfloat16)
        gate_up_cotangent = jnp.concatenate([d_gate, d_up], axis=-1)
        g_gate_up = jnp.einsum(
            "td,tf->df",
            own_blocks(normed_mlp),
            flat_all(gate_up_cotangent),
            preferred_element_type=jnp.float32,
        )
        d_normed_mlp = jnp.einsum(
            "ouz,tz->out",
            gate_up_cotangent,
            gate_up_matrix[layer_index],
            preferred_element_type=jnp.float32,
        )
        d_norm_two, gain_terms_two = norm_back(
            d_normed_mlp, hidden_in, r_two, mlp_gain[layer_index]
        )
        g_mlp_gain = jnp.sum(own_rows(gain_terms_two), axis=0)
        d_hidden_in = grad_state + d_norm_two
        attention_grad = d_hidden_in.astype(jnp.bfloat16)
        g_out = jnp.einsum(
            "td,tf->df",
            own_blocks(attention_grad),
            flat_all(heads_out),
            preferred_element_type=jnp.float32,
        )
        g_bias = jnp.sum(own_rows(attention_grad).astype(jnp.float32), axis=0)
        output_rows = lax.dynamic_slice_in_dim(
            out_weight[layer_index], own_group * group_cols, group_cols, 0
        )
        d_heads = jnp.einsum(
            "kqm,zm->kqz", attention_grad, output_rows, preferred_element_type=jnp.float32
        ).astype(jnp.bfloat16)
        d_heads_seq = lax.all_to_all(
            to_heads(d_heads, heads_per), "seq", split_axis=0, concat_axis=1, tiled=True
        )[0]
        d_head_blocks = d_heads_seq.reshape(block_count, block_rows, HD)

        def backward_block(carry, block_args, k_seq=k_seq, v_seq=v_seq):
            d_keys_acc, d_vals_acc = carry
            q_block, d_block, log_block, first_row = block_args
            scores = (
                jnp.einsum("qd,kd->qk", q_block, k_seq, preferred_element_type=jnp.float32)
                * att_scale
            )
            scores = jnp.where(allowed_rows(first_row), scores, NEG_FILL)
            probs = jnp.exp(scores - log_block[:, None])
            d_probs = jnp.einsum("qd,kd->qk", d_block, v_seq, preferred_element_type=jnp.float32)
            d_vals_acc = d_vals_acc + jnp.einsum(
                "qk,qd->kd", probs.astype(jnp.bfloat16), d_block, preferred_element_type=jnp.float32
            )
            row_delta = jnp.sum(probs * d_probs, axis=-1, keepdims=True)
            d_scores = (probs * (d_probs - row_delta)).astype(jnp.bfloat16)
            d_query_block = (
                jnp.einsum("qk,kd->qd", d_scores, k_seq, preferred_element_type=jnp.float32)
                * att_scale
            ).astype(jnp.bfloat16)
            d_keys_acc = (
                d_keys_acc
                + jnp.einsum("qk,qd->kd", d_scores, q_block, preferred_element_type=jnp.float32)
                * att_scale
            )
            return ((d_keys_acc, d_vals_acc), d_query_block)

        start_acc = jnp.zeros((full_len, HD), jnp.float32)
        (d_keys_acc, d_vals_acc), d_query_blocks = lax.scan(
            backward_block,
            (start_acc, start_acc),
            (q_blocks, d_head_blocks, log_blocks, block_firsts),
        )
        d_query_seq = d_query_blocks.reshape(full_len, HD)
        dq_recv, dk_recv, dv_recv = (
            lax.all_to_all(d_query_seq[None], "seq", split_axis=1, concat_axis=0, tiled=True),
            lax.all_to_all(
                d_keys_acc.astype(jnp.bfloat16)[None],
                "seq",
                split_axis=1,
                concat_axis=0,
                tiled=True,
            ),
            lax.all_to_all(
                d_vals_acc.astype(jnp.bfloat16)[None],
                "seq",
                split_axis=1,
                concat_axis=0,
                tiled=True,
            ),
        )
        query_cotangent = from_heads(dq_recv, heads_per)
        d_keys = from_heads(dk_recv, heads_per)
        d_vals = from_heads(dv_recv, heads_per)
        latent_cotangent = (
            jnp.einsum("slf,rf->slr", d_keys, key_cols, preferred_element_type=jnp.float32)
            + jnp.einsum("slf,rf->slr", d_vals, val_cols, preferred_element_type=jnp.float32)
        ).astype(jnp.bfloat16)
        flat_lat = flat_all(latents)
        g_up_keys = jnp.einsum(
            "tr,tf->rf", flat_lat, flat_all(d_keys), preferred_element_type=jnp.float32
        )
        g_up_vals = jnp.einsum(
            "tr,tf->rf", flat_lat, flat_all(d_vals), preferred_element_type=jnp.float32
        )
        flat_normed = flat_all(normed_attn)
        g_query_own = jnp.einsum(
            "td,tf->df", flat_normed, flat_all(query_cotangent), preferred_element_type=jnp.float32
        )
        g_latent_own = jnp.einsum(
            "td,tf->df", flat_normed, flat_all(latent_cotangent), preferred_element_type=jnp.float32
        )
        partial_part = jnp.einsum(
            "ouz,tz->out", query_cotangent, query_columns, preferred_element_type=jnp.float32
        ) + jnp.einsum(
            "zxm,om->zxo", latent_cotangent, latent_columns, preferred_element_type=jnp.float32
        )
        d_normed_attn = lax.psum(partial_part.astype(jnp.bfloat16), "rep").astype(jnp.float32)
        d_norm_one, gain_terms_one = norm_back(
            d_normed_attn, state_in, r_one, attn_gain[layer_index]
        )
        g_attn_gain = jnp.sum(own_rows(gain_terms_one), axis=0)
        grad_state = d_hidden_in + d_norm_one
        g_up_own = jnp.concatenate([g_up_keys, g_up_vals], axis=1).T
        all_sums = (
            lax.psum_scatter(g_attn_gain, ("seq", "rep"), scatter_dimension=0, tiled=True),
            own_half(seq_sum(g_query_own)),
            own_half(seq_sum(g_latent_own)),
            lax.ppermute(seq_sum(g_up_own), ("seq", "rep"), up_moves).T,
            seq_sum(g_out).T,
            lax.psum_scatter(g_bias, ("seq", "rep"), scatter_dimension=0, tiled=True),
            lax.psum_scatter(g_mlp_gain, ("seq", "rep"), scatter_dimension=0, tiled=True),
            seq_sum(g_gate_up),
            seq_sum(g_down).T,
        )
        layer_grads.insert(0, all_sums)
    stacked = [jnp.stack([grads_one[member] for grads_one in layer_grads]) for member in range(9)]
    return (
        output,
        grad_state.astype(jnp.bfloat16),
        stacked[0],
        stacked[1],
        stacked[2],
        stacked[3],
        stacked[4],
        stacked[5],
        stacked[6],
        stacked[7],
        stacked[8],
    )


def solution(mesh):
    return jax.shard_map(
        shards,
        mesh=mesh,
        in_specs=(
            P(None, "seq", None),
            P(None, "seq", None),
            P(None, "seq"),
            P(),
            P(),
            P(),
            P(),
            P(),
            P(),
            P(),
            P(),
            P(),
            P(),
            P(),
            P(),
        ),
        out_specs=(
            P(None, "seq", None),
            P(None, "seq", None),
            P(None, ("seq", "rep")),
            P(None, ("seq", "rep"), None),
            P(None, ("seq", "rep"), None),
            P(None, None, ("seq", "rep")),
            P(None, None, ("seq", "rep")),
            P(None, ("seq", "rep")),
            P(None, ("seq", "rep")),
            P(None, ("seq", "rep"), None),
            P(None, None, ("seq", "rep")),
        ),
        check_vma=False,
    )
```

```python
import functools

import jax
import jax.numpy as jnp
from jax import lax
from jax.experimental import pallas as pl
from jax.experimental.pallas import tpu as pltpu
from jax.sharding import PartitionSpec as P

HD = 64
LAYERS = 2
GROUPS = 2
NEG_FILL = -1e30
LOG2E = 1.4426950408889634
ATT_SCALE = HD ** (-0.5)
NT = (((1,), (1,)), ((), ()))
TN = (((0,), (0,)), ((), ()))
F32 = jnp.float32
BF16 = jnp.bfloat16
KEY_BLOCK = 512
QUERY_BLOCK = 1024


def dot_as(left, right, dims):
    return lax.dot_general(left, right, dims, preferred_element_type=F32)


def dot(left, right):
    return jnp.dot(left, right, preferred_element_type=F32)


def slot_of(piece, place, seq_count):
    source = piece // 2 if piece % 2 == 0 else (2 * seq_count - 1 - piece) // 2
    return source ^ place


def order_keys(place, lat_ref, keys, keys_t, seq_count, half):
    for piece in range(2 * seq_count):
        slot = slot_of(piece, place, seq_count)
        keys[pl.ds(piece * half, half), :] = lat_ref[0, slot, pl.ds((piece % 2) * half, half), :]
    for first in range(0, 2 * seq_count * half, 256):
        keys_t[:, first : first + 256] = keys[first : first + 256, :].T


def block_bounds(scalars, row, part, half):
    first = scalars[1 + part]
    cut = scalars[3 + row]
    last = first + half - 1
    low_min = jnp.where(first >= cut, cut, 0)
    low_max = jnp.where(last >= cut, cut, 0)
    return first, cut, low_min // KEY_BLOCK, last // KEY_BLOCK + 1, low_max


def hide(scores, block_at, first, cut, half):
    lanes = lax.broadcasted_iota(jnp.int32, (1, scores.shape[1]), 1)
    query_at = first + lanes % half
    low = jnp.where(query_at >= cut, cut, 0)
    key_at = block_at * KEY_BLOCK + lax.broadcasted_iota(jnp.int32, scores.shape, 0)
    return jnp.where((key_at <= query_at) & (key_at >= low), scores, NEG_FILL)


def over_blocks(bounds, block):
    first, _, start, stop, low_max = bounds

    def body(block_at, carry):
        edge = (block_at * KEY_BLOCK + KEY_BLOCK - 1 > first) | (block_at * KEY_BLOCK < low_max)

        @pl.when(edge)
        def _():
            block(block_at, True)

        @pl.when(jnp.logical_not(edge))
        def _():
            block(block_at, False)

        return carry

    lax.fori_loop(start, stop, body, 0)


def attend_kernel(
    scalars,
    q_ref,
    lat_ref,
    up_k_ref,
    up_v_ref,
    out_ref,
    out_t_ref,
    log_ref,
    query_ref,
    mixed_ref,
    keys,
    keys_t,
    top,
    total,
    acc,
    *,
    seq_count,
    half,
    heads,
):
    row, part = pl.program_id(0), pl.program_id(1)

    @pl.when(part == 0)
    def _():
        order_keys(scalars[0], lat_ref, keys, keys_t, seq_count, half)

    for head in range(heads):
        feats = slice(head * HD, (head + 1) * HD)
        lifted = dot_as(q_ref[0, 0, feats, :], up_k_ref[feats, :], TN)
        query_ref[0, 0, head * half : (head + 1) * half, :] = (lifted * (LOG2E * ATT_SCALE)).astype(
            BF16
        )
    top[...] = jnp.full_like(top, NEG_FILL)
    total[...] = jnp.zeros_like(total)
    acc[...] = jnp.zeros_like(acc)
    bounds = block_bounds(scalars, row, part, half)
    columns = heads * half
    width = min(QUERY_BLOCK, columns)

    def block(block_at, edge):
        at = pl.multiple_of(block_at * KEY_BLOCK, KEY_BLOCK)
        key_rows = keys[pl.ds(at, KEY_BLOCK), :]
        key_cols = keys_t[:, pl.ds(at, KEY_BLOCK)]
        for col in range(0, columns, width):
            cols = slice(col, col + width)
            scores = dot_as(key_rows, query_ref[0, 0, cols, :], NT)
            if edge:
                scores = hide(scores, block_at, bounds[0], bounds[1], half)
            old_top = top[:, cols]
            new_top = jnp.maximum(old_top, jnp.max(scores, axis=0, keepdims=True))
            probs = jnp.exp2(scores - new_top)
            fade = jnp.exp2(old_top - new_top)
            total[:, cols] = total[:, cols] * fade + jnp.sum(probs, axis=0, keepdims=True)
            top[:, cols] = new_top
            acc[:, cols] = acc[:, cols] * fade + dot(key_cols, probs.astype(BF16))

    over_blocks(bounds, block)
    mixed_ref[0, 0, :, :] = (acc[...] * (1.0 / total[...])).astype(BF16)
    log_ref[0, 0, :, :] = top[...] + jnp.log2(total[...])
    for head in range(heads):
        feats = slice(head * HD, (head + 1) * HD)
        out_t = dot(
            up_v_ref[feats, :], mixed_ref[0, 0, :, head * half : (head + 1) * half]
        ).astype(BF16)
        out_t_ref[0, 0, feats, :] = out_t
        out_ref[0, 0, :, feats] = out_t.T


def attend_back_kernel(
    scalars,
    q_ref,
    d_out_ref,
    out_ref,
    lat_ref,
    up_k_ref,
    up_v_ref,
    query_ref,
    mixed_ref,
    log_ref,
    dq_ref,
    d_lat_ref,
    d_up_k_ref,
    d_up_v_ref,
    keys,
    keys_t,
    d_keys,
    query_plain,
    d_mixed,
    delta,
    d_query,
    *,
    seq_count,
    half,
    heads,
):
    row, part = pl.program_id(0), pl.program_id(1)

    @pl.when(part == 0)
    def _():
        order_keys(scalars[0], lat_ref, keys, keys_t, seq_count, half)
        d_keys[...] = jnp.zeros_like(d_keys)

    @pl.when((part == 0) & (row == 0))
    def _():
        d_up_k_ref[...] = jnp.zeros_like(d_up_k_ref)
        d_up_v_ref[...] = jnp.zeros_like(d_up_v_ref)

    for head in range(heads):
        feats = slice(head * HD, (head + 1) * HD)
        cols = slice(head * half, (head + 1) * half)
        d_out = d_out_ref[0, 0, feats, :]
        query_plain[cols, :] = (
            dot_as(q_ref[0, 0, feats, :], up_k_ref[feats, :], TN) * ATT_SCALE
        ).astype(BF16)
        d_mixed[cols, :] = dot_as(d_out, up_v_ref[feats, :], TN).astype(BF16)
        delta[:, cols] = jnp.sum(
            d_out.astype(F32) * out_ref[0, 0, feats, :].astype(F32), axis=0, keepdims=True
        )
    d_query[...] = jnp.zeros_like(d_query)
    bounds = block_bounds(scalars, row, part, half)
    columns = heads * half
    width = min(QUERY_BLOCK, columns)

    def block(block_at, edge):
        at = pl.multiple_of(block_at * KEY_BLOCK, KEY_BLOCK)
        key_rows = keys[pl.ds(at, KEY_BLOCK), :]
        key_cols = keys_t[:, pl.ds(at, KEY_BLOCK)]
        key_total = d_keys[pl.ds(at, KEY_BLOCK), :]
        for col in range(0, columns, width):
            cols = slice(col, col + width)
            scores = dot_as(key_rows, query_ref[0, 0, cols, :], NT)
            if edge:
                scores = hide(scores, block_at, bounds[0], bounds[1], half)
            probs = jnp.exp2(scores - log_ref[0, 0, :, cols])
            d_probs = dot_as(key_rows, d_mixed[cols, :], NT)
            d_scores = (probs * (d_probs - delta[:, cols])).astype(BF16)
            key_total = key_total + (
                dot(d_scores, query_plain[cols, :]) + dot(probs.astype(BF16), d_mixed[cols, :])
            )
            d_query[:, cols] += dot(key_cols, d_scores)
        d_keys[pl.ds(at, KEY_BLOCK), :] = key_total

    over_blocks(bounds, block)
    for head in range(heads):
        feats = slice(head * HD, (head + 1) * HD)
        cols = slice(head * half, (head + 1) * half)
        d_lifted = (d_query[:, cols] * ATT_SCALE).astype(BF16)
        dq_ref[0, 0, :, feats] = dot(up_k_ref[feats, :], d_lifted).astype(BF16).T
        d_up_k_ref[feats, :] += dot_as(q_ref[0, 0, feats, :], d_lifted, NT)
        d_up_v_ref[feats, :] += dot_as(d_out_ref[0, 0, feats, :], mixed_ref[0, 0, :, cols], NT)

    @pl.when(part == 1)
    def _():
        for piece in range(2 * seq_count):
            slot = slot_of(piece, scalars[0], seq_count)
            d_lat_ref[0, slot, pl.ds((piece % 2) * half, half), :] = d_keys[
                pl.ds(piece * half, half), :
            ].astype(BF16)


def attention_sizes(queries_t, lats):
    rows, _, feats, half = queries_t.shape
    group_feats = feats // GROUPS
    heads = group_feats // HD
    seq_count, size = lats.shape[1], lats.shape[3]
    return rows, half, group_feats, heads, heads * half, seq_count, size, seq_count * 2 * half


def head_spec(group_feats, half, group):
    return pl.BlockSpec((1, 1, group_feats, half), lambda row, part, _: (row, part, group, 0))


def plain_spec(*block):
    return pl.BlockSpec((1, 1) + block, lambda row, part, _: (row, part, 0, 0))


def up_spec(group_feats, size, at):
    return pl.BlockSpec((group_feats, size), lambda row, part, _: (at, 0))


def attend(scalars, queries_t, lats, up_t, group):
    rows, half, group_feats, heads, columns, seq_count, size, keys = attention_sizes(
        queries_t, lats
    )
    return pl.pallas_call(
        functools.partial(attend_kernel, seq_count=seq_count, half=half, heads=heads),
        grid_spec=pltpu.PrefetchScalarGridSpec(
            num_scalar_prefetch=1,
            grid=(rows, 2),
            in_specs=[
                head_spec(group_feats, half, group),
                pl.BlockSpec((1,) + lats.shape[1:], lambda row, part, _: (row, 0, 0, 0)),
                up_spec(group_feats, size, group),
                up_spec(group_feats, size, GROUPS + group),
            ],
            out_specs=[
                plain_spec(half, group_feats),
                plain_spec(group_feats, half),
                plain_spec(1, columns),
                plain_spec(columns, size),
                plain_spec(size, columns),
            ],
            scratch_shapes=[
                pltpu.VMEM((keys, size), BF16),
                pltpu.VMEM((size, keys), BF16),
                pltpu.VMEM((1, columns), F32),
                pltpu.VMEM((1, columns), F32),
                pltpu.VMEM((size, columns), F32),
            ],
        ),
        out_shape=[
            jax.ShapeDtypeStruct((rows, 2, half, group_feats), BF16),
            jax.ShapeDtypeStruct((rows, 2, group_feats, half), BF16),
            jax.ShapeDtypeStruct((rows, 2, 1, columns), F32),
            jax.ShapeDtypeStruct((rows, 2, columns, size), BF16),
            jax.ShapeDtypeStruct((rows, 2, size, columns), BF16),
        ],
        compiler_params=pltpu.CompilerParams(
            dimension_semantics=("arbitrary", "arbitrary"), vmem_limit_bytes=40 << 20
        ),
        cost_estimate=pl.CostEstimate(
            flops=rows * 2 * columns * keys * size * 2,
            bytes_accessed=rows * (2 * keys * size + 8 * columns * size),
            transcendentals=rows * columns * keys,
        ),
        name="attend",
    )(scalars, queries_t, lats, up_t, up_t)


def attend_back(scalars, queries_t, d_heads_t, heads_t, lats, up_t, kept, group):
    rows, half, group_feats, heads, columns, seq_count, size, keys = attention_sizes(
        queries_t, lats
    )
    logs, lifted, mixed = kept
    lat_spec = pl.BlockSpec((1,) + lats.shape[1:], lambda row, part, _: (row, 0, 0, 0))
    return pl.pallas_call(
        functools.partial(attend_back_kernel, seq_count=seq_count, half=half, heads=heads),
        grid_spec=pltpu.PrefetchScalarGridSpec(
            num_scalar_prefetch=1,
            grid=(rows, 2),
            in_specs=[
                head_spec(group_feats, half, group),
                head_spec(group_feats, half, group),
                plain_spec(group_feats, half),
                lat_spec,
                up_spec(group_feats, size, group),
                up_spec(group_feats, size, GROUPS + group),
                plain_spec(columns, size),
                plain_spec(size, columns),
                plain_spec(1, columns),
            ],
            out_specs=[
                plain_spec(half, group_feats),
                lat_spec,
                up_spec(group_feats, size, 0),
                up_spec(group_feats, size, 0),
            ],
            scratch_shapes=[
                pltpu.VMEM((keys, size), BF16),
                pltpu.VMEM((size, keys), BF16),
                pltpu.VMEM((keys, size), F32),
                pltpu.VMEM((columns, size), BF16),
                pltpu.VMEM((columns, size), BF16),
                pltpu.VMEM((1, columns), F32),
                pltpu.VMEM((size, columns), F32),
            ],
        ),
        out_shape=[
            jax.ShapeDtypeStruct((rows, 2, half, group_feats), BF16),
            jax.ShapeDtypeStruct(lats.shape, BF16),
            jax.ShapeDtypeStruct((group_feats, size), F32),
            jax.ShapeDtypeStruct((group_feats, size), F32),
        ],
        compiler_params=pltpu.CompilerParams(
            dimension_semantics=("arbitrary", "arbitrary"), vmem_limit_bytes=48 << 20
        ),
        cost_estimate=pl.CostEstimate(
            flops=rows * 5 * columns * keys * size * 2,
            bytes_accessed=rows * (4 * keys * size + 12 * columns * size),
            transcendentals=rows * columns * keys,
        ),
        name="attend_back",
    )(scalars, queries_t, d_heads_t, heads_t, lats, up_t, up_t, lifted, mixed, logs)


def rms_scale(value_rows):
    return lax.rsqrt(jnp.mean(value_rows * value_rows, axis=-1, keepdims=True) + 1e-06)


def norm_back(grad_in, value_rows, scale_rows, gain_vec):
    normed = value_rows * scale_rows
    upstream = grad_in * gain_vec
    return (
        scale_rows * (upstream - normed * jnp.mean(upstream * normed, axis=-1, keepdims=True)),
        jnp.sum(grad_in * normed, axis=0),
    )


def hidden_tile(hidden):
    return 256 if hidden % 256 == 0 else hidden


def feed_kernel(
    heads_a,
    heads_b,
    state,
    w_out,
    bias,
    gain,
    next_gain,
    w_gate,
    w_up,
    w_down,
    hidden_in,
    normed_mlp,
    gate,
    up,
    act,
    following,
    normed_next,
):
    step = pl.program_id(0)
    group_cols = heads_a.shape[1]

    @pl.when(step == 0)
    def _():
        value = state[...] + (
            dot(heads_a[...], w_out[0, :group_cols, :])
            + dot(heads_b[...], w_out[0, group_cols:, :])
            + bias[0]
        )
        hidden_in[...] = value
        normed_mlp[...] = (value * rms_scale(value) * gain[0]).astype(BF16)
        following[...] = value

    gate_part = dot(normed_mlp[...], w_gate[0])
    up_part = dot(normed_mlp[...], w_up[0])
    act_part = (gate_part * jax.nn.sigmoid(gate_part) * up_part).astype(BF16)
    gate[...] = gate_part.astype(BF16)
    up[...] = up_part.astype(BF16)
    act[...] = act_part
    following[...] += dot(act_part, w_down[0])

    @pl.when(step == pl.num_programs(0) - 1)
    def _():
        value = following[...]
        normed_next[...] = (value * rms_scale(value) * next_gain[0]).astype(BF16)


def feed(state, heads, layer, next_layer, weights):
    out_weight, out_bias, mlp_gain, attn_gain, gate_up_matrix, down_matrix = weights
    toks, width = state.shape
    hidden = down_matrix.shape[1]
    tile = hidden_tile(hidden)
    steps = hidden // tile
    whole = lambda value: pl.BlockSpec(value.shape, lambda step: (0,) * value.ndim)
    tokens_full = pl.BlockSpec((toks, width), lambda step: (0, 0))
    tokens_tile = pl.BlockSpec((toks, tile), lambda step: (0, step))
    vector = lambda at: pl.BlockSpec((1, 1, width), lambda step: (at, 0, 0))
    wide = lambda dtype: jax.ShapeDtypeStruct((toks, width), dtype)
    tiled = jax.ShapeDtypeStruct((toks, hidden), BF16)
    return pl.pallas_call(
        feed_kernel,
        grid=(steps,),
        in_specs=[
            whole(heads[0]),
            whole(heads[1]),
            tokens_full,
            pl.BlockSpec((1,) + out_weight.shape[1:], lambda step: (layer, 0, 0)),
            vector(layer),
            vector(layer),
            vector(next_layer),
            pl.BlockSpec((1, width, tile), lambda step: (layer, 0, step)),
            pl.BlockSpec((1, width, tile), lambda step: (layer, 0, steps + step)),
            pl.BlockSpec((1, tile, width), lambda step: (layer, step, 0)),
        ],
        out_specs=[
            tokens_full,
            tokens_full,
            tokens_tile,
            tokens_tile,
            tokens_tile,
            tokens_full,
            tokens_full,
        ],
        out_shape=[wide(F32), wide(BF16), tiled, tiled, tiled, wide(F32), wide(BF16)],
        compiler_params=pltpu.CompilerParams(
            dimension_semantics=("arbitrary",), vmem_limit_bytes=36 << 20
        ),
        cost_estimate=pl.CostEstimate(
            flops=2 * toks * width * (3 * hidden + width),
            bytes_accessed=2 * width * (3 * hidden + width) + 6 * toks * hidden,
            transcendentals=toks * hidden,
        ),
        name="feed",
    )(
        heads[0],
        heads[1],
        state,
        out_weight,
        out_bias[:, None],
        mlp_gain[:, None],
        attn_gain[:, None],
        gate_up_matrix,
        gate_up_matrix,
        down_matrix,
    )


def feed_back_kernel(
    grad,
    hidden_in,
    gain,
    w_out,
    gate,
    up,
    w_gate,
    w_up,
    w_down,
    d_gate,
    d_up,
    d_mlp,
    d_hidden_in,
    d_attn,
    d_heads_t,
    gain_sum,
    bias_sum,
    acc,
    *,
    half,
):
    step = pl.program_id(0)

    @pl.when(step == 0)
    def _():
        d_mlp[...] = grad[...].astype(BF16)
        acc[...] = jnp.zeros_like(acc)

    d_act = dot_as(d_mlp[...], w_down[0], NT)
    gate_part = gate[...].astype(F32)
    up_part = up[...].astype(F32)
    sig_gate = jax.nn.sigmoid(gate_part)
    d_gate_part = (d_act * up_part * sig_gate * (1.0 + gate_part * (1.0 - sig_gate))).astype(BF16)
    d_up_part = (d_act * gate_part * sig_gate).astype(BF16)
    d_gate[...] = d_gate_part
    d_up[...] = d_up_part
    acc[...] += dot_as(d_gate_part, w_gate[0], NT) + dot_as(d_up_part, w_up[0], NT)

    @pl.when(step == pl.num_programs(0) - 1)
    def _():
        value = hidden_in[...]
        scale_rows = rms_scale(value)
        d_norm, gain_terms = norm_back(acc[...], value, scale_rows, gain[0])
        gain_sum[...] = gain_terms[None]
        total = grad[...] + d_norm
        low = total.astype(BF16)
        d_hidden_in[...] = total
        d_attn[...] = low
        bias_sum[...] = jnp.sum(low.astype(F32), axis=0, keepdims=True)
        for piece in range(d_heads_t.shape[0]):
            d_heads_t[piece] = dot_as(w_out[0], low[piece * half : (piece + 1) * half], NT).astype(
                BF16
            )


def feed_back(grad, hidden_in, gate, up, layer, half, weights):
    out_weight, _, mlp_gain, _, gate_up_matrix, down_matrix = weights
    toks, width = grad.shape
    heads_dim = out_weight.shape[1]
    hidden = down_matrix.shape[1]
    tile = hidden_tile(hidden)
    steps = hidden // tile
    tokens_full = pl.BlockSpec((toks, width), lambda step: (0, 0))
    tokens_tile = pl.BlockSpec((toks, tile), lambda step: (0, step))
    vector_out = pl.BlockSpec((1, width), lambda step: (0, 0))
    wide = lambda dtype: jax.ShapeDtypeStruct((toks, width), dtype)
    tiled = jax.ShapeDtypeStruct((toks, hidden), BF16)
    pieces = toks // half
    return pl.pallas_call(
        functools.partial(feed_back_kernel, half=half),
        grid=(steps,),
        in_specs=[
            tokens_full,
            tokens_full,
            pl.BlockSpec((1, 1, width), lambda step: (layer, 0, 0)),
            pl.BlockSpec((1,) + out_weight.shape[1:], lambda step: (layer, 0, 0)),
            tokens_tile,
            tokens_tile,
            pl.BlockSpec((1, width, tile), lambda step: (layer, 0, step)),
            pl.BlockSpec((1, width, tile), lambda step: (layer, 0, steps + step)),
            pl.BlockSpec((1, tile, width), lambda step: (layer, step, 0)),
        ],
        out_specs=[
            tokens_tile,
            tokens_tile,
            tokens_full,
            tokens_full,
            tokens_full,
            pl.BlockSpec((pieces, heads_dim, half), lambda step: (0, 0, 0)),
            vector_out,
            vector_out,
        ],
        out_shape=[
            tiled,
            tiled,
            wide(BF16),
            wide(F32),
            wide(BF16),
            jax.ShapeDtypeStruct((pieces, heads_dim, half), BF16),
            jax.ShapeDtypeStruct((1, width), F32),
            jax.ShapeDtypeStruct((1, width), F32),
        ],
        scratch_shapes=[pltpu.VMEM((toks, width), F32)],
        compiler_params=pltpu.CompilerParams(
            dimension_semantics=("arbitrary",), vmem_limit_bytes=36 << 20
        ),
        cost_estimate=pl.CostEstimate(
            flops=2 * toks * width * (3 * hidden + heads_dim),
            bytes_accessed=2 * width * (3 * hidden + heads_dim) + 8 * toks * hidden,
            transcendentals=toks * hidden,
        ),
        name="feed_back",
    )(
        grad,
        hidden_in,
        mlp_gain[:, None],
        out_weight,
        gate,
        up,
        gate_up_matrix,
        gate_up_matrix,
        down_matrix,
    )


def wide_sum_kernel(left_a, left_b, gate_a, gate_b, up_a, up_b, act_a, act_b, total):
    step = pl.program_id(0)
    third = pl.num_programs(0) // 3

    def add(right_a, right_b):
        total[...] = (dot(left_a[0], right_a[...]) + dot(left_b[0], right_b[...])).astype(BF16)

    @pl.when(step < third)
    def _():
        add(gate_a, gate_b)

    @pl.when((step >= third) & (step < 2 * third))
    def _():
        add(up_a, up_b)

    @pl.when(step >= 2 * third)
    def _():
        add(act_a, act_b)


def wide_sum(lefts, gates, ups, acts, columns):
    rows, toks = lefts[0].shape[1:]
    hidden = gates[0].shape[1]
    tile = hidden // 2 if hidden % 256 == 0 else hidden
    third = hidden // tile
    left_spec = pl.BlockSpec((1, rows, toks), lambda step: (step // (2 * third), 0, 0))

    def right_spec(at):
        return pl.BlockSpec(
            (toks, tile), lambda step: (0, jnp.clip(step - at * third, 0, third - 1))
        )

    return pl.pallas_call(
        wide_sum_kernel,
        grid=(3 * third,),
        in_specs=[left_spec] * 2 + [right_spec(at) for at in range(3) for _ in range(2)],
        out_specs=pl.BlockSpec((rows, tile), lambda step: (0, step)),
        out_shape=jax.ShapeDtypeStruct((rows, columns), BF16),
        compiler_params=pltpu.CompilerParams(
            dimension_semantics=("arbitrary",), vmem_limit_bytes=36 << 20
        ),
        cost_estimate=pl.CostEstimate(
            flops=4 * rows * toks * 3 * hidden,
            bytes_accessed=6 * hidden * (2 * toks + rows),
            transcendentals=0,
        ),
        name="wide_sum",
    )(*lefts, *gates, *ups, *acts)


def fill_kernel(left_a, left_b, a_first, a_second, b_first, b_second, _, total):
    step = pl.program_id(0)
    split = pl.num_programs(0) // 2

    @pl.when(step < split)
    def _():
        total[...] = (dot(left_a[...], a_first[...]) + dot(left_b[...], b_first[...])).astype(BF16)

    @pl.when(step >= split)
    def _():
        total[...] = (dot(left_a[...], a_second[...]) + dot(left_b[...], b_second[...])).astype(
            BF16
        )


def fill(lefts, rights, buffer, at):
    rows, toks = lefts[0].shape
    group_cols = rights[0][0].shape[1]
    tile = 256
    split = group_cols // tile
    first = at // tile
    whole = pl.BlockSpec((rows, toks), lambda step: (0, 0))
    spec_a = pl.BlockSpec((toks, tile), lambda step: (0, jnp.minimum(step, split - 1)))
    spec_b = pl.BlockSpec((toks, tile), lambda step: (0, jnp.maximum(step - split, 0)))
    return pl.pallas_call(
        fill_kernel,
        grid=(2 * split,),
        in_specs=[whole] * 2 + [spec_a, spec_b] * 2 + [pl.BlockSpec(memory_space=pl.ANY)],
        out_specs=pl.BlockSpec((rows, tile), lambda step: (0, first + step)),
        out_shape=jax.ShapeDtypeStruct(buffer.shape, buffer.dtype),
        input_output_aliases={6: 0},
        compiler_params=pltpu.CompilerParams(dimension_semantics=("arbitrary",)),
        cost_estimate=pl.CostEstimate(
            flops=8 * rows * toks * group_cols,
            bytes_accessed=8 * group_cols * toks + 4 * rows * group_cols,
            transcendentals=0,
        ),
        name="fill",
    )(*lefts, *rights[0], *rights[1], buffer)


def small_sum_kernel(*refs, count):
    left_a, left_b = refs[:2]
    rights, extra, total = refs[2 : 2 + 2 * count], refs[2 + 2 * count], refs[3 + 2 * count]
    at = 0
    for one in range(count):
        right_a, right_b = rights[one], rights[count + one]
        cols = right_a.shape[1]
        total[:, at : at + cols] = (
            dot(left_a[...], right_a[...]) + dot(left_b[...], right_b[...])
        ).astype(BF16)
        at += cols
    total[:, at:] = extra[...]


def small_sum(lefts, rights, extra):
    rows, toks = lefts[0].shape
    count = len(rights[0])
    cols = sum(value.shape[1] for value in rights[0])
    return pl.pallas_call(
        functools.partial(small_sum_kernel, count=count),
        out_shape=jax.ShapeDtypeStruct((rows, cols + extra.shape[1]), BF16),
        compiler_params=pltpu.CompilerParams(vmem_limit_bytes=36 << 20),
        cost_estimate=pl.CostEstimate(
            flops=4 * rows * toks * cols,
            bytes_accessed=4 * toks * cols + 2 * rows * cols,
            transcendentals=0,
        ),
        name="small_sum",
    )(*lefts, *rights[0], *rights[1], extra)


def shards(
    tokens,
    cotangent,
    domain_ids,
    domain_counts,
    domain_weights,
    seq_cuts,
    attn_gain,
    query_weight,
    latent_weight,
    latent_up,
    out_weight,
    out_bias,
    mlp_gain,
    gate_up_matrix,
    down_matrix,
):
    seq_count = lax.axis_size("seq")
    rep_count = lax.axis_size("rep")
    place = lax.axis_index("seq").astype(jnp.int32)
    side = lax.axis_index("rep").astype(jnp.int32)
    seq_rows, loc_len, width = tokens.shape
    rows = seq_rows // rep_count
    half = loc_len // 2
    toks = rows * loc_len
    heads_dim = query_weight.shape[2]
    size = latent_up.shape[1]
    hidden = down_matrix.shape[1]
    group_cols = heads_dim // GROUPS
    bits = [1 << at for at in range(seq_count.bit_length() - 1)]
    weights = (out_weight, out_bias, mlp_gain, attn_gain, gate_up_matrix, down_matrix)

    def swap_ends(value):
        moves = [(at, seq_count - 1 - at) for at in range(seq_count)]
        return lax.ppermute(value, "seq", moves)

    def across(value):
        return lax.ppermute(value, "rep", [(at, rep_count - 1 - at) for at in range(rep_count)])

    def trade(value, bit):
        return lax.ppermute(value, "seq", [(at, at ^ bit) for at in range(seq_count)])

    def rows_of(value, owner):
        return lax.dynamic_slice_in_dim(value, owner * rows, rows, 0)

    def zigzag(value, owner):
        mine = rows_of(value, owner)
        mine = mine.reshape((rows, 2, half) + mine.shape[2:])
        return jnp.stack([mine[:, 0], swap_ends(mine[:, 1])], axis=1)

    def zigzag_tokens(value, owner):
        return zigzag(value, owner).reshape(toks, value.shape[-1])

    def spread(value):
        value = value[:, None]
        for bit in reversed(bits):
            held = value.shape[1]
            value = jnp.stack([value, trade(value, bit)], axis=2).reshape(
                (rows, 2 * held) + value.shape[2:]
            )
        return value

    def gather_sum(value):
        for bit in bits:
            left = value.shape[1] // 2
            pairs = value.reshape((rows, left, 2) + value.shape[2:])
            got = trade(pairs[:, :, 1], bit)
            value = (pairs[:, :, 0].astype(F32) + got.astype(F32)).astype(BF16)
        return value[:, 0]

    block = width // (seq_count * rep_count)
    kept_rows = seq_count * block
    row_at = jnp.arange(kept_rows, dtype=jnp.int32)
    step_at = row_at // block
    distance = jnp.zeros_like(row_at)
    for level, bit in enumerate(bits):
        distance = distance + (step_at // (seq_count // 2 >> level)) % 2 * bit
    halving_step = place ^ distance
    col_at = jnp.arange(width, dtype=jnp.int32)

    def picker(steps):
        source = (steps * rep_count + side) * block + row_at % block
        return (source[:, None] == col_at[None, :]).astype(BF16)

    pick = picker(step_at)
    pick_halving = picker(halving_step)
    to_halving = (
        (halving_step * block + row_at % block)[:, None] == row_at[None, :]
    ).astype(BF16)

    def picked(picks, value):
        return dot_as(picks, value, NT).astype(BF16)

    def halving_sum(value):
        kept, sent = value[: kept_rows // 2], value[kept_rows // 2 :]
        for bit in bits:
            got = trade(sent, bit)
            if bit == bits[-1]:
                return kept.astype(F32) + got.astype(F32)
            left = kept.shape[0] // 2
            sent = (kept[left:].astype(F32) + got[left:].astype(F32)).astype(BF16)
            kept = (kept[:left].astype(F32) + got[:left].astype(F32)).astype(BF16)

    domain_total = domain_counts.shape[0]
    all_tokens = seq_rows * loc_len * seq_count
    per_domain = domain_weights * (all_tokens / domain_total) / domain_counts.astype(F32)
    one_hot = (domain_ids[..., None] == jnp.arange(domain_total, dtype=jnp.int32)).astype(F32)
    row_scale = jnp.sum(one_hot * per_domain, axis=-1)
    scalars = jnp.concatenate(
        [
            jnp.stack([place, place * loc_len, (2 * seq_count - 1 - 2 * place) * half]),
            rows_of(seq_cuts, side),
        ]
    )

    def project_back(d_hidden_in, dq, d_lat, state, layer):
        d_normed = 0.0
        for group in range(GROUPS):
            d_normed = d_normed + dot_as(
                dq[group],
                query_weight[layer, :, group * group_cols : (group + 1) * group_cols],
                NT,
            )
            d_normed = d_normed + dot_as(
                d_lat[group], latent_weight[layer, :, group * size : (group + 1) * size], NT
            )
        d_norm, g_gain = norm_back(d_normed, state, rms_scale(state), attn_gain[layer])
        return d_hidden_in + d_norm, g_gain

    def first_normed(state):
        return (state * rms_scale(state) * attn_gain[0]).astype(BF16)

    own = zigzag_tokens(tokens, side).astype(F32)
    other = zigzag_tokens(tokens, rep_count - 1 - side).astype(F32)
    normed_own, normed_other = first_normed(own), first_normed(other)
    saved = []
    for layer in range(LAYERS):
        next_layer = min(layer + 1, LAYERS - 1)
        lats = [
            spread(
                dot(normed_own, latent_weight[layer, :, group * size : (group + 1) * size])
                .astype(BF16)
                .reshape(rows, loc_len, size)
            )
            for group in range(GROUPS)
        ]
        queries_t = jnp.einsum(
            "rpid,df->rpfi",
            normed_own.reshape(rows, 2, half, width),
            query_weight[layer],
            preferred_element_type=F32,
        ).astype(BF16)
        up_t = latent_up[layer].T
        heads, attended = [], []
        for group in range(GROUPS):
            out, *rest = attend(scalars, queries_t, lats[group], up_t, group)
            heads.append(out.reshape(toks, group_cols))
            attended.append(rest)
        other_heads = [across(out) for out in heads]
        hidden_own = feed(own, heads, layer, next_layer, weights)
        hidden_other = feed(other, other_heads, layer, next_layer, weights)
        saved.append(
            (
                (own, normed_own, heads, hidden_own),
                (other, normed_other, other_heads, hidden_other),
                (lats, queries_t, up_t, attended),
            )
        )
        own, normed_own = hidden_own[5:]
        other, normed_other = hidden_other[5:]

    def natural(value):
        value = value.reshape(rows, 2, half, width)
        value = jnp.concatenate([value[:, 0], swap_ends(value[:, 1])], axis=1)
        both = jnp.stack([value, across(value)])
        return jnp.where(side == 0, both, both[::-1]).reshape(seq_rows, loc_len, width)

    output = natural(own.astype(BF16))
    grad_own = zigzag_tokens(cotangent, side).astype(F32) * zigzag(row_scale, side).reshape(toks, 1)
    grad_other = zigzag_tokens(cotangent, rep_count - 1 - side).astype(F32) * zigzag(
        row_scale, rep_count - 1 - side
    ).reshape(toks, 1)
    wide_cols = 3 * hidden + heads_dim
    layer_grads = []
    for layer in reversed(range(LAYERS)):
        kept_own, kept_other, (lats, queries_t, up_t, attended) = saved[layer]
        own, normed_own, heads, hidden_own = kept_own
        other, normed_other, other_heads, hidden_other = kept_other
        back_own, back_other = (
            feed_back(grad, kept[0], kept[2], kept[3], layer, half, weights)
            for grad, kept in ((grad_own, hidden_own), (grad_other, hidden_other))
        )
        d_heads_t = back_own[5].reshape(rows, 2, heads_dim, half)
        dq, d_lat, up_k, up_v = [], [], [], []
        for group in range(GROUPS):
            dq_one, d_lat_one, up_k_one, up_v_one = attend_back(
                scalars,
                queries_t,
                d_heads_t,
                attended[group][0],
                lats[group],
                up_t,
                attended[group][1:],
                group,
            )
            dq.append(dq_one.reshape(toks, group_cols))
            d_lat.append(gather_sum(d_lat_one).reshape(toks, size))
            up_k.append(up_k_one)
            up_v.append(up_v_one)
        dq_other = [across(value) for value in dq]
        d_lat_other = [across(value) for value in d_lat]
        grad_own, attn_gain_own = project_back(back_own[3], dq, d_lat, own, layer)
        grad_other, attn_gain_other = project_back(
            back_other[3], dq_other, d_lat_other, other, layer
        )

        backs = (back_own, back_other)
        hiddens = (hidden_own, hidden_other)
        lefts = [
            jnp.stack([picked(pick, hid[1]), picked(pick, back[2])])
            for hid, back in zip(hiddens, backs)
        ]
        wide = wide_sum(
            lefts,
            [back[0] for back in backs],
            [back[1] for back in backs],
            [hid[4] for hid in hiddens],
            wide_cols,
        )
        wide = fill(
            [picked(pick, back[4]) for back in backs], [heads, other_heads], wide, 3 * hidden
        )
        wide = lax.psum_scatter(wide, "seq", scatter_dimension=0, tiled=True).astype(F32)

        up_rows = jnp.concatenate(up_k + up_v, axis=0)
        up_block = up_rows.shape[0] // (seq_count * rep_count)
        up_rows = up_rows.reshape(seq_count, rep_count, up_block, size)
        up_kept = lax.dynamic_index_in_dim(up_rows, side, 1, False)
        up_sent = lax.dynamic_index_in_dim(up_rows, rep_count - 1 - side, 1, False).astype(BF16)
        up_rows = (up_kept + across(up_sent).astype(F32)).astype(BF16)
        folds = up_block // block
        up_rows = jnp.concatenate(
            [up_rows[:, at * block : (at + 1) * block] for at in range(folds)], axis=2
        ).reshape(kept_rows, folds * size)
        up_rows = dot(to_halving, up_rows).astype(BF16)
        normed = [picked(pick_halving, normed_own), picked(pick_halving, normed_other)]
        g_query = halving_sum(small_sum(normed, [dq, dq_other], up_rows))
        vectors = jnp.concatenate(
            [back_own[6] + back_other[6], back_own[7] + back_other[7]]
            + [(attn_gain_own + attn_gain_other)[None]]
            + [jnp.zeros((125, width), F32)]
        ).astype(BF16)
        g_latent = halving_sum(
            small_sum(normed, [d_lat, d_lat_other], picked(pick_halving, vectors))
        )
        g_vectors = g_latent[:, GROUPS * size :]
        g_up = jnp.concatenate(
            [
                g_query[:, heads_dim + at * size : heads_dim + (at + 1) * size]
                for at in range(folds)
            ]
        )
        layer_grads.insert(
            0,
            (
                g_vectors[:, 2],
                g_query[:, :heads_dim],
                g_latent[:, : GROUPS * size],
                g_up.T,
                wide[:, 3 * hidden :].T,
                g_vectors[:, 1],
                g_vectors[:, 0],
                wide[:, : 2 * hidden],
                wide[:, 2 * hidden : 3 * hidden].T,
            ),
        )
    stacked = [jnp.stack([grads[member] for grads in layer_grads]) for member in range(9)]
    return (output, natural(grad_own.astype(BF16)), *stacked)


def solution(mesh):
    rows = P(None, "seq", None)
    scattered = P(None, ("seq", "rep"))
    first = P(None, ("seq", "rep"), None)
    second = P(None, None, ("seq", "rep"))
    return jax.shard_map(
        shards,
        mesh=mesh,
        in_specs=(rows, rows, P(None, "seq")) + (P(),) * 12,
        out_specs=(
            rows,
            rows,
            scattered,
            first,
            first,
            second,
            second,
            scattered,
            scattered,
            first,
            second,
        ),
        check_vma=False,
    )
```

```python
import functools

import jax
import jax.numpy as jnp
from jax import lax
from jax.experimental import pallas as pl
from jax.experimental.pallas import tpu as pltpu
from jax.sharding import PartitionSpec as P

HD = 64
LAYERS = 2
GROUPS = 2
NEG_FILL = -1e30
LOG2E = 1.4426950408889634
ATT_SCALE = HD ** (-0.5)
NT = (((1,), (1,)), ((), ()))
TN = (((0,), (0,)), ((), ()))
F32 = jnp.float32
BF16 = jnp.bfloat16
KEY_BLOCK = 512
QUERY_BLOCK = 1024
FEED_STEP, FEED_AHEAD = 768, 16
BACK_STEP, BACK_AHEAD = 1408, 6


def dot_as(left, right, dims):
    return lax.dot_general(left, right, dims, preferred_element_type=F32)


def dot(left, right):
    return jnp.dot(left, right, preferred_element_type=F32)


def order_keys(scalars, lat_ref, keys, keys_t, seq_count, half):
    for piece in range(2 * seq_count):
        slot = scalars[2 + piece]
        keys[pl.ds(piece * half, half), :] = lat_ref[0, slot, pl.ds((piece % 2) * half, half), :]
    for first in range(0, 2 * seq_count * half, 256):
        keys_t[:, first : first + 256] = keys[first : first + 256, :].T


def block_bounds(scalars, row, part, half, seq_count):
    first = scalars[part]
    cut = scalars[2 + 2 * seq_count + row]
    last = first + half - 1
    low_min = jnp.where(first >= cut, cut, 0)
    low_max = jnp.where(last >= cut, cut, 0)
    return first, cut, low_min // KEY_BLOCK, last // KEY_BLOCK + 1, low_max


def hide(scores, block_at, first, cut, half):
    lanes = lax.broadcasted_iota(jnp.int32, (1, scores.shape[1]), 1)
    query_at = first + lanes % half
    low = jnp.where(query_at >= cut, cut, 0)
    key_at = block_at * KEY_BLOCK + lax.broadcasted_iota(jnp.int32, scores.shape, 0)
    return jnp.where((key_at <= query_at) & (key_at >= low), scores, NEG_FILL)


def over_blocks(bounds, block):
    first, _, start, stop, low_max = bounds

    def body(block_at, carry):
        edge = (block_at * KEY_BLOCK + KEY_BLOCK - 1 > first) | (block_at * KEY_BLOCK < low_max)

        @pl.when(edge)
        def _():
            block(block_at, True)

        @pl.when(jnp.logical_not(edge))
        def _():
            block(block_at, False)

        return carry

    lax.fori_loop(start, stop, body, 0)


def attend_kernel(
    scalars,
    q_ref,
    lat_ref,
    up_k_ref,
    up_v_ref,
    *refs,
    seq_count,
    half,
    heads,
):
    out_ref, out_t_ref, log_ref, query_ref, mixed_ref, keys, keys_t, top, total, acc = refs[-10:]
    row, part = pl.program_id(0), pl.program_id(1)

    @pl.when(part == 0)
    def _():
        order_keys(scalars, lat_ref, keys, keys_t, seq_count, half)

    for head in range(heads):
        feats = slice(head * HD, (head + 1) * HD)
        lifted = dot_as(q_ref[0, 0, feats, :], up_k_ref[feats, :], TN)
        query_ref[0, 0, head * half : (head + 1) * half, :] = (lifted * (LOG2E * ATT_SCALE)).astype(
            BF16
        )
    top[...] = jnp.full_like(top, NEG_FILL)
    total[...] = jnp.zeros_like(total)
    acc[...] = jnp.zeros_like(acc)
    bounds = block_bounds(scalars, row, part, half, seq_count)
    columns = heads * half
    width = min(QUERY_BLOCK, columns)

    def block(block_at, edge):
        at = pl.multiple_of(block_at * KEY_BLOCK, KEY_BLOCK)
        key_rows = keys[pl.ds(at, KEY_BLOCK), :]
        key_cols = keys_t[:, pl.ds(at, KEY_BLOCK)]
        for col in range(0, columns, width):
            cols = slice(col, col + width)
            scores = dot_as(key_rows, query_ref[0, 0, cols, :], NT)
            if edge:
                scores = hide(scores, block_at, bounds[0], bounds[1], half)
            old_top = top[:, cols]
            new_top = jnp.maximum(old_top, jnp.max(scores, axis=0, keepdims=True))
            probs = jnp.exp2(scores - new_top)
            fade = jnp.exp2(old_top - new_top)
            total[:, cols] = total[:, cols] * fade + jnp.sum(probs, axis=0, keepdims=True)
            top[:, cols] = new_top
            acc[:, cols] = acc[:, cols] * fade + dot(key_cols, probs.astype(BF16))

    over_blocks(bounds, block)
    mixed_ref[0, 0, :, :] = (acc[...] * (1.0 / total[...])).astype(BF16)
    log_ref[0, 0, :, :] = top[...] + jnp.log2(total[...])
    for head in range(heads):
        feats = slice(head * HD, (head + 1) * HD)
        out_t = dot(
            up_v_ref[feats, :], mixed_ref[0, 0, :, head * half : (head + 1) * half]
        ).astype(BF16)
        out_t_ref[0, 0, feats, :] = out_t
        out_ref[0, 0, :, feats] = out_t.T


def attend_back_kernel(
    scalars,
    q_ref,
    d_out_ref,
    out_ref,
    lat_ref,
    up_k_ref,
    up_v_ref,
    query_ref,
    mixed_ref,
    log_ref,
    *refs,
    seq_count,
    half,
    heads,
):
    dq_ref, d_lat_ref, d_up_k_ref, d_up_v_ref = refs[-11:-7]
    keys, keys_t, d_keys, query_plain, d_mixed, delta, d_query = refs[-7:]
    row, part = pl.program_id(0), pl.program_id(1)

    @pl.when(part == 0)
    def _():
        order_keys(scalars, lat_ref, keys, keys_t, seq_count, half)
        d_keys[...] = jnp.zeros_like(d_keys)

    @pl.when((part == 0) & (row == 0))
    def _():
        d_up_k_ref[...] = jnp.zeros_like(d_up_k_ref)
        d_up_v_ref[...] = jnp.zeros_like(d_up_v_ref)

    for head in range(heads):
        feats = slice(head * HD, (head + 1) * HD)
        cols = slice(head * half, (head + 1) * half)
        d_out = d_out_ref[0, 0, feats, :]
        query_plain[cols, :] = (
            dot_as(q_ref[0, 0, feats, :], up_k_ref[feats, :], TN) * ATT_SCALE
        ).astype(BF16)
        d_mixed[cols, :] = dot_as(d_out, up_v_ref[feats, :], TN).astype(BF16)
        delta[:, cols] = jnp.sum(
            d_out.astype(F32) * out_ref[0, 0, feats, :].astype(F32), axis=0, keepdims=True
        )
    d_query[...] = jnp.zeros_like(d_query)
    bounds = block_bounds(scalars, row, part, half, seq_count)
    columns = heads * half
    width = min(QUERY_BLOCK, columns)

    def block(block_at, edge):
        at = pl.multiple_of(block_at * KEY_BLOCK, KEY_BLOCK)
        key_rows = keys[pl.ds(at, KEY_BLOCK), :]
        key_cols = keys_t[:, pl.ds(at, KEY_BLOCK)]
        key_total = d_keys[pl.ds(at, KEY_BLOCK), :]
        for col in range(0, columns, width):
            cols = slice(col, col + width)
            scores = dot_as(key_rows, query_ref[0, 0, cols, :], NT)
            if edge:
                scores = hide(scores, block_at, bounds[0], bounds[1], half)
            probs = jnp.exp2(scores - log_ref[0, 0, :, cols])
            d_probs = dot_as(key_rows, d_mixed[cols, :], NT)
            d_scores = (probs * (d_probs - delta[:, cols])).astype(BF16)
            key_total = key_total + (
                dot(d_scores, query_plain[cols, :]) + dot(probs.astype(BF16), d_mixed[cols, :])
            )
            d_query[:, cols] += dot(key_cols, d_scores)
        d_keys[pl.ds(at, KEY_BLOCK), :] = key_total

    over_blocks(bounds, block)
    for head in range(heads):
        feats = slice(head * HD, (head + 1) * HD)
        cols = slice(head * half, (head + 1) * half)
        d_lifted = (d_query[:, cols] * ATT_SCALE).astype(BF16)
        dq_ref[0, 0, :, feats] = dot(up_k_ref[feats, :], d_lifted).astype(BF16).T
        d_up_k_ref[feats, :] += dot_as(q_ref[0, 0, feats, :], d_lifted, NT)
        d_up_v_ref[feats, :] += dot_as(d_out_ref[0, 0, feats, :], mixed_ref[0, 0, :, cols], NT)

    @pl.when(part == 1)
    def _():
        for piece in range(2 * seq_count):
            slot = scalars[2 + piece]
            d_lat_ref[0, slot, pl.ds((piece % 2) * half, half), :] = d_keys[
                pl.ds(piece * half, half), :
            ].astype(BF16)


def attention_sizes(queries_t, lats):
    rows, _, feats, half = queries_t.shape
    group_feats = feats // GROUPS
    heads = group_feats // HD
    seq_count, size = lats.shape[1], lats.shape[3]
    return rows, half, group_feats, heads, heads * half, seq_count, size, seq_count * 2 * half


def head_spec(group_feats, half, group):
    return pl.BlockSpec((1, 1, group_feats, half), lambda row, part, _: (row, part, group, 0))


def token_spec(group_feats, half, group):
    return pl.BlockSpec((1, 1, half, group_feats), lambda row, part, _: (row, part, 0, group))


def lat_spec(lats):
    return pl.BlockSpec((1,) + lats.shape[1:], lambda row, part, _: (row, 0, 0, 0))


ANY = pl.BlockSpec(memory_space=pl.ANY)


def plain_spec(*block):
    return pl.BlockSpec((1, 1) + block, lambda row, part, _: (row, part, 0, 0))


def up_spec(group_feats, size, at):
    return pl.BlockSpec((group_feats, size), lambda row, part, _: (at, 0))


def in_hbm(value):
    return pltpu.with_memory_space_constraint(value, pltpu.HBM)


def attend(scalars, queries_t, lats, up_t, group, filled):
    rows, half, group_feats, heads, columns, seq_count, size, keys = attention_sizes(
        queries_t, lats
    )
    return pl.pallas_call(
        functools.partial(
            attend_kernel, seq_count=seq_count, half=half, heads=heads
        ),
        grid_spec=pltpu.PrefetchScalarGridSpec(
            num_scalar_prefetch=1,
            grid=(rows, 2),
            in_specs=[
                head_spec(group_feats, half, group),
                lat_spec(lats),
                up_spec(group_feats, size, group),
                up_spec(group_feats, size, GROUPS + group),
            ]
            + [ANY] * len(filled),
            out_specs=[
                token_spec(group_feats, half, group),
                plain_spec(group_feats, half),
                plain_spec(1, columns),
                plain_spec(columns, size),
                plain_spec(size, columns),
            ],
            scratch_shapes=[
                pltpu.VMEM((keys, size), BF16),
                pltpu.VMEM((size, keys), BF16),
                pltpu.VMEM((1, columns), F32),
                pltpu.VMEM((1, columns), F32),
                pltpu.VMEM((size, columns), F32),
            ],
        ),
        out_shape=[
            jax.ShapeDtypeStruct((rows, 2, half, GROUPS * group_feats), BF16),
            pltpu.HBM((rows, 2, group_feats, half), BF16),
            pltpu.HBM((rows, 2, 1, columns), F32),
            pltpu.HBM((rows, 2, columns, size), BF16),
            pltpu.HBM((rows, 2, size, columns), BF16),
        ],
        compiler_params=pltpu.CompilerParams(
            dimension_semantics=("arbitrary", "arbitrary"), vmem_limit_bytes=40 << 20
        ),
        cost_estimate=pl.CostEstimate(
            flops=rows * 2 * columns * keys * size * 2,
            bytes_accessed=rows * (2 * keys * size + 8 * columns * size),
            transcendentals=rows * columns * keys,
        ),
        input_output_aliases={5: 0} if filled else {},
        name="attend",
    )(scalars, queries_t, lats, up_t, up_t, *filled)


def attend_back(
    scalars, queries_t, d_heads_t, heads_t, lats, up_t, kept, group, filled
):
    rows, half, group_feats, heads, columns, seq_count, size, keys = attention_sizes(
        queries_t, lats
    )
    logs, lifted, mixed = kept
    return pl.pallas_call(
        functools.partial(
            attend_back_kernel, seq_count=seq_count, half=half, heads=heads
        ),
        grid_spec=pltpu.PrefetchScalarGridSpec(
            num_scalar_prefetch=1,
            grid=(rows, 2),
            in_specs=[
                head_spec(group_feats, half, group),
                head_spec(group_feats, half, group),
                plain_spec(group_feats, half),
                lat_spec(lats),
                up_spec(group_feats, size, group),
                up_spec(group_feats, size, GROUPS + group),
                plain_spec(columns, size),
                plain_spec(size, columns),
                plain_spec(1, columns),
            ]
            + [ANY] * len(filled),
            out_specs=[
                token_spec(group_feats, half, group),
                lat_spec(lats),
                up_spec(group_feats, size, 0),
                up_spec(group_feats, size, 0),
            ],
            scratch_shapes=[
                pltpu.VMEM((keys, size), BF16),
                pltpu.VMEM((size, keys), BF16),
                pltpu.VMEM((keys, size), F32),
                pltpu.VMEM((columns, size), BF16),
                pltpu.VMEM((columns, size), BF16),
                pltpu.VMEM((1, columns), F32),
                pltpu.VMEM((size, columns), F32),
            ],
        ),
        out_shape=[
            jax.ShapeDtypeStruct((rows, 2, half, GROUPS * group_feats), BF16),
            jax.ShapeDtypeStruct(lats.shape, BF16),
            jax.ShapeDtypeStruct((group_feats, size), F32),
            jax.ShapeDtypeStruct((group_feats, size), F32),
        ],
        compiler_params=pltpu.CompilerParams(
            dimension_semantics=("arbitrary", "arbitrary"), vmem_limit_bytes=48 << 20
        ),
        cost_estimate=pl.CostEstimate(
            flops=rows * 5 * columns * keys * size * 2,
            bytes_accessed=rows * (4 * keys * size + 12 * columns * size),
            transcendentals=rows * columns * keys,
        ),
        input_output_aliases={10: 0} if filled else {},
        name="attend_back",
    )(
        scalars,
        *map(
            in_hbm, (queries_t, d_heads_t, heads_t, lats, up_t, up_t, lifted, mixed, logs)
        ),
        *filled,
    )


def rms_scale(value_rows):
    return lax.rsqrt(jnp.mean(value_rows * value_rows, axis=-1, keepdims=True) + 1e-06)


def norm_back(grad_in, value_rows, scale_rows, gain_vec):
    normed = value_rows * scale_rows
    upstream = grad_in * gain_vec
    return (
        scale_rows * (upstream - normed * jnp.mean(upstream * normed, axis=-1, keepdims=True)),
        jnp.sum(grad_in * normed, axis=0),
    )


def hidden_chunks(hidden, step):
    return [(at, min(step, hidden - at)) for at in range(0, hidden, step)]


class Copies:
    def __init__(self, sems, ahead):
        self.sems, self.made, self.begun, self.done, self.ahead = sems, [], 0, 0, ahead

    def add(self, source, target):
        self.made.append(pltpu.make_async_copy(source, target, self.sems.at[len(self.made)]))

    def begin(self, count):
        while self.begun < min(count, len(self.made)):
            self.made[self.begun].start()
            self.begun += 1

    def need(self, count):
        while self.done < count:
            self.made[self.done].wait()
            self.done += 1
            self.begin(self.done + self.ahead)


def feed_kernel(
    heads,
    state,
    bias,
    gain,
    next_gain,
    w_out,
    w_both,
    w_down,
    hidden_in,
    normed_mlp,
    gate,
    up,
    act,
    following,
    normed_next,
    v_heads,
    v_state,
    v_out,
    v_gate_w,
    v_up_w,
    v_down_w,
    v_normed,
    v_gate,
    v_up,
    v_act,
    v_next,
    v_normed_next,
    in_sems,
    out_sems,
    *,
    layer,
    hidden,
):
    chunks = hidden_chunks(hidden, FEED_STEP)
    loads, stores = Copies(in_sems, FEED_AHEAD), Copies(out_sems, 1)
    loads.add(heads, v_heads)
    loads.add(state, v_state)
    loads.add(w_out.at[layer], v_out)
    for at, count in chunks:
        cols = pl.ds(at, count)
        loads.add(w_both.at[layer, :, cols], v_gate_w.at[:, cols])
        loads.add(w_both.at[layer, :, pl.ds(hidden + at, count)], v_up_w.at[:, cols])
        loads.add(w_down.at[layer, cols, :], v_down_w.at[cols, :])
    loads.begin(FEED_AHEAD)
    loads.need(3)

    def store(source, target):
        stores.add(source, target)
        stores.begin(len(stores.made))

    value = v_state[...] + (dot(v_heads[...], v_out[...]) + bias[0])
    v_state[...] = value
    store(v_state, hidden_in)
    normed = (value * rms_scale(value) * gain[0]).astype(BF16)
    v_normed[...] = normed
    store(v_normed, normed_mlp)
    v_next[...] = value
    needed = 3
    for at, count in chunks:
        cols = pl.ds(at, count)
        loads.need(needed + 2)
        gate_part = dot(v_normed[...], v_gate_w[:, cols])
        up_part = dot(v_normed[...], v_up_w[:, cols])
        act_part = (gate_part * jax.nn.sigmoid(gate_part) * up_part).astype(BF16)
        v_gate[:, cols] = gate_part.astype(BF16)
        v_up[:, cols] = up_part.astype(BF16)
        v_act[:, cols] = act_part
        store(v_gate.at[:, cols], gate.at[:, cols])
        store(v_up.at[:, cols], up.at[:, cols])
        store(v_act.at[:, cols], act.at[:, cols])
        needed += 3
        loads.need(needed)
        v_next[...] += dot(act_part, v_down_w[cols, :])
    value = v_next[...]
    store(v_next, following)
    v_normed_next[...] = (value * rms_scale(value) * next_gain[0]).astype(BF16)
    store(v_normed_next, normed_next)
    stores.need(len(stores.made))


def vector_spec(at, width):
    return pl.BlockSpec((1, 1, width), lambda step: (at, 0, 0))


def feed(state, heads, layer, next_layer, weights):
    out_weight, out_bias, mlp_gain, attn_gain, gate_up_matrix, down_matrix = weights
    toks, width = state.shape
    hidden = down_matrix.shape[1]
    count = len(hidden_chunks(hidden, FEED_STEP))
    wide = lambda dtype: jax.ShapeDtypeStruct((toks, width), dtype)
    tiled = jax.ShapeDtypeStruct((toks, hidden), BF16)
    return pl.pallas_call(
        functools.partial(feed_kernel, layer=layer, hidden=hidden),
        grid=(1,),
        in_specs=[ANY] * 2
        + [vector_spec(layer, width), vector_spec(layer, width), vector_spec(next_layer, width)]
        + [ANY] * 3,
        out_specs=[ANY] * 7,
        out_shape=[wide(F32), wide(BF16), tiled, tiled, tiled, wide(F32), wide(BF16)],
        scratch_shapes=[
            pltpu.VMEM(heads.shape, BF16),
            pltpu.VMEM((toks, width), F32),
            pltpu.VMEM(out_weight.shape[1:], BF16),
            pltpu.VMEM((width, hidden), BF16),
            pltpu.VMEM((width, hidden), BF16),
            pltpu.VMEM((hidden, width), BF16),
            pltpu.VMEM((toks, width), BF16),
            pltpu.VMEM((toks, hidden), BF16),
            pltpu.VMEM((toks, hidden), BF16),
            pltpu.VMEM((toks, hidden), BF16),
            pltpu.VMEM((toks, width), F32),
            pltpu.VMEM((toks, width), BF16),
            pltpu.SemaphoreType.DMA((3 + 3 * count,)),
            pltpu.SemaphoreType.DMA((4 + 3 * count,)),
        ],
        compiler_params=pltpu.CompilerParams(
            dimension_semantics=("arbitrary",), vmem_limit_bytes=40 << 20
        ),
        cost_estimate=pl.CostEstimate(
            flops=2 * toks * width * (3 * hidden + width),
            bytes_accessed=2 * width * (3 * hidden + width) + 6 * toks * hidden,
            transcendentals=toks * hidden,
        ),
        name="feed",
    )(
        heads,
        state,
        out_bias[:, None],
        mlp_gain[:, None],
        attn_gain[:, None],
        out_weight,
        gate_up_matrix,
        down_matrix,
    )


def feed_back_kernel(
    grad,
    hidden_in,
    gain,
    gate,
    up,
    w_out,
    w_both,
    w_down,
    d_gate,
    d_up,
    d_mlp,
    d_hidden_in,
    d_attn,
    d_heads_t,
    gain_sum,
    bias_sum,
    v_grad,
    v_hidden_in,
    v_gate,
    v_up,
    v_out,
    v_gate_w,
    v_up_w,
    v_down_w,
    v_d_mlp,
    v_d_attn,
    v_d_heads,
    acc,
    in_sems,
    out_sems,
    *,
    layer,
    hidden,
    half,
):
    chunks = hidden_chunks(hidden, BACK_STEP)
    loads, stores = Copies(in_sems, BACK_AHEAD), Copies(out_sems, 1)
    loads.add(grad, v_grad)
    for at, count in chunks:
        cols = pl.ds(at, count)
        loads.add(gate.at[:, cols], v_gate.at[:, cols])
        loads.add(up.at[:, cols], v_up.at[:, cols])
        loads.add(w_down.at[layer, cols, :], v_down_w.at[cols, :])
        loads.add(w_both.at[layer, :, cols], v_gate_w.at[:, cols])
        loads.add(w_both.at[layer, :, pl.ds(hidden + at, count)], v_up_w.at[:, cols])
    loads.add(hidden_in, v_hidden_in)
    loads.add(w_out.at[layer], v_out)
    loads.begin(BACK_AHEAD)
    loads.need(1)

    def store(source, target):
        stores.add(source, target)
        stores.begin(len(stores.made))

    v_d_mlp[...] = v_grad[...].astype(BF16)
    store(v_d_mlp, d_mlp)
    needed = 1
    for at, count in chunks:
        cols = pl.ds(at, count)
        loads.need(needed + 3)
        d_act = dot_as(v_d_mlp[...], v_down_w[cols, :], NT)
        gate_part = v_gate[:, cols].astype(F32)
        up_part = v_up[:, cols].astype(F32)
        sig_gate = jax.nn.sigmoid(gate_part)
        d_gate_part = (d_act * up_part * sig_gate * (1.0 + gate_part * (1.0 - sig_gate))).astype(
            BF16
        )
        d_up_part = (d_act * gate_part * sig_gate).astype(BF16)
        v_gate[:, cols] = d_gate_part
        v_up[:, cols] = d_up_part
        store(v_gate.at[:, cols], d_gate.at[:, cols])
        store(v_up.at[:, cols], d_up.at[:, cols])
        needed += 5
        loads.need(needed)
        part = dot_as(d_gate_part, v_gate_w[:, cols], NT) + dot_as(d_up_part, v_up_w[:, cols], NT)
        if at == 0:
            acc[...] = part
        else:
            acc[...] += part
    loads.need(needed + 1)
    value = v_hidden_in[...]
    d_norm, gain_terms = norm_back(acc[...], value, rms_scale(value), gain[0])
    gain_sum[...] = gain_terms[None]
    total = v_grad[...] + d_norm
    low = total.astype(BF16)
    v_grad[...] = total
    store(v_grad, d_hidden_in)
    v_d_attn[...] = low
    store(v_d_attn, d_attn)
    bias_sum[...] = jnp.sum(low.astype(F32), axis=0, keepdims=True)
    loads.need(needed + 2)
    for piece in range(d_heads_t.shape[0]):
        v_d_heads[piece] = dot_as(v_out[...], low[piece * half : (piece + 1) * half], NT).astype(
            BF16
        )
    store(v_d_heads, d_heads_t)
    stores.need(len(stores.made))


def feed_back(grad, hidden_in, gate, up, layer, half, weights):
    out_weight, _, mlp_gain, _, gate_up_matrix, down_matrix = weights
    toks, width = grad.shape
    heads_dim = out_weight.shape[1]
    hidden = down_matrix.shape[1]
    vector_out = pl.BlockSpec((1, width), lambda step: (0, 0))
    wide = lambda dtype: jax.ShapeDtypeStruct((toks, width), dtype)
    tiled = jax.ShapeDtypeStruct((toks, hidden), BF16)
    pieces = toks // half
    count = len(hidden_chunks(hidden, BACK_STEP))
    return pl.pallas_call(
        functools.partial(feed_back_kernel, layer=layer, hidden=hidden, half=half),
        grid=(1,),
        in_specs=[ANY, ANY, vector_spec(layer, width)] + [ANY] * 5,
        out_specs=[ANY] * 6 + [vector_out] * 2,
        out_shape=[
            tiled,
            tiled,
            wide(BF16),
            wide(F32),
            wide(BF16),
            jax.ShapeDtypeStruct((pieces, heads_dim, half), BF16),
            jax.ShapeDtypeStruct((1, width), F32),
            jax.ShapeDtypeStruct((1, width), F32),
        ],
        scratch_shapes=[
            pltpu.VMEM((toks, width), F32),
            pltpu.VMEM((toks, width), F32),
            pltpu.VMEM((toks, hidden), BF16),
            pltpu.VMEM((toks, hidden), BF16),
            pltpu.VMEM(out_weight.shape[1:], BF16),
            pltpu.VMEM((width, hidden), BF16),
            pltpu.VMEM((width, hidden), BF16),
            pltpu.VMEM((hidden, width), BF16),
            pltpu.VMEM((toks, width), BF16),
            pltpu.VMEM((toks, width), BF16),
            pltpu.VMEM((pieces, heads_dim, half), BF16),
            pltpu.VMEM((toks, width), F32),
            pltpu.SemaphoreType.DMA((3 + 5 * count,)),
            pltpu.SemaphoreType.DMA((4 + 2 * count,)),
        ],
        compiler_params=pltpu.CompilerParams(
            dimension_semantics=("arbitrary",), vmem_limit_bytes=40 << 20
        ),
        cost_estimate=pl.CostEstimate(
            flops=2 * toks * width * (3 * hidden + heads_dim),
            bytes_accessed=2 * width * (3 * hidden + heads_dim) + 8 * toks * hidden,
            transcendentals=toks * hidden,
        ),
        name="feed_back",
    )(
        grad,
        hidden_in,
        mlp_gain[:, None],
        gate,
        up,
        out_weight,
        gate_up_matrix,
        down_matrix,
    )


def gated_sum_kernel(left_a, left_b, gate_a, gate_b, up_a, up_b, kept, sent):
    half_rows = kept.shape[0]

    def add(right_a, right_b):
        value = (dot(left_a[...], right_a[...]) + dot(left_b[...], right_b[...])).astype(BF16)
        kept[...] = value[:half_rows]
        sent[...] = value[half_rows:]

    first = pl.program_id(0) < pl.num_programs(0) // 2

    @pl.when(first)
    def _():
        add(gate_a, gate_b)

    @pl.when(jnp.logical_not(first))
    def _():
        add(up_a, up_b)


def gated_sum(lefts, gates, ups):
    rows, toks = lefts[0].shape
    hidden = gates[0].shape[1]
    tile = hidden // 2 if hidden % 256 == 0 else hidden
    count = hidden // tile
    whole = pl.BlockSpec((rows, toks), lambda step: (0, 0))
    gate_spec = pl.BlockSpec((toks, tile), lambda step: (0, jnp.minimum(step, count - 1)))
    up_spec_ = pl.BlockSpec((toks, tile), lambda step: (0, jnp.maximum(step - count, 0)))
    return pl.pallas_call(
        gated_sum_kernel,
        grid=(2 * count,),
        in_specs=[whole] * 2 + [gate_spec] * 2 + [up_spec_] * 2,
        out_specs=[pl.BlockSpec((rows // 2, tile), lambda step: (0, step))] * 2,
        out_shape=[jax.ShapeDtypeStruct((rows // 2, 2 * hidden), BF16)] * 2,
        compiler_params=pltpu.CompilerParams(
            dimension_semantics=("arbitrary",), vmem_limit_bytes=36 << 20
        ),
        cost_estimate=pl.CostEstimate(
            flops=8 * rows * toks * hidden,
            bytes_accessed=4 * hidden * (2 * toks + rows),
            transcendentals=0,
        ),
        name="gated_sum",
    )(*lefts, *gates, *ups)


def pair_sum_kernel(*refs, count):
    lefts, rights = refs[: 2 * count], refs[2 * count : 4 * count]
    kept, sent = refs[-2:]
    half_rows = kept.shape[0]
    at = 0
    for one in range(0, 2 * count, 2):
        cols = slice(at, at + rights[one].shape[1])
        value = (
            dot(lefts[one][...], rights[one][...]) + dot(lefts[one + 1][...], rights[one + 1][...])
        ).astype(BF16)
        kept[:, cols] = value[:half_rows]
        sent[:, cols] = value[half_rows:]
        at = cols.stop
    for extra in refs[4 * count : -2]:
        cols = slice(at, at + extra.shape[1])
        kept[:, cols] = extra[:half_rows]
        sent[:, cols] = extra[half_rows:]
        at = cols.stop


def pair_sum(terms, extras=()):
    rows, toks = terms[0][0][0].shape
    cols = sum(rights[0].shape[1] for _, rights in terms)
    total = cols + sum(value.shape[1] for value in extras)
    return pl.pallas_call(
        functools.partial(pair_sum_kernel, count=len(terms)),
        out_shape=[jax.ShapeDtypeStruct((rows // 2, total), BF16)] * 2,
        compiler_params=pltpu.CompilerParams(vmem_limit_bytes=36 << 20),
        cost_estimate=pl.CostEstimate(
            flops=4 * rows * toks * cols,
            bytes_accessed=4 * toks * cols + 2 * rows * total,
            transcendentals=0,
        ),
        name="pair_sum",
    )(*[left for lefts, _ in terms for left in lefts], *[r for _, rights in terms for r in rights], *extras)


class HalvingSum:
    def __init__(self, trade, pair, order, begin=True):
        self.trade, self.order, self.step = trade, order, 1
        self.kept, self.sent = pair
        self.got = self.result = None
        if begin:
            self.got = trade(self.sent, order[0])

    def advance_first(self, gate):
        (self.kept, self.sent), _ = lax.optimization_barrier(((self.kept, self.sent), gate))
        self.got = self.trade(self.sent, self.order[0])

    def advance(self, gate=None):
        if self.result is not None:
            return
        kept, got = self.kept, self.got
        if gate is not None:
            (kept, got), _ = lax.optimization_barrier(((kept, got), gate))
        if self.step == len(self.order):
            self.result = kept.astype(F32) + got.astype(F32)
            return
        left = kept.shape[0] // 2
        self.sent = (kept[left:].astype(F32) + got[left:].astype(F32)).astype(BF16)
        self.kept = (kept[:left].astype(F32) + got[:left].astype(F32)).astype(BF16)
        self.got = self.trade(self.sent, self.order[self.step])
        self.step += 1

    def finish(self):
        while self.result is None:
            self.advance()
        return self.result


class SlotSum:
    def __init__(self, trade, value, order):
        self.trade, self.value, self.order, self.step = trade, value, order, 0
        self.send()

    def send(self):
        left = self.value.shape[1] // 2
        self.kept, self.sent = self.value[:, :left], self.value[:, left:]
        self.got = self.trade(self.sent, self.order[self.step])
        self.step += 1

    def advance(self, gate):
        if self.got is None:
            return
        kept, got = self.kept, self.got
        if gate is not None:
            (kept, got), _ = lax.optimization_barrier(((kept, got), gate))
        self.value = (kept.astype(F32) + got.astype(F32)).astype(BF16)
        self.got = None
        if self.step < len(self.order):
            self.send()
        else:
            self.sent = self.value


def shards(
    tokens,
    cotangent,
    domain_ids,
    domain_counts,
    domain_weights,
    seq_cuts,
    attn_gain,
    query_weight,
    latent_weight,
    latent_up,
    out_weight,
    out_bias,
    mlp_gain,
    gate_up_matrix,
    down_matrix,
):
    seq_count = lax.axis_size("seq")
    rep_count = lax.axis_size("rep")
    place = lax.axis_index("seq").astype(jnp.int32)
    side = lax.axis_index("rep").astype(jnp.int32)
    seq_rows, loc_len, width = tokens.shape
    rows = seq_rows // rep_count
    half = loc_len // 2
    toks = rows * loc_len
    heads_dim = query_weight.shape[2]
    size = latent_up.shape[1]
    hidden = down_matrix.shape[1]
    group_cols = heads_dim // GROUPS
    bits = [1 << at for at in range(seq_count.bit_length() - 1)]
    far_late = bits[:1] + bits[2:3] + bits[1:2] + bits[3:]
    weights = (out_weight, out_bias, mlp_gain, attn_gain, gate_up_matrix, down_matrix)

    def after(value, gate):
        return lax.optimization_barrier((value, gate))[0]

    def swap_ends(value):
        moves = [(at, seq_count - 1 - at) for at in range(seq_count)]
        return lax.ppermute(value, "seq", moves)

    def across(value):
        return lax.ppermute(value, "rep", [(at, rep_count - 1 - at) for at in range(rep_count)])

    def trade(value, bit):
        return lax.ppermute(value, "seq", [(at, at ^ bit) for at in range(seq_count)])

    def rows_of(value, owner):
        return lax.dynamic_slice_in_dim(value, owner * rows, rows, 0)

    def turned(value):
        split = value.reshape((rows, 2, half) + value.shape[1:])
        return jnp.stack([split[:, 0], swap_ends(split[:, 1])], axis=1).reshape(value.shape)

    def tokens_of(value, owner):
        return rows_of(value, owner).reshape((toks,) + value.shape[2:])

    def spread(values, fill_at, fill):
        values = [value.reshape(rows, 1, loc_len, size) for value in values]
        filled = None
        for at, bit in enumerate(reversed(bits)):
            got = [trade(value, bit) for value in values]
            if at == fill_at:
                filled = fill(values)
                values, got = after((values, got), filled)
            values = [jnp.concatenate(pair, axis=1) for pair in zip(values, got)]
        return values, filled

    block = width // (seq_count * rep_count)
    kept_rows = seq_count * block
    row_at = jnp.arange(kept_rows, dtype=jnp.int32)
    col_at = jnp.arange(width, dtype=jnp.int32)

    def halving_step(order):
        distance = jnp.zeros_like(row_at)
        for level, bit in enumerate(order):
            distance = distance + (row_at // block // (seq_count // 2 >> level)) % 2 * bit
        return place ^ distance

    def picker(order, owner):
        source = (halving_step(order) * rep_count + owner) * block + row_at % block
        return (source[:, None] == col_at[None, :]).astype(BF16)

    pick, pick_late = picker(bits, side), picker(far_late, side)
    pick_other = picker(bits, rep_count - 1 - side)
    vector_at = jnp.arange(128, dtype=jnp.int32)[:, None]
    to_halving = (
        (halving_step(bits) * block + row_at % block)[:, None] == row_at[None, :]
    ).astype(BF16)

    def picked(picks, value):
        return dot_as(picks, value, NT).astype(BF16)

    domain_total = domain_counts.shape[0]
    all_tokens = seq_rows * loc_len * seq_count
    per_domain = domain_weights * (all_tokens / domain_total) / domain_counts.astype(F32)
    one_hot = (domain_ids[..., None] == jnp.arange(domain_total, dtype=jnp.int32)).astype(F32)
    row_scale = jnp.sum(one_hot * per_domain, axis=-1)
    pieces = jnp.arange(2 * seq_count, dtype=jnp.int32)

    def scalars_of(zigzag):
        source = pieces // 2
        if zigzag:
            source = jnp.where(pieces % 2 == 0, source, (2 * seq_count - 1 - pieces) // 2)
        distance = source ^ place
        slots = jnp.zeros_like(pieces)
        for level, bit in enumerate(bits):
            slots = slots + distance // bit % 2 * (seq_count // 2 >> level)
        starts = jnp.stack([place * loc_len, (2 * seq_count - 1 - 2 * place) * half])
        return jnp.concatenate([starts, slots, rows_of(seq_cuts, side)])

    def project_back(d_hidden_in, dq, d_lat, state, layer):
        d_normed = dot_as(dq, query_weight[layer], NT) + dot_as(d_lat, latent_weight[layer], NT)
        d_norm, g_gain = norm_back(d_normed, state, rms_scale(state), attn_gain[layer])
        return d_hidden_in + d_norm, g_gain

    def grad_of(owner, gate):
        value = tokens_of(cotangent, owner).astype(F32) * tokens_of(row_scale, owner)[:, None]
        split = value.reshape(rows, 2, half, width)
        swapped = swap_ends(after(split[:, 1].astype(BF16), gate))
        return jnp.stack([split[:, 0], swapped.astype(F32)], axis=1).reshape(toks, width)

    def first_normed(state):
        return (state * rms_scale(state) * attn_gain[0]).astype(BF16)

    natural_own = tokens_of(tokens, side)
    natural_normed = [first_normed(natural_own.astype(F32))]
    hidden_other = None
    saved = []
    for layer in range(LAYERS):
        last = layer == LAYERS - 1
        next_layer = min(layer + 1, LAYERS - 1)
        scalars = scalars_of(layer > 0)
        lat_input = normed_own if layer else natural_normed[0]
        lats = [
            dot(lat_input, latent_weight[layer, :, group * size : (group + 1) * size]).astype(BF16)
            for group in range(GROUPS)
        ]
        if layer == 0:
            lats, own = spread(
                lats, 2, lambda values: turned(after(natural_own, values)).astype(F32)
            )
            normed_own = first_normed(own)
        else:
            lats, hidden_other = spread(
                lats,
                0,
                lambda values: feed(
                    after(other, values), other_heads, layer - 1, next_layer, weights
                ),
            )
            saved[-1].append(hidden_other)
            other, normed_other = hidden_other[5:]
        queries_t = jnp.einsum(
            "rpid,df->rpfi",
            normed_own.reshape(rows, 2, half, width),
            query_weight[layer],
            preferred_element_type=F32,
        ).astype(BF16)
        up_t = latent_up[layer].T
        heads, attended = [], []
        for group in range(GROUPS):
            out, *rest = attend(scalars, queries_t, lats[group], up_t, group, heads)
            heads = [out]
            attended.append(rest)
            if group == 0:
                if last:
                    grad_own = grad_of(side, out)
                else:
                    natural_other = tokens_of(after(tokens, out), rep_count - 1 - side)
                    natural_normed.append(first_normed(natural_other.astype(F32)))
                    other = turned(natural_other)
        heads = heads[0].reshape(toks, heads_dim)
        other_heads = across(heads)
        if last:
            own, grad_own = after((own, grad_own), heads)
        else:
            own, other = after((own, other), heads)
            other = other.astype(F32)
        hidden_own = feed(own, heads, layer, next_layer, weights)
        saved.append([own, normed_own, heads, hidden_own, lats, queries_t, up_t, attended, scalars])
        saved[-1] += [other, normed_other if layer else None, other_heads]
        own, normed_own = hidden_own[5:]

    def placed(value, moved):
        both = jnp.stack([value, moved]).reshape(2, rows, loc_len, width)
        return jnp.where(side == 0, both, both[::-1]).reshape(seq_rows, loc_len, width)

    output = turned(own.astype(BF16))
    grad_other = None
    pending = []
    other_input = None
    layer_sums = []
    for layer in reversed(range(LAYERS)):
        last = layer == LAYERS - 1
        own, normed_own, heads, hidden_own, lats, queries_t, up_t, attended, scalars = saved[layer][:9]
        other, normed_other, other_heads = saved[layer][9:12]
        back_own = feed_back(
            grad_own, hidden_own[0], hidden_own[2], hidden_own[3], layer, half, weights
        )
        d_heads_t = back_own[5].reshape(rows, 2, heads_dim, half)
        d_in_own = back_own[3]
        d_lat, up_k, up_v, filled = [], [], [], []

        def stepped(gate):
            for late in d_lat:
                late.advance(gate)
            return [late.sent for late in d_lat]

        def sents_of(sums):
            return [one.sent for one in sums]

        def wide_sums(back_other, gate):
            backs = (back_own, back_other)
            hiddens = (hidden_own, hidden_other)
            gates, acts = after(([back[0] for back in backs], [hid[4] for hid in hiddens]), gate)
            gated = gated_sum(
                [picked(pick, hid[1]) for hid in hiddens], gates, [back[1] for back in backs]
            )
            plain = pair_sum(
                [
                    ([picked(pick_late, back[2]) for back in backs], acts),
                    ([picked(pick_late, back[4]) for back in backs], [heads, other_heads]),
                ]
            )
            return [HalvingSum(trade, gated, bits), HalvingSum(trade, plain, far_late)]

        def other_back(gate):
            return feed_back(
                after(grad_other, gate),
                hidden_other[0],
                hidden_other[2],
                hidden_other[3],
                layer,
                half,
                weights,
            )

        if last:
            d_heads_t = after(d_heads_t, output)
            output_moved = across(output)
        else:
            d_in_own = turned(d_in_own.astype(BF16)).astype(F32)
            hidden_other = saved[layer][12]
            grad_other, _ = project_back(*after(other_input, back_own[3]), layer + 1)
            back_other = other_back(back_own[3])
            for late in pending[:2]:
                late.advance(back_other[3])
            sums = wide_sums(back_other, (sents_of(pending[:2]), d_in_own))
            pending[2].advance_first([sums[0].kept, sums[1].kept])
            for late in pending[:2]:
                late.advance(pending[2].sent)
            for one in sums:
                one.advance(sents_of(pending[:2]))
            d_heads_t = after(d_heads_t, sents_of(sums + pending))
        for group in range(GROUPS):
            dq, d_lat_one, up_k_one, up_v_one = attend_back(
                scalars,
                queries_t,
                d_heads_t,
                attended[group][0],
                lats[group],
                up_t,
                attended[group][1:],
                group,
                filled,
            )
            up_k.append(up_k_one)
            up_v.append(up_v_one)
            for late in pending + d_lat:
                late.advance(up_k_one)
            d_lat.append(SlotSum(trade, d_lat_one, bits))
            sents = sents_of(pending + d_lat)
            filled = [dq]
            if group == 0:
                d_heads_t = after(d_heads_t, (sents, output_moved) if last else sents)
                if last:
                    grad_other = grad_of(rep_count - 1 - side, sents)
        dq = dq.reshape(toks, heads_dim)
        up_block = latent_up.shape[2] // (seq_count * rep_count)
        folds = up_block // block
        split = [value.reshape(-1, rep_count, up_block, size) for value in up_k + up_v]

        def up_of(owner):
            chosen = [lax.dynamic_index_in_dim(value, owner, 1, False) for value in split]
            return jnp.concatenate([value.astype(BF16) for value in chosen], axis=0)

        up_sent = up_of(rep_count - 1 - side)
        if last:
            grad_other = after(grad_other, dq)
            state, _ = after((other, grad_other), sents)
            dq_other = across(dq)
            hidden_other = feed(state, other_heads, layer, layer, weights)
            sents = stepped(hidden_other[0])
            dq_other = after(dq_other, hidden_other[0])
            up_got = across(up_sent)
            back_other = other_back(sents + [dq_other, up_sent])
            sents = stepped(back_other[3])
            up_got = after(up_got, back_other[3])
            sums = wide_sums(back_other, sents + [up_got])
            sents = stepped([sums[0].kept, sums[1].kept])
            for one in sums:
                one.advance(sents)
            stepped(sents_of(sums))
        else:
            dq = turned(dq)
            up_got = across(up_sent)
            sents = stepped(up_sent)
            for one in sums:
                one.advance(sents)
            sents = stepped(sents_of(sums))
            dq = after(dq, sents)
            dq_other = across(dq)
            pending[2].advance(sents)
            sents = stepped(pending[2].sent)
            up_got = after(up_got, sents)
            pending[2].advance(sents)
        while any(late.got is not None for late in d_lat):
            stepped(None)
        d_lat = jnp.concatenate([late.value.reshape(toks, size) for late in d_lat], axis=1)
        d_lat_other = across(d_lat)
        state = own if layer else natural_own.astype(F32)
        grad_own, attn_gain_own = project_back(d_in_own, dq, d_lat, state, layer)
        if last:
            other_input = (back_other[3], dq_other, d_lat_other, other)
        normed = [
            picked(pick, value)
            for value in ((normed_own, normed_other) if layer else natural_normed)
        ]

        up_rows = (up_of(side).astype(F32) + up_got.astype(F32)).astype(BF16)
        up_rows = jnp.concatenate(
            [up_rows[:, at * block : (at + 1) * block] for at in range(folds)], axis=2
        ).reshape(kept_rows, folds * size)
        up_rows = dot(to_halving, up_rows).astype(BF16)
        vectors = jnp.where(
            vector_at == 0,
            back_own[6] + back_other[6],
            jnp.where(
                vector_at == 1,
                back_own[7] + back_other[7],
                jnp.where(vector_at == 2, attn_gain_own[None], 0.0),
            ),
        )
        vectors_other = jnp.where(vector_at == 3, attn_gain_own[None], 0.0)
        vectors = (
            dot_as(pick, vectors.astype(BF16), NT) + dot_as(pick_other, vectors_other.astype(BF16), NT)
        ).astype(BF16)
        terms = [(normed, [dq, dq_other]), (normed, [d_lat, d_lat_other])]
        rest = HalvingSum(trade, pair_sum(terms, [up_rows, vectors]), bits, begin=not last)
        if not last:
            sums[1].advance(rest.sent)
            sums[0].advance(sums[1].sent)
            rest.advance(sums[0].sent)
        sums.append(rest)
        pending = sums
        layer_sums.insert(0, sums)
    layer_grads = []
    for sums in layer_sums:
        g_gate_up, g_plain, g_rest = [one.finish() for one in sums]
        lat_at, up_at = heads_dim, heads_dim + GROUPS * size
        vectors_at = up_at + folds * size
        g_up = jnp.concatenate(
            [g_rest[:, up_at + at * size : up_at + (at + 1) * size] for at in range(folds)]
        )
        layer_grads.append(
            (
                g_rest[:, vectors_at + 2] + across(g_rest[:, vectors_at + 3]),
                g_rest[:, :lat_at],
                g_rest[:, lat_at:up_at],
                g_up.T,
                g_plain[:, hidden:].T,
                g_rest[:, vectors_at + 1],
                g_rest[:, vectors_at],
                g_gate_up,
                g_plain[:, :hidden].T,
            )
        )
    stacked = [jnp.stack([grads[member] for grads in layer_grads]) for member in range(9)]
    input_grad = grad_own.astype(BF16)
    return (
        placed(output, output_moved),
        placed(input_grad, across(input_grad)),
        *stacked,
    )


def solution(mesh):
    rows = P(None, "seq", None)
    scattered = P(None, ("seq", "rep"))
    first = P(None, ("seq", "rep"), None)
    second = P(None, None, ("seq", "rep"))
    return jax.shard_map(
        shards,
        mesh=mesh,
        in_specs=(rows, rows, P(None, "seq")) + (P(),) * 12,
        out_specs=(
            rows,
            rows,
            scattered,
            first,
            first,
            second,
            second,
            scattered,
            scattered,
            first,
            second,
        ),
        check_vma=False,
    )
```

```python
import functools

import jax
import jax.numpy as jnp
from jax import lax
from jax.experimental import pallas as pl
from jax.experimental.pallas import tpu as pltpu
from jax.sharding import PartitionSpec as P

HD = 64
LAYERS = 2
GROUPS = 2
NEG_FILL = -1e30
LOG2E = 1.4426950408889634
ATT_SCALE = HD ** (-0.5)
NT = (((1,), (1,)), ((), ()))
TN = (((0,), (0,)), ((), ()))
F32 = jnp.float32
BF16 = jnp.bfloat16
KEY_BLOCK = 512
QUERY_BLOCK = 1024
FEED_STEP, FEED_AHEAD = 768, 16
BACK_STEP, BACK_AHEAD = 1408, 6


def dot_as(left, right, dims):
    return lax.dot_general(left, right, dims, preferred_element_type=F32)


def dot(left, right):
    return jnp.dot(left, right, preferred_element_type=F32)


def order_keys(scalars, lat_ref, keys, keys_t, seq_count, half):
    for piece in range(2 * seq_count):
        slot = scalars[2 + piece]
        keys[pl.ds(piece * half, half), :] = lat_ref[0, slot, pl.ds((piece % 2) * half, half), :]
    for first in range(0, 2 * seq_count * half, 256):
        keys_t[:, first : first + 256] = keys[first : first + 256, :].T


def block_bounds(scalars, row, part, half, seq_count):
    first = scalars[part]
    cut = scalars[2 + 2 * seq_count + row]
    last = first + half - 1
    low_min = jnp.where(first >= cut, cut, 0)
    low_max = jnp.where(last >= cut, cut, 0)
    return first, cut, low_min // KEY_BLOCK, last // KEY_BLOCK + 1, low_max


def hide(scores, block_at, first, cut, half):
    lanes = lax.broadcasted_iota(jnp.int32, (1, scores.shape[1]), 1)
    query_at = first + lanes % half
    low = jnp.where(query_at >= cut, cut, 0)
    key_at = block_at * KEY_BLOCK + lax.broadcasted_iota(jnp.int32, scores.shape, 0)
    return jnp.where((key_at <= query_at) & (key_at >= low), scores, NEG_FILL)


def over_blocks(bounds, block):
    first, _, start, stop, low_max = bounds

    def body(block_at, carry):
        edge = (block_at * KEY_BLOCK + KEY_BLOCK - 1 > first) | (block_at * KEY_BLOCK < low_max)

        @pl.when(edge)
        def _():
            block(block_at, True)

        @pl.when(jnp.logical_not(edge))
        def _():
            block(block_at, False)

        return carry

    lax.fori_loop(start, stop, body, 0)


def attend_kernel(
    scalars,
    q_ref,
    lat_ref,
    up_k_ref,
    up_v_ref,
    *refs,
    seq_count,
    half,
    heads,
):
    out_ref, out_t_ref, log_ref, query_ref, mixed_ref, keys, keys_t, top, total, acc = refs[-10:]
    row, part = pl.program_id(0), pl.program_id(1)

    @pl.when(part == 0)
    def _():
        order_keys(scalars, lat_ref, keys, keys_t, seq_count, half)

    for head in range(heads):
        feats = slice(head * HD, (head + 1) * HD)
        lifted = dot_as(q_ref[0, 0, feats, :], up_k_ref[feats, :], TN)
        query_ref[0, 0, head * half : (head + 1) * half, :] = (lifted * (LOG2E * ATT_SCALE)).astype(
            BF16
        )
    top[...] = jnp.full_like(top, NEG_FILL)
    total[...] = jnp.zeros_like(total)
    acc[...] = jnp.zeros_like(acc)
    bounds = block_bounds(scalars, row, part, half, seq_count)
    columns = heads * half
    width = min(QUERY_BLOCK, columns)

    def block(block_at, edge):
        at = pl.multiple_of(block_at * KEY_BLOCK, KEY_BLOCK)
        key_rows = keys[pl.ds(at, KEY_BLOCK), :]
        key_cols = keys_t[:, pl.ds(at, KEY_BLOCK)]
        for col in range(0, columns, width):
            cols = slice(col, col + width)
            scores = dot_as(key_rows, query_ref[0, 0, cols, :], NT)
            if edge:
                scores = hide(scores, block_at, bounds[0], bounds[1], half)
            old_top = top[:, cols]
            new_top = jnp.maximum(old_top, jnp.max(scores, axis=0, keepdims=True))
            probs = jnp.exp2(scores - new_top)
            fade = jnp.exp2(old_top - new_top)
            total[:, cols] = total[:, cols] * fade + jnp.sum(probs, axis=0, keepdims=True)
            top[:, cols] = new_top
            acc[:, cols] = acc[:, cols] * fade + dot(key_cols, probs.astype(BF16))

    over_blocks(bounds, block)
    mixed_ref[0, 0, :, :] = (acc[...] * (1.0 / total[...])).astype(BF16)
    log_ref[0, 0, :, :] = top[...] + jnp.log2(total[...])
    for head in range(heads):
        feats = slice(head * HD, (head + 1) * HD)
        out_t = dot(
            up_v_ref[feats, :], mixed_ref[0, 0, :, head * half : (head + 1) * half]
        ).astype(BF16)
        out_t_ref[0, 0, feats, :] = out_t
        out_ref[0, 0, :, feats] = out_t.T


def attend_back_kernel(
    scalars,
    q_ref,
    d_out_ref,
    out_ref,
    lat_ref,
    up_k_ref,
    up_v_ref,
    query_ref,
    mixed_ref,
    log_ref,
    *refs,
    seq_count,
    half,
    heads,
):
    dq_ref, d_lat_ref, d_up_k_ref, d_up_v_ref = refs[-11:-7]
    keys, keys_t, d_keys, query_plain, d_mixed, delta, d_query = refs[-7:]
    row, part = pl.program_id(0), pl.program_id(1)

    @pl.when(part == 0)
    def _():
        order_keys(scalars, lat_ref, keys, keys_t, seq_count, half)
        d_keys[...] = jnp.zeros_like(d_keys)

    @pl.when((part == 0) & (row == 0))
    def _():
        d_up_k_ref[...] = jnp.zeros_like(d_up_k_ref)
        d_up_v_ref[...] = jnp.zeros_like(d_up_v_ref)

    for head in range(heads):
        feats = slice(head * HD, (head + 1) * HD)
        cols = slice(head * half, (head + 1) * half)
        d_out = d_out_ref[0, 0, feats, :]
        query_plain[cols, :] = (
            dot_as(q_ref[0, 0, feats, :], up_k_ref[feats, :], TN) * ATT_SCALE
        ).astype(BF16)
        d_mixed[cols, :] = dot_as(d_out, up_v_ref[feats, :], TN).astype(BF16)
        delta[:, cols] = jnp.sum(
            d_out.astype(F32) * out_ref[0, 0, feats, :].astype(F32), axis=0, keepdims=True
        )
    d_query[...] = jnp.zeros_like(d_query)
    bounds = block_bounds(scalars, row, part, half, seq_count)
    columns = heads * half
    width = min(QUERY_BLOCK, columns)

    def block(block_at, edge):
        at = pl.multiple_of(block_at * KEY_BLOCK, KEY_BLOCK)
        key_rows = keys[pl.ds(at, KEY_BLOCK), :]
        key_cols = keys_t[:, pl.ds(at, KEY_BLOCK)]
        key_total = d_keys[pl.ds(at, KEY_BLOCK), :]
        for col in range(0, columns, width):
            cols = slice(col, col + width)
            scores = dot_as(key_rows, query_ref[0, 0, cols, :], NT)
            if edge:
                scores = hide(scores, block_at, bounds[0], bounds[1], half)
            probs = jnp.exp2(scores - log_ref[0, 0, :, cols])
            d_probs = dot_as(key_rows, d_mixed[cols, :], NT)
            d_scores = (probs * (d_probs - delta[:, cols])).astype(BF16)
            key_total = key_total + (
                dot(d_scores, query_plain[cols, :]) + dot(probs.astype(BF16), d_mixed[cols, :])
            )
            d_query[:, cols] += dot(key_cols, d_scores)
        d_keys[pl.ds(at, KEY_BLOCK), :] = key_total

    over_blocks(bounds, block)
    for head in range(heads):
        feats = slice(head * HD, (head + 1) * HD)
        cols = slice(head * half, (head + 1) * half)
        d_lifted = (d_query[:, cols] * ATT_SCALE).astype(BF16)
        dq_ref[0, 0, :, feats] = dot(up_k_ref[feats, :], d_lifted).astype(BF16).T
        d_up_k_ref[feats, :] += dot_as(q_ref[0, 0, feats, :], d_lifted, NT)
        d_up_v_ref[feats, :] += dot_as(d_out_ref[0, 0, feats, :], mixed_ref[0, 0, :, cols], NT)

    @pl.when(part == 1)
    def _():
        for piece in range(2 * seq_count):
            slot = scalars[2 + piece]
            d_lat_ref[0, slot, pl.ds((piece % 2) * half, half), :] = d_keys[
                pl.ds(piece * half, half), :
            ].astype(BF16)


def attention_sizes(queries_t, lats):
    rows, _, feats, half = queries_t.shape
    group_feats = feats // GROUPS
    heads = group_feats // HD
    seq_count, size = lats.shape[1], lats.shape[3]
    return rows, half, group_feats, heads, heads * half, seq_count, size, seq_count * 2 * half


def head_spec(group_feats, half, group):
    return pl.BlockSpec((1, 1, group_feats, half), lambda row, part, _: (row, part, group, 0))


def token_spec(group_feats, half, group):
    return pl.BlockSpec((1, 1, half, group_feats), lambda row, part, _: (row, part, 0, group))


def lat_spec(lats):
    return pl.BlockSpec((1,) + lats.shape[1:], lambda row, part, _: (row, 0, 0, 0))


ANY = pl.BlockSpec(memory_space=pl.ANY)


def plain_spec(*block):
    return pl.BlockSpec((1, 1) + block, lambda row, part, _: (row, part, 0, 0))


def up_spec(group_feats, size, at):
    return pl.BlockSpec((group_feats, size), lambda row, part, _: (at, 0))


def in_hbm(value):
    return pltpu.with_memory_space_constraint(value, pltpu.HBM)


def attend(scalars, queries_t, lats, up_t, group, filled):
    rows, half, group_feats, heads, columns, seq_count, size, keys = attention_sizes(
        queries_t, lats
    )
    return pl.pallas_call(
        functools.partial(
            attend_kernel, seq_count=seq_count, half=half, heads=heads
        ),
        grid_spec=pltpu.PrefetchScalarGridSpec(
            num_scalar_prefetch=1,
            grid=(rows, 2),
            in_specs=[
                head_spec(group_feats, half, group),
                lat_spec(lats),
                up_spec(group_feats, size, group),
                up_spec(group_feats, size, GROUPS + group),
            ]
            + [ANY] * len(filled),
            out_specs=[
                token_spec(group_feats, half, group),
                plain_spec(group_feats, half),
                plain_spec(1, columns),
                plain_spec(columns, size),
                plain_spec(size, columns),
            ],
            scratch_shapes=[
                pltpu.VMEM((keys, size), BF16),
                pltpu.VMEM((size, keys), BF16),
                pltpu.VMEM((1, columns), F32),
                pltpu.VMEM((1, columns), F32),
                pltpu.VMEM((size, columns), F32),
            ],
        ),
        out_shape=[
            jax.ShapeDtypeStruct((rows, 2, half, GROUPS * group_feats), BF16),
            pltpu.HBM((rows, 2, group_feats, half), BF16),
            pltpu.HBM((rows, 2, 1, columns), F32),
            pltpu.HBM((rows, 2, columns, size), BF16),
            pltpu.HBM((rows, 2, size, columns), BF16),
        ],
        compiler_params=pltpu.CompilerParams(
            dimension_semantics=("arbitrary", "arbitrary"), vmem_limit_bytes=40 << 20
        ),
        cost_estimate=pl.CostEstimate(
            flops=rows * 2 * columns * keys * size * 2,
            bytes_accessed=rows * (2 * keys * size + 8 * columns * size),
            transcendentals=rows * columns * keys,
        ),
        input_output_aliases={5: 0} if filled else {},
        name="attend",
    )(scalars, queries_t, lats, up_t, up_t, *filled)


def attend_back(
    scalars, queries_t, d_heads_t, heads_t, lats, up_t, kept, group, filled
):
    rows, half, group_feats, heads, columns, seq_count, size, keys = attention_sizes(
        queries_t, lats
    )
    logs, lifted, mixed = kept
    return pl.pallas_call(
        functools.partial(
            attend_back_kernel, seq_count=seq_count, half=half, heads=heads
        ),
        grid_spec=pltpu.PrefetchScalarGridSpec(
            num_scalar_prefetch=1,
            grid=(rows, 2),
            in_specs=[
                head_spec(group_feats, half, group),
                head_spec(group_feats, half, group),
                plain_spec(group_feats, half),
                lat_spec(lats),
                up_spec(group_feats, size, group),
                up_spec(group_feats, size, GROUPS + group),
                plain_spec(columns, size),
                plain_spec(size, columns),
                plain_spec(1, columns),
            ]
            + [ANY] * len(filled),
            out_specs=[
                token_spec(group_feats, half, group),
                lat_spec(lats),
                up_spec(group_feats, size, 0),
                up_spec(group_feats, size, 0),
            ],
            scratch_shapes=[
                pltpu.VMEM((keys, size), BF16),
                pltpu.VMEM((size, keys), BF16),
                pltpu.VMEM((keys, size), F32),
                pltpu.VMEM((columns, size), BF16),
                pltpu.VMEM((columns, size), BF16),
                pltpu.VMEM((1, columns), F32),
                pltpu.VMEM((size, columns), F32),
            ],
        ),
        out_shape=[
            jax.ShapeDtypeStruct((rows, 2, half, GROUPS * group_feats), BF16),
            jax.ShapeDtypeStruct(lats.shape, BF16),
            jax.ShapeDtypeStruct((group_feats, size), F32),
            jax.ShapeDtypeStruct((group_feats, size), F32),
        ],
        compiler_params=pltpu.CompilerParams(
            dimension_semantics=("arbitrary", "arbitrary"), vmem_limit_bytes=48 << 20
        ),
        cost_estimate=pl.CostEstimate(
            flops=rows * 5 * columns * keys * size * 2,
            bytes_accessed=rows * (4 * keys * size + 12 * columns * size),
            transcendentals=rows * columns * keys,
        ),
        input_output_aliases={10: 0} if filled else {},
        name="attend_back",
    )(
        scalars,
        *map(
            in_hbm, (queries_t, d_heads_t, heads_t, lats, up_t, up_t, lifted, mixed, logs)
        ),
        *filled,
    )


def rms_scale(value_rows):
    return lax.rsqrt(jnp.mean(value_rows * value_rows, axis=-1, keepdims=True) + 1e-06)


def norm_back(grad_in, value_rows, scale_rows, gain_vec):
    normed = value_rows * scale_rows
    upstream = grad_in * gain_vec
    return (
        scale_rows * (upstream - normed * jnp.mean(upstream * normed, axis=-1, keepdims=True)),
        jnp.sum(grad_in * normed, axis=0),
    )


def hidden_chunks(hidden, step):
    return [(at, min(step, hidden - at)) for at in range(0, hidden, step)]


class Copies:
    def __init__(self, sems, ahead):
        self.sems, self.made, self.begun, self.done, self.ahead = sems, [], 0, 0, ahead

    def add(self, source, target):
        self.made.append(pltpu.make_async_copy(source, target, self.sems.at[len(self.made)]))

    def begin(self, count):
        while self.begun < min(count, len(self.made)):
            self.made[self.begun].start()
            self.begun += 1

    def need(self, count):
        while self.done < count:
            self.made[self.done].wait()
            self.done += 1
            self.begin(self.done + self.ahead)


def feed_kernel(
    heads,
    state,
    bias,
    gain,
    next_gain,
    w_out,
    w_both,
    w_down,
    hidden_in,
    normed_mlp,
    gate,
    up,
    act,
    following,
    normed_next,
    v_heads,
    v_state,
    v_out,
    v_gate_w,
    v_up_w,
    v_down_w,
    v_normed,
    v_gate,
    v_up,
    v_act,
    v_next,
    v_normed_next,
    in_sems,
    out_sems,
    *,
    layer,
    hidden,
):
    chunks = hidden_chunks(hidden, FEED_STEP)
    loads, stores = Copies(in_sems, FEED_AHEAD), Copies(out_sems, 1)
    loads.add(heads, v_heads)
    loads.add(state, v_state)
    loads.add(w_out.at[layer], v_out)
    for at, count in chunks:
        cols = pl.ds(at, count)
        loads.add(w_both.at[layer, :, cols], v_gate_w.at[:, cols])
        loads.add(w_both.at[layer, :, pl.ds(hidden + at, count)], v_up_w.at[:, cols])
        loads.add(w_down.at[layer, cols, :], v_down_w.at[cols, :])
    loads.begin(FEED_AHEAD)
    loads.need(3)

    def store(source, target):
        stores.add(source, target)
        stores.begin(len(stores.made))

    value = v_state[...] + (dot(v_heads[...], v_out[...]) + bias[0])
    v_state[...] = value
    store(v_state, hidden_in)
    normed = (value * rms_scale(value) * gain[0]).astype(BF16)
    v_normed[...] = normed
    store(v_normed, normed_mlp)
    v_next[...] = value
    needed = 3
    for at, count in chunks:
        cols = pl.ds(at, count)
        loads.need(needed + 2)
        gate_part = dot(v_normed[...], v_gate_w[:, cols])
        up_part = dot(v_normed[...], v_up_w[:, cols])
        act_part = (gate_part * jax.nn.sigmoid(gate_part) * up_part).astype(BF16)
        v_gate[:, cols] = gate_part.astype(BF16)
        v_up[:, cols] = up_part.astype(BF16)
        v_act[:, cols] = act_part
        store(v_gate.at[:, cols], gate.at[:, cols])
        store(v_up.at[:, cols], up.at[:, cols])
        store(v_act.at[:, cols], act.at[:, cols])
        needed += 3
        loads.need(needed)
        v_next[...] += dot(act_part, v_down_w[cols, :])
    value = v_next[...]
    store(v_next, following)
    v_normed_next[...] = (value * rms_scale(value) * next_gain[0]).astype(BF16)
    store(v_normed_next, normed_next)
    stores.need(len(stores.made))


def vector_spec(at, width):
    return pl.BlockSpec((1, 1, width), lambda step: (at, 0, 0))


def feed(state, heads, layer, next_layer, weights):
    out_weight, out_bias, mlp_gain, attn_gain, gate_up_matrix, down_matrix = weights
    toks, width = state.shape
    hidden = down_matrix.shape[1]
    count = len(hidden_chunks(hidden, FEED_STEP))
    wide = lambda dtype: jax.ShapeDtypeStruct((toks, width), dtype)
    tiled = jax.ShapeDtypeStruct((toks, hidden), BF16)
    return pl.pallas_call(
        functools.partial(feed_kernel, layer=layer, hidden=hidden),
        grid=(1,),
        in_specs=[ANY] * 2
        + [vector_spec(layer, width), vector_spec(layer, width), vector_spec(next_layer, width)]
        + [ANY] * 3,
        out_specs=[ANY] * 7,
        out_shape=[wide(F32), wide(BF16), tiled, tiled, tiled, wide(F32), wide(BF16)],
        scratch_shapes=[
            pltpu.VMEM(heads.shape, BF16),
            pltpu.VMEM((toks, width), F32),
            pltpu.VMEM(out_weight.shape[1:], BF16),
            pltpu.VMEM((width, hidden), BF16),
            pltpu.VMEM((width, hidden), BF16),
            pltpu.VMEM((hidden, width), BF16),
            pltpu.VMEM((toks, width), BF16),
            pltpu.VMEM((toks, hidden), BF16),
            pltpu.VMEM((toks, hidden), BF16),
            pltpu.VMEM((toks, hidden), BF16),
            pltpu.VMEM((toks, width), F32),
            pltpu.VMEM((toks, width), BF16),
            pltpu.SemaphoreType.DMA((3 + 3 * count,)),
            pltpu.SemaphoreType.DMA((4 + 3 * count,)),
        ],
        compiler_params=pltpu.CompilerParams(
            dimension_semantics=("arbitrary",), vmem_limit_bytes=40 << 20
        ),
        cost_estimate=pl.CostEstimate(
            flops=2 * toks * width * (3 * hidden + width),
            bytes_accessed=2 * width * (3 * hidden + width) + 6 * toks * hidden,
            transcendentals=toks * hidden,
        ),
        name="feed",
    )(
        heads,
        state,
        out_bias[:, None],
        mlp_gain[:, None],
        attn_gain[:, None],
        out_weight,
        gate_up_matrix,
        down_matrix,
    )


def feed_back_kernel(
    grad,
    hidden_in,
    gain,
    gate,
    up,
    w_out,
    w_both,
    w_down,
    d_gate,
    d_up,
    d_mlp,
    d_hidden_in,
    d_attn,
    d_heads_t,
    gain_sum,
    bias_sum,
    v_grad,
    v_hidden_in,
    v_gate,
    v_up,
    v_out,
    v_gate_w,
    v_up_w,
    v_down_w,
    v_d_mlp,
    v_d_attn,
    v_d_heads,
    acc,
    in_sems,
    out_sems,
    *,
    layer,
    hidden,
    half,
):
    chunks = hidden_chunks(hidden, BACK_STEP)
    loads, stores = Copies(in_sems, BACK_AHEAD), Copies(out_sems, 1)
    loads.add(grad, v_grad)
    for at, count in chunks:
        cols = pl.ds(at, count)
        loads.add(gate.at[:, cols], v_gate.at[:, cols])
        loads.add(up.at[:, cols], v_up.at[:, cols])
        loads.add(w_down.at[layer, cols, :], v_down_w.at[cols, :])
        loads.add(w_both.at[layer, :, cols], v_gate_w.at[:, cols])
        loads.add(w_both.at[layer, :, pl.ds(hidden + at, count)], v_up_w.at[:, cols])
    loads.add(hidden_in, v_hidden_in)
    loads.add(w_out.at[layer], v_out)
    loads.begin(BACK_AHEAD)
    loads.need(1)

    def store(source, target):
        stores.add(source, target)
        stores.begin(len(stores.made))

    v_d_mlp[...] = v_grad[...].astype(BF16)
    store(v_d_mlp, d_mlp)
    needed = 1
    for at, count in chunks:
        cols = pl.ds(at, count)
        loads.need(needed + 3)
        d_act = dot_as(v_d_mlp[...], v_down_w[cols, :], NT)
        gate_part = v_gate[:, cols].astype(F32)
        up_part = v_up[:, cols].astype(F32)
        sig_gate = jax.nn.sigmoid(gate_part)
        d_gate_part = (d_act * up_part * sig_gate * (1.0 + gate_part * (1.0 - sig_gate))).astype(
            BF16
        )
        d_up_part = (d_act * gate_part * sig_gate).astype(BF16)
        v_gate[:, cols] = d_gate_part
        v_up[:, cols] = d_up_part
        store(v_gate.at[:, cols], d_gate.at[:, cols])
        store(v_up.at[:, cols], d_up.at[:, cols])
        needed += 5
        loads.need(needed)
        part = dot_as(d_gate_part, v_gate_w[:, cols], NT) + dot_as(d_up_part, v_up_w[:, cols], NT)
        if at == 0:
            acc[...] = part
        else:
            acc[...] += part
    loads.need(needed + 1)
    value = v_hidden_in[...]
    d_norm, gain_terms = norm_back(acc[...], value, rms_scale(value), gain[0])
    gain_sum[...] = gain_terms[None]
    total = v_grad[...] + d_norm
    low = total.astype(BF16)
    v_grad[...] = total
    store(v_grad, d_hidden_in)
    v_d_attn[...] = low
    store(v_d_attn, d_attn)
    bias_sum[...] = jnp.sum(low.astype(F32), axis=0, keepdims=True)
    loads.need(needed + 2)
    for piece in range(d_heads_t.shape[0]):
        v_d_heads[piece] = dot_as(v_out[...], low[piece * half : (piece + 1) * half], NT).astype(
            BF16
        )
    store(v_d_heads, d_heads_t)
    stores.need(len(stores.made))


def feed_back(grad, hidden_in, gate, up, layer, half, weights):
    out_weight, _, mlp_gain, _, gate_up_matrix, down_matrix = weights
    toks, width = grad.shape
    heads_dim = out_weight.shape[1]
    hidden = down_matrix.shape[1]
    vector_out = pl.BlockSpec((1, width), lambda step: (0, 0))
    wide = lambda dtype: jax.ShapeDtypeStruct((toks, width), dtype)
    tiled = jax.ShapeDtypeStruct((toks, hidden), BF16)
    pieces = toks // half
    count = len(hidden_chunks(hidden, BACK_STEP))
    return pl.pallas_call(
        functools.partial(feed_back_kernel, layer=layer, hidden=hidden, half=half),
        grid=(1,),
        in_specs=[ANY, ANY, vector_spec(layer, width)] + [ANY] * 5,
        out_specs=[ANY] * 6 + [vector_out] * 2,
        out_shape=[
            tiled,
            tiled,
            wide(BF16),
            wide(F32),
            wide(BF16),
            jax.ShapeDtypeStruct((pieces, heads_dim, half), BF16),
            jax.ShapeDtypeStruct((1, width), F32),
            jax.ShapeDtypeStruct((1, width), F32),
        ],
        scratch_shapes=[
            pltpu.VMEM((toks, width), F32),
            pltpu.VMEM((toks, width), F32),
            pltpu.VMEM((toks, hidden), BF16),
            pltpu.VMEM((toks, hidden), BF16),
            pltpu.VMEM(out_weight.shape[1:], BF16),
            pltpu.VMEM((width, hidden), BF16),
            pltpu.VMEM((width, hidden), BF16),
            pltpu.VMEM((hidden, width), BF16),
            pltpu.VMEM((toks, width), BF16),
            pltpu.VMEM((toks, width), BF16),
            pltpu.VMEM((pieces, heads_dim, half), BF16),
            pltpu.VMEM((toks, width), F32),
            pltpu.SemaphoreType.DMA((3 + 5 * count,)),
            pltpu.SemaphoreType.DMA((4 + 2 * count,)),
        ],
        compiler_params=pltpu.CompilerParams(
            dimension_semantics=("arbitrary",), vmem_limit_bytes=40 << 20
        ),
        cost_estimate=pl.CostEstimate(
            flops=2 * toks * width * (3 * hidden + heads_dim),
            bytes_accessed=2 * width * (3 * hidden + heads_dim) + 8 * toks * hidden,
            transcendentals=toks * hidden,
        ),
        name="feed_back",
    )(
        grad,
        hidden_in,
        mlp_gain[:, None],
        gate,
        up,
        out_weight,
        gate_up_matrix,
        down_matrix,
    )


def gated_sum_kernel(left_a, left_b, gate_a, gate_b, up_a, up_b, kept, sent):
    half_rows = kept.shape[0]

    def add(right_a, right_b):
        value = (dot(left_a[...], right_a[...]) + dot(left_b[...], right_b[...])).astype(BF16)
        kept[...] = value[:half_rows]
        sent[...] = value[half_rows:]

    first = pl.program_id(0) < pl.num_programs(0) // 2

    @pl.when(first)
    def _():
        add(gate_a, gate_b)

    @pl.when(jnp.logical_not(first))
    def _():
        add(up_a, up_b)


def gated_sum(lefts, gates, ups):
    rows, toks = lefts[0].shape
    hidden = gates[0].shape[1]
    tile = hidden // 2 if hidden % 256 == 0 else hidden
    count = hidden // tile
    whole = pl.BlockSpec((rows, toks), lambda step: (0, 0))
    gate_spec = pl.BlockSpec((toks, tile), lambda step: (0, jnp.minimum(step, count - 1)))
    up_spec_ = pl.BlockSpec((toks, tile), lambda step: (0, jnp.maximum(step - count, 0)))
    return pl.pallas_call(
        gated_sum_kernel,
        grid=(2 * count,),
        in_specs=[whole] * 2 + [gate_spec] * 2 + [up_spec_] * 2,
        out_specs=[pl.BlockSpec((rows // 2, tile), lambda step: (0, step))] * 2,
        out_shape=[jax.ShapeDtypeStruct((rows // 2, 2 * hidden), BF16)] * 2,
        compiler_params=pltpu.CompilerParams(
            dimension_semantics=("arbitrary",), vmem_limit_bytes=36 << 20
        ),
        cost_estimate=pl.CostEstimate(
            flops=8 * rows * toks * hidden,
            bytes_accessed=4 * hidden * (2 * toks + rows),
            transcendentals=0,
        ),
        name="gated_sum",
    )(*lefts, *gates, *ups)


def pair_sum_kernel(*refs, count):
    lefts, rights = refs[: 2 * count], refs[2 * count : 4 * count]
    kept, sent = refs[-2:]
    half_rows = kept.shape[0]
    at = 0
    for one in range(0, 2 * count, 2):
        cols = slice(at, at + rights[one].shape[1])
        value = (
            dot(lefts[one][...], rights[one][...]) + dot(lefts[one + 1][...], rights[one + 1][...])
        ).astype(BF16)
        kept[:, cols] = value[:half_rows]
        sent[:, cols] = value[half_rows:]
        at = cols.stop
    for extra in refs[4 * count : -2]:
        cols = slice(at, at + extra.shape[1])
        kept[:, cols] = extra[:half_rows]
        sent[:, cols] = extra[half_rows:]
        at = cols.stop


def pair_sum(terms, extras=()):
    rows, toks = terms[0][0][0].shape
    cols = sum(rights[0].shape[1] for _, rights in terms)
    total = cols + sum(value.shape[1] for value in extras)
    return pl.pallas_call(
        functools.partial(pair_sum_kernel, count=len(terms)),
        out_shape=[jax.ShapeDtypeStruct((rows // 2, total), BF16)] * 2,
        compiler_params=pltpu.CompilerParams(vmem_limit_bytes=36 << 20),
        cost_estimate=pl.CostEstimate(
            flops=4 * rows * toks * cols,
            bytes_accessed=4 * toks * cols + 2 * rows * total,
            transcendentals=0,
        ),
        name="pair_sum",
    )(*[left for lefts, _ in terms for left in lefts], *[r for _, rights in terms for r in rights], *extras)


class HalvingSum:
    def __init__(self, trade, pair, order):
        self.trade, self.order, self.step = trade, order, 1
        self.kept, self.sent = pair
        self.got = trade(self.sent, order[0])
        self.result = None

    def advance(self, gate=None):
        if self.result is not None:
            return
        kept, got = self.kept, self.got
        if gate is not None:
            (kept, got), _ = lax.optimization_barrier(((kept, got), gate))
        if self.step == len(self.order):
            self.result = kept.astype(F32) + got.astype(F32)
            return
        left = kept.shape[0] // 2
        self.sent = (kept[left:].astype(F32) + got[left:].astype(F32)).astype(BF16)
        self.kept = (kept[:left].astype(F32) + got[:left].astype(F32)).astype(BF16)
        self.got = self.trade(self.sent, self.order[self.step])
        self.step += 1

    def finish(self):
        while self.result is None:
            self.advance()
        return self.result


class SlotSum:
    result = None

    def __init__(self, trade, value, order):
        self.trade, self.value, self.order, self.step = trade, value, order, 0
        self.send()

    def send(self):
        left = self.value.shape[1] // 2
        self.kept, self.sent = self.value[:, :left], self.value[:, left:]
        self.got = self.trade(self.sent, self.order[self.step])
        self.step += 1

    def advance(self, gate):
        if self.got is None:
            return
        kept, got = self.kept, self.got
        if gate is not None:
            (kept, got), _ = lax.optimization_barrier(((kept, got), gate))
        self.value = (kept.astype(F32) + got.astype(F32)).astype(BF16)
        self.got = None
        if self.step < len(self.order):
            self.send()
        else:
            self.sent = self.value


def shards(
    tokens,
    cotangent,
    domain_ids,
    domain_counts,
    domain_weights,
    seq_cuts,
    attn_gain,
    query_weight,
    latent_weight,
    latent_up,
    out_weight,
    out_bias,
    mlp_gain,
    gate_up_matrix,
    down_matrix,
):
    seq_count = lax.axis_size("seq")
    rep_count = lax.axis_size("rep")
    place = lax.axis_index("seq").astype(jnp.int32)
    side = lax.axis_index("rep").astype(jnp.int32)
    seq_rows, loc_len, width = tokens.shape
    rows = seq_rows // rep_count
    half = loc_len // 2
    toks = rows * loc_len
    heads_dim = query_weight.shape[2]
    size = latent_up.shape[1]
    hidden = down_matrix.shape[1]
    group_cols = heads_dim // GROUPS
    bits = [1 << at for at in range(seq_count.bit_length() - 1)]
    far_late = bits[:1] + bits[2:3] + bits[1:2] + bits[3:]
    weights = (out_weight, out_bias, mlp_gain, attn_gain, gate_up_matrix, down_matrix)

    def after(value, gate):
        return lax.optimization_barrier((value, gate))[0]

    def swap_ends(value):
        moves = [(at, seq_count - 1 - at) for at in range(seq_count)]
        return lax.ppermute(value, "seq", moves)

    def across(value):
        return lax.ppermute(value, "rep", [(at, rep_count - 1 - at) for at in range(rep_count)])

    def trade(value, bit):
        return lax.ppermute(value, "seq", [(at, at ^ bit) for at in range(seq_count)])

    def rows_of(value, owner):
        return lax.dynamic_slice_in_dim(value, owner * rows, rows, 0)

    def turned(value):
        split = value.reshape((rows, 2, half) + value.shape[1:])
        return jnp.stack([split[:, 0], swap_ends(split[:, 1])], axis=1).reshape(value.shape)

    def tokens_of(value, owner):
        return rows_of(value, owner).reshape((toks,) + value.shape[2:])

    def spread(values, fill_at, fill):
        values = [value.reshape(rows, 1, loc_len, size) for value in values]
        filled = None
        for at, bit in enumerate(reversed(bits)):
            got = [trade(value, bit) for value in values]
            if at == fill_at:
                filled = fill(values)
                values, got = after((values, got), filled)
            values = [jnp.concatenate(pair, axis=1) for pair in zip(values, got)]
        return values, filled

    block = width // (seq_count * rep_count)
    kept_rows = seq_count * block
    row_at = jnp.arange(kept_rows, dtype=jnp.int32)
    col_at = jnp.arange(width, dtype=jnp.int32)

    def halving_step(order):
        distance = jnp.zeros_like(row_at)
        for level, bit in enumerate(order):
            distance = distance + (row_at // block // (seq_count // 2 >> level)) % 2 * bit
        return place ^ distance

    def picker(order, owner):
        source = (halving_step(order) * rep_count + owner) * block + row_at % block
        return (source[:, None] == col_at[None, :]).astype(BF16)

    pick, pick_late = picker(bits, side), picker(far_late, side)
    pick_other = picker(bits, rep_count - 1 - side)
    vector_at = jnp.arange(128, dtype=jnp.int32)[:, None]
    to_halving = (
        (halving_step(bits) * block + row_at % block)[:, None] == row_at[None, :]
    ).astype(BF16)

    def picked(picks, value):
        return dot_as(picks, value, NT).astype(BF16)

    domain_total = domain_counts.shape[0]
    all_tokens = seq_rows * loc_len * seq_count
    per_domain = domain_weights * (all_tokens / domain_total) / domain_counts.astype(F32)
    one_hot = (domain_ids[..., None] == jnp.arange(domain_total, dtype=jnp.int32)).astype(F32)
    row_scale = jnp.sum(one_hot * per_domain, axis=-1)
    pieces = jnp.arange(2 * seq_count, dtype=jnp.int32)

    def scalars_of(zigzag):
        source = pieces // 2
        if zigzag:
            source = jnp.where(pieces % 2 == 0, source, (2 * seq_count - 1 - pieces) // 2)
        distance = source ^ place
        slots = jnp.zeros_like(pieces)
        for level, bit in enumerate(bits):
            slots = slots + distance // bit % 2 * (seq_count // 2 >> level)
        starts = jnp.stack([place * loc_len, (2 * seq_count - 1 - 2 * place) * half])
        return jnp.concatenate([starts, slots, rows_of(seq_cuts, side)])

    def project_back(d_hidden_in, dq, d_lat, state, layer):
        d_normed = dot_as(dq, query_weight[layer], NT) + dot_as(d_lat, latent_weight[layer], NT)
        d_norm, g_gain = norm_back(d_normed, state, rms_scale(state), attn_gain[layer])
        return d_hidden_in + d_norm, g_gain

    def grad_of(owner, gate):
        value = tokens_of(cotangent, owner).astype(F32) * tokens_of(row_scale, owner)[:, None]
        split = value.reshape(rows, 2, half, width)
        swapped = swap_ends(after(split[:, 1].astype(BF16), gate))
        return jnp.stack([split[:, 0], swapped.astype(F32)], axis=1).reshape(toks, width)

    def first_normed(state):
        return (state * rms_scale(state) * attn_gain[0]).astype(BF16)

    natural_own = tokens_of(tokens, side)
    natural_normed = [first_normed(natural_own.astype(F32))]
    hidden_other = None
    saved = []
    for layer in range(LAYERS):
        last = layer == LAYERS - 1
        next_layer = min(layer + 1, LAYERS - 1)
        scalars = scalars_of(layer > 0)
        lat_input = normed_own if layer else natural_normed[0]
        lats = [
            dot(lat_input, latent_weight[layer, :, group * size : (group + 1) * size]).astype(BF16)
            for group in range(GROUPS)
        ]
        if layer == 0:
            lats, own = spread(
                lats, 2, lambda values: turned(after(natural_own, values)).astype(F32)
            )
            normed_own = first_normed(own)
        else:
            lats, hidden_other = spread(
                lats,
                0,
                lambda values: feed(
                    after(other, values), other_heads, layer - 1, next_layer, weights
                ),
            )
            saved[-1].append(hidden_other)
            other, normed_other = hidden_other[5:]
        queries_t = jnp.einsum(
            "rpid,df->rpfi",
            normed_own.reshape(rows, 2, half, width),
            query_weight[layer],
            preferred_element_type=F32,
        ).astype(BF16)
        up_t = latent_up[layer].T
        heads, attended = [], []
        for group in range(GROUPS):
            out, *rest = attend(scalars, queries_t, lats[group], up_t, group, heads)
            heads = [out]
            attended.append(rest)
            if group == 0:
                if last:
                    grad_own = grad_of(side, out)
                else:
                    natural_other = tokens_of(after(tokens, out), rep_count - 1 - side)
                    natural_normed.append(first_normed(natural_other.astype(F32)))
                    other = turned(natural_other)
        heads = heads[0].reshape(toks, heads_dim)
        other_heads = across(heads)
        if last:
            own, grad_own = after((own, grad_own), heads)
        else:
            own, other = after((own, other), heads)
            other = other.astype(F32)
        hidden_own = feed(own, heads, layer, next_layer, weights)
        saved.append([own, normed_own, heads, hidden_own, lats, queries_t, up_t, attended, scalars])
        saved[-1] += [other, normed_other if layer else None, other_heads]
        own, normed_own = hidden_own[5:]

    def placed(value, moved):
        both = jnp.stack([value, moved]).reshape(2, rows, loc_len, width)
        return jnp.where(side == 0, both, both[::-1]).reshape(seq_rows, loc_len, width)

    output = turned(own.astype(BF16))
    grad_other = None
    pending = []
    other_input = None
    layer_sums = []
    for layer in reversed(range(LAYERS)):
        last = layer == LAYERS - 1
        own, normed_own, heads, hidden_own, lats, queries_t, up_t, attended, scalars = saved[layer][:9]
        other, normed_other, other_heads = saved[layer][9:12]
        back_own = feed_back(
            grad_own, hidden_own[0], hidden_own[2], hidden_own[3], layer, half, weights
        )
        d_heads_t = back_own[5].reshape(rows, 2, heads_dim, half)
        d_in_own = back_own[3]
        d_lat, up_k, up_v, filled = [], [], [], []

        def stepped(gate):
            for late in d_lat:
                late.advance(gate)
            return [late.sent for late in d_lat]

        def sents_of(sums):
            return [one.sent if one.result is None else one.result for one in sums]

        def wide_sums(back_other, gate):
            backs = (back_own, back_other)
            hiddens = (hidden_own, hidden_other)
            gates, acts = after(([back[0] for back in backs], [hid[4] for hid in hiddens]), gate)
            gated = gated_sum(
                [picked(pick, hid[1]) for hid in hiddens], gates, [back[1] for back in backs]
            )
            plain = pair_sum(
                [
                    ([picked(pick_late, back[2]) for back in backs], acts),
                    ([picked(pick_late, back[4]) for back in backs], [heads, other_heads]),
                ]
            )
            return [HalvingSum(trade, gated, bits), HalvingSum(trade, plain, far_late)]

        def other_back(gate):
            return feed_back(
                after(grad_other, gate),
                hidden_other[0],
                hidden_other[2],
                hidden_other[3],
                layer,
                half,
                weights,
            )

        if last:
            d_heads_t = after(d_heads_t, output)
            output_moved = across(output)
        else:
            d_in_own = turned(d_in_own.astype(BF16)).astype(F32)
            hidden_other = saved[layer][12]
            grad_other, _ = project_back(*after(other_input, back_own[3]), layer + 1)
            back_other = other_back((back_own[3], pending[2].sent))
            for late in pending[:2]:
                late.advance(back_other[3])
            pending[2].advance(back_other[3])
            sums = wide_sums(back_other, (sents_of(pending), d_in_own))
            for late in pending[:2]:
                late.advance([sums[0].kept, sums[1].kept])
            for one in sums:
                one.advance(sents_of(pending[:2]))
            d_heads_t = after(d_heads_t, sents_of(sums + pending))
        for group in range(GROUPS):
            dq, d_lat_one, up_k_one, up_v_one = attend_back(
                scalars,
                queries_t,
                d_heads_t,
                attended[group][0],
                lats[group],
                up_t,
                attended[group][1:],
                group,
                filled,
            )
            up_k.append(up_k_one)
            up_v.append(up_v_one)
            for late in (pending if group == 0 else []) + d_lat:
                late.advance(up_k_one)
            d_lat.append(SlotSum(trade, d_lat_one, bits))
            sents = sents_of(pending + d_lat)
            filled = [dq]
            if group == 0:
                d_heads_t = after(d_heads_t, (sents, output_moved) if last else sents)
                if last:
                    grad_other = grad_of(rep_count - 1 - side, sents)
        dq = dq.reshape(toks, heads_dim)
        up_block = latent_up.shape[2] // (seq_count * rep_count)
        folds = up_block // block
        split = [value.reshape(-1, rep_count, up_block, size) for value in up_k + up_v]

        def up_of(owner):
            chosen = [lax.dynamic_index_in_dim(value, owner, 1, False) for value in split]
            return jnp.concatenate([value.astype(BF16) for value in chosen], axis=0)

        up_sent = up_of(rep_count - 1 - side)
        if last:
            grad_other = after(grad_other, dq)
            state, _ = after((other, grad_other), sents)
            dq_other = across(dq)
            hidden_other = feed(state, other_heads, layer, layer, weights)
            sents = stepped(hidden_other[0])
            dq_other = after(dq_other, hidden_other[0])
            up_got = across(up_sent)
            back_other = other_back(sents + [dq_other, up_sent])
            sents = stepped(back_other[3])
            up_got = after(up_got, back_other[3])
            sums = wide_sums(back_other, sents + [up_got])
            sents = stepped([sums[0].kept, sums[1].kept])
            for one in sums:
                one.advance(sents)
            stepped(sents_of(sums))
        else:
            pending[2].advance(up_k[-1])
            sents = stepped(up_k[-1])
            for one in sums:
                one.advance(sents)
            dq, up_sent = after((dq, up_sent), sents_of(sums))
            dq = turned(dq)
            up_got = across(up_sent)
            sents = stepped(sents_of(sums))
            dq = after(dq, sents)
            dq_other = across(dq)
            pending[2].advance(sents)
            sents = stepped(None)
            up_got = after(up_got, sents)
        while any(late.got is not None for late in d_lat):
            stepped(None)
        d_lat = jnp.concatenate([late.value.reshape(toks, size) for late in d_lat], axis=1)
        d_lat_other = across(d_lat)
        state = own if layer else natural_own.astype(F32)
        grad_own, attn_gain_own = project_back(d_in_own, dq, d_lat, state, layer)
        if last:
            other_input = (back_other[3], dq_other, d_lat_other, other)
        normed = [
            picked(pick, value)
            for value in ((normed_own, normed_other) if layer else natural_normed)
        ]

        up_rows = (up_of(side).astype(F32) + up_got.astype(F32)).astype(BF16)
        up_rows = jnp.concatenate(
            [up_rows[:, at * block : (at + 1) * block] for at in range(folds)], axis=2
        ).reshape(kept_rows, folds * size)
        up_rows = dot(to_halving, up_rows).astype(BF16)
        vectors = jnp.where(
            vector_at == 0,
            back_own[6] + back_other[6],
            jnp.where(
                vector_at == 1,
                back_own[7] + back_other[7],
                jnp.where(vector_at == 2, attn_gain_own[None], 0.0),
            ),
        )
        vectors_other = jnp.where(vector_at == 3, attn_gain_own[None], 0.0)
        vectors = (
            dot_as(pick, vectors.astype(BF16), NT) + dot_as(pick_other, vectors_other.astype(BF16), NT)
        ).astype(BF16)
        terms = [(normed, [dq, dq_other]), (normed, [d_lat, d_lat_other])]
        rest = HalvingSum(trade, pair_sum(terms, [up_rows, vectors]), bits)
        if not last:
            sums[1].advance(rest.sent)
            sums[0].advance(sums[1].sent)
            for _ in bits[1:]:
                rest.advance(sums[0].sent)
            for one in (sums[1], sums[0]):
                while one.result is None:
                    one.advance(rest.sent)
        sums.append(rest)
        pending = sums
        layer_sums.insert(0, sums)
    layer_grads = []
    for sums in layer_sums:
        g_gate_up, g_plain, g_rest = [one.finish() for one in sums]
        lat_at, up_at = heads_dim, heads_dim + GROUPS * size
        vectors_at = up_at + folds * size
        g_up = jnp.concatenate(
            [g_rest[:, up_at + at * size : up_at + (at + 1) * size] for at in range(folds)]
        )
        layer_grads.append(
            (
                g_rest[:, vectors_at + 2] + across(g_rest[:, vectors_at + 3]),
                g_rest[:, :lat_at],
                g_rest[:, lat_at:up_at],
                g_up.T,
                g_plain[:, hidden:].T,
                g_rest[:, vectors_at + 1],
                g_rest[:, vectors_at],
                g_gate_up,
                g_plain[:, :hidden].T,
            )
        )
    stacked = [jnp.stack([grads[member] for grads in layer_grads]) for member in range(9)]
    input_grad = grad_own.astype(BF16)
    return (
        placed(output, output_moved),
        placed(input_grad, across(input_grad)),
        *stacked,
    )


def solution(mesh):
    rows = P(None, "seq", None)
    scattered = P(None, ("seq", "rep"))
    first = P(None, ("seq", "rep"), None)
    second = P(None, None, ("seq", "rep"))
    return jax.shard_map(
        shards,
        mesh=mesh,
        in_specs=(rows, rows, P(None, "seq")) + (P(),) * 12,
        out_specs=(
            rows,
            rows,
            scattered,
            first,
            first,
            second,
            second,
            scattered,
            scattered,
            first,
            second,
        ),
        check_vma=False,
    )
```

```python
import functools

import jax
import jax.numpy as jnp
from jax import lax
from jax.experimental import pallas as pl
from jax.experimental.pallas import tpu as pltpu
from jax.sharding import PartitionSpec as P

HD = 64
LAYERS = 2
GROUPS = 2
NEG_FILL = -1e30
LOG2E = 1.4426950408889634
ATT_SCALE = HD ** (-0.5)
NT = (((1,), (1,)), ((), ()))
TN = (((0,), (0,)), ((), ()))
F32 = jnp.float32
BF16 = jnp.bfloat16
KEY_BLOCK = 512
QUERY_BLOCK = 1024
FORWARD_QUERIES = 256
FEED_STEP, FEED_AHEAD = 768, 16
BACK_STEP, BACK_AHEAD = 1408, 6


def dot_as(left, right, dims):
    return lax.dot_general(left, right, dims, preferred_element_type=F32)


def dot(left, right):
    return jnp.dot(left, right, preferred_element_type=F32)


def order_keys(scalars, lat_ref, keys, keys_t, seq_count, half):
    for piece in range(2 * seq_count):
        slot = scalars[2 + piece]
        keys[pl.ds(piece * half, half), :] = lat_ref[0, slot, pl.ds((piece % 2) * half, half), :]
    for first in range(0, 2 * seq_count * half, 256):
        keys_t[:, first : first + 256] = keys[first : first + 256, :].T


def block_bounds(scalars, row, part, half, seq_count):
    first = scalars[part]
    cut = scalars[2 + 2 * seq_count + row]
    last = first + half - 1
    low_min = jnp.where(first >= cut, cut, 0)
    low_max = jnp.where(last >= cut, cut, 0)
    return first, cut, low_min // KEY_BLOCK, last // KEY_BLOCK + 1, low_max


def hide(scores, block_at, first, cut, half):
    lanes = lax.broadcasted_iota(jnp.int32, (1, scores.shape[1]), 1)
    query_at = first + lanes % half
    low = jnp.where(query_at >= cut, cut, 0)
    key_at = block_at * KEY_BLOCK + lax.broadcasted_iota(jnp.int32, scores.shape, 0)
    return jnp.where((key_at <= query_at) & (key_at >= low), scores, NEG_FILL)


def over_blocks(bounds, block):
    first, _, start, stop, low_max = bounds

    def body(block_at, carry):
        edge = (block_at * KEY_BLOCK + KEY_BLOCK - 1 > first) | (block_at * KEY_BLOCK < low_max)

        @pl.when(edge)
        def _():
            block(block_at, True)

        @pl.when(jnp.logical_not(edge))
        def _():
            block(block_at, False)

        return carry

    lax.fori_loop(start, stop, body, 0)


def attend_kernel(
    scalars,
    q_ref,
    lat_ref,
    up_k_ref,
    up_v_ref,
    *refs,
    seq_count,
    half,
    heads,
):
    out_ref, out_t_ref, log_ref, query_ref, mixed_ref, keys, keys_t, top, total, acc = refs[-10:]
    row, part = pl.program_id(0), pl.program_id(1)

    @pl.when(part == 0)
    def _():
        order_keys(scalars, lat_ref, keys, keys_t, seq_count, half)

    for head in range(heads):
        feats = slice(head * HD, (head + 1) * HD)
        lifted = dot_as(q_ref[0, 0, feats, :], up_k_ref[feats, :], TN)
        query_ref[0, 0, head * half : (head + 1) * half, :] = (lifted * (LOG2E * ATT_SCALE)).astype(
            BF16
        )
    top[...] = jnp.full_like(top, NEG_FILL)
    total[...] = jnp.zeros_like(total)
    acc[...] = jnp.zeros_like(acc)
    bounds = block_bounds(scalars, row, part, half, seq_count)
    columns = heads * half
    width = min(FORWARD_QUERIES, columns)

    def block(block_at, edge):
        at = pl.multiple_of(block_at * KEY_BLOCK, KEY_BLOCK)
        key_rows = keys[pl.ds(at, KEY_BLOCK), :]
        key_cols = keys_t[:, pl.ds(at, KEY_BLOCK)]
        parts = [slice(col, col + width) for col in range(0, columns, width)]
        olds = [(top[:, cols], total[:, cols]) for cols in parts]

        def scores_of(cols):
            scores = dot_as(key_rows, query_ref[0, 0, cols, :], NT)
            return hide(scores, block_at, bounds[0], bounds[1], half) if edge else scores

        all_scores = [scores_of(cols) for cols in parts]
        for cols, scores, (old_top, old_total) in zip(parts, all_scores, olds):
            new_top = jnp.maximum(old_top, jnp.max(scores, axis=0, keepdims=True))
            probs = jnp.exp2(scores - new_top)
            fade = jnp.exp2(old_top - new_top)
            total[:, cols] = old_total * fade + jnp.sum(probs, axis=0, keepdims=True)
            top[:, cols] = new_top
            acc[:, cols] = acc[:, cols] * fade + dot(key_cols, probs.astype(BF16))

    over_blocks(bounds, block)
    mixed_ref[0, 0, :, :] = (acc[...] * (1.0 / total[...])).astype(BF16)
    log_ref[0, 0, :, :] = top[...] + jnp.log2(total[...])
    for head in range(heads):
        feats = slice(head * HD, (head + 1) * HD)
        out_t = dot(
            up_v_ref[feats, :], mixed_ref[0, 0, :, head * half : (head + 1) * half]
        ).astype(BF16)
        out_t_ref[0, 0, feats, :] = out_t
        out_ref[0, 0, :, feats] = out_t.T


def attend_back_kernel(
    scalars,
    q_ref,
    d_out_ref,
    out_ref,
    lat_ref,
    up_k_ref,
    up_v_ref,
    query_ref,
    mixed_ref,
    log_ref,
    *refs,
    seq_count,
    half,
    heads,
):
    dq_ref, d_lat_ref, d_up_k_ref, d_up_v_ref = refs[-11:-7]
    keys, keys_t, d_keys, query_plain, d_mixed, delta, d_query = refs[-7:]
    row, part = pl.program_id(0), pl.program_id(1)

    @pl.when(part == 0)
    def _():
        order_keys(scalars, lat_ref, keys, keys_t, seq_count, half)
        d_keys[...] = jnp.zeros_like(d_keys)

    @pl.when((part == 0) & (row == 0))
    def _():
        d_up_k_ref[...] = jnp.zeros_like(d_up_k_ref)
        d_up_v_ref[...] = jnp.zeros_like(d_up_v_ref)

    for head in range(heads):
        feats = slice(head * HD, (head + 1) * HD)
        cols = slice(head * half, (head + 1) * half)
        d_out = d_out_ref[0, 0, feats, :]
        query_plain[cols, :] = (
            dot_as(q_ref[0, 0, feats, :], up_k_ref[feats, :], TN) * ATT_SCALE
        ).astype(BF16)
        d_mixed[cols, :] = dot_as(d_out, up_v_ref[feats, :], TN).astype(BF16)
        delta[:, cols] = jnp.sum(
            d_out.astype(F32) * out_ref[0, 0, feats, :].astype(F32), axis=0, keepdims=True
        )
    d_query[...] = jnp.zeros_like(d_query)
    bounds = block_bounds(scalars, row, part, half, seq_count)
    columns = heads * half
    width = min(QUERY_BLOCK, columns)

    def block(block_at, edge):
        at = pl.multiple_of(block_at * KEY_BLOCK, KEY_BLOCK)
        key_rows = keys[pl.ds(at, KEY_BLOCK), :]
        key_cols = keys_t[:, pl.ds(at, KEY_BLOCK)]
        key_total = d_keys[pl.ds(at, KEY_BLOCK), :]
        for col in range(0, columns, width):
            cols = slice(col, col + width)
            scores = dot_as(key_rows, query_ref[0, 0, cols, :], NT)
            if edge:
                scores = hide(scores, block_at, bounds[0], bounds[1], half)
            probs = jnp.exp2(scores - log_ref[0, 0, :, cols])
            d_probs = dot_as(key_rows, d_mixed[cols, :], NT)
            d_scores = (probs * (d_probs - delta[:, cols])).astype(BF16)
            key_total = key_total + (
                dot(d_scores, query_plain[cols, :]) + dot(probs.astype(BF16), d_mixed[cols, :])
            )
            d_query[:, cols] += dot(key_cols, d_scores)
        d_keys[pl.ds(at, KEY_BLOCK), :] = key_total

    over_blocks(bounds, block)
    for head in range(heads):
        feats = slice(head * HD, (head + 1) * HD)
        cols = slice(head * half, (head + 1) * half)
        d_lifted = (d_query[:, cols] * ATT_SCALE).astype(BF16)
        dq_ref[0, 0, :, feats] = dot(up_k_ref[feats, :], d_lifted).astype(BF16).T
        d_up_k_ref[feats, :] += dot_as(q_ref[0, 0, feats, :], d_lifted, NT)
        d_up_v_ref[feats, :] += dot_as(d_out_ref[0, 0, feats, :], mixed_ref[0, 0, :, cols], NT)

    @pl.when(part == 1)
    def _():
        for piece in range(2 * seq_count):
            slot = scalars[2 + piece]
            d_lat_ref[0, slot, pl.ds((piece % 2) * half, half), :] = d_keys[
                pl.ds(piece * half, half), :
            ].astype(BF16)


def attention_sizes(queries_t, lats):
    rows, _, feats, half = queries_t.shape
    group_feats = feats // GROUPS
    heads = group_feats // HD
    seq_count, size = lats.shape[1], lats.shape[3]
    return rows, half, group_feats, heads, heads * half, seq_count, size, seq_count * 2 * half


def head_spec(group_feats, half, group):
    return pl.BlockSpec((1, 1, group_feats, half), lambda row, part, _: (row, part, group, 0))


def token_spec(group_feats, half, group):
    return pl.BlockSpec((1, 1, half, group_feats), lambda row, part, _: (row, part, 0, group))


def lat_spec(lats):
    return pl.BlockSpec((1,) + lats.shape[1:], lambda row, part, _: (row, 0, 0, 0))


ANY = pl.BlockSpec(memory_space=pl.ANY)


def plain_spec(*block):
    return pl.BlockSpec((1, 1) + block, lambda row, part, _: (row, part, 0, 0))


def up_spec(group_feats, size, at):
    return pl.BlockSpec((group_feats, size), lambda row, part, _: (at, 0))


def in_hbm(value):
    return pltpu.with_memory_space_constraint(value, pltpu.HBM)


def attend(scalars, queries_t, lats, up_t, group, filled):
    rows, half, group_feats, heads, columns, seq_count, size, keys = attention_sizes(
        queries_t, lats
    )
    return pl.pallas_call(
        functools.partial(
            attend_kernel, seq_count=seq_count, half=half, heads=heads
        ),
        grid_spec=pltpu.PrefetchScalarGridSpec(
            num_scalar_prefetch=1,
            grid=(rows, 2),
            in_specs=[
                head_spec(group_feats, half, group),
                lat_spec(lats),
                up_spec(group_feats, size, group),
                up_spec(group_feats, size, GROUPS + group),
            ]
            + [ANY] * len(filled),
            out_specs=[
                token_spec(group_feats, half, group),
                plain_spec(group_feats, half),
                plain_spec(1, columns),
                plain_spec(columns, size),
                plain_spec(size, columns),
            ],
            scratch_shapes=[
                pltpu.VMEM((keys, size), BF16),
                pltpu.VMEM((size, keys), BF16),
                pltpu.VMEM((1, columns), F32),
                pltpu.VMEM((1, columns), F32),
                pltpu.VMEM((size, columns), F32),
            ],
        ),
        out_shape=[
            jax.ShapeDtypeStruct((rows, 2, half, GROUPS * group_feats), BF16),
            pltpu.HBM((rows, 2, group_feats, half), BF16),
            pltpu.HBM((rows, 2, 1, columns), F32),
            pltpu.HBM((rows, 2, columns, size), BF16),
            pltpu.HBM((rows, 2, size, columns), BF16),
        ],
        compiler_params=pltpu.CompilerParams(
            dimension_semantics=("arbitrary", "arbitrary"), vmem_limit_bytes=40 << 20
        ),
        cost_estimate=pl.CostEstimate(
            flops=rows * 2 * columns * keys * size * 2,
            bytes_accessed=rows * (2 * keys * size + 8 * columns * size),
            transcendentals=rows * columns * keys,
        ),
        input_output_aliases={5: 0} if filled else {},
        name="attend",
    )(scalars, queries_t, lats, up_t, up_t, *filled)


def attend_back(
    scalars, queries_t, d_heads_t, heads_t, lats, up_t, kept, group, filled
):
    rows, half, group_feats, heads, columns, seq_count, size, keys = attention_sizes(
        queries_t, lats
    )
    logs, lifted, mixed = kept
    return pl.pallas_call(
        functools.partial(
            attend_back_kernel, seq_count=seq_count, half=half, heads=heads
        ),
        grid_spec=pltpu.PrefetchScalarGridSpec(
            num_scalar_prefetch=1,
            grid=(rows, 2),
            in_specs=[
                head_spec(group_feats, half, group),
                head_spec(group_feats, half, group),
                plain_spec(group_feats, half),
                lat_spec(lats),
                up_spec(group_feats, size, group),
                up_spec(group_feats, size, GROUPS + group),
                plain_spec(columns, size),
                plain_spec(size, columns),
                plain_spec(1, columns),
            ]
            + [ANY] * len(filled),
            out_specs=[
                token_spec(group_feats, half, group),
                lat_spec(lats),
                up_spec(group_feats, size, 0),
                up_spec(group_feats, size, 0),
            ],
            scratch_shapes=[
                pltpu.VMEM((keys, size), BF16),
                pltpu.VMEM((size, keys), BF16),
                pltpu.VMEM((keys, size), F32),
                pltpu.VMEM((columns, size), BF16),
                pltpu.VMEM((columns, size), BF16),
                pltpu.VMEM((1, columns), F32),
                pltpu.VMEM((size, columns), F32),
            ],
        ),
        out_shape=[
            jax.ShapeDtypeStruct((rows, 2, half, GROUPS * group_feats), BF16),
            jax.ShapeDtypeStruct(lats.shape, BF16),
            jax.ShapeDtypeStruct((group_feats, size), F32),
            jax.ShapeDtypeStruct((group_feats, size), F32),
        ],
        compiler_params=pltpu.CompilerParams(
            dimension_semantics=("arbitrary", "arbitrary"), vmem_limit_bytes=48 << 20
        ),
        cost_estimate=pl.CostEstimate(
            flops=rows * 5 * columns * keys * size * 2,
            bytes_accessed=rows * (4 * keys * size + 12 * columns * size),
            transcendentals=rows * columns * keys,
        ),
        input_output_aliases={10: 0} if filled else {},
        name="attend_back",
    )(
        scalars,
        *map(
            in_hbm, (queries_t, d_heads_t, heads_t, lats, up_t, up_t, lifted, mixed, logs)
        ),
        *filled,
    )


def rms_scale(value_rows):
    return lax.rsqrt(jnp.mean(value_rows * value_rows, axis=-1, keepdims=True) + 1e-06)


def norm_back(grad_in, value_rows, scale_rows, gain_vec):
    normed = value_rows * scale_rows
    upstream = grad_in * gain_vec
    return (
        scale_rows * (upstream - normed * jnp.mean(upstream * normed, axis=-1, keepdims=True)),
        jnp.sum(grad_in * normed, axis=0),
    )


def hidden_chunks(hidden, step):
    return [(at, min(step, hidden - at)) for at in range(0, hidden, step)]


class Copies:
    def __init__(self, sems, ahead):
        self.sems, self.made, self.begun, self.done, self.ahead = sems, [], 0, 0, ahead

    def add(self, source, target):
        self.made.append(pltpu.make_async_copy(source, target, self.sems.at[len(self.made)]))

    def begin(self, count):
        while self.begun < min(count, len(self.made)):
            self.made[self.begun].start()
            self.begun += 1

    def need(self, count):
        while self.done < count:
            self.made[self.done].wait()
            self.done += 1
            self.begin(self.done + self.ahead)


def feed_kernel(
    heads,
    state,
    bias,
    gain,
    next_gain,
    w_out,
    w_both,
    w_down,
    hidden_in,
    normed_mlp,
    gate,
    up,
    act,
    following,
    normed_next,
    v_heads,
    v_state,
    v_out,
    v_gate_w,
    v_up_w,
    v_down_w,
    v_normed,
    v_gate,
    v_up,
    v_act,
    v_next,
    v_normed_next,
    in_sems,
    out_sems,
    *,
    layer,
    hidden,
):
    chunks = hidden_chunks(hidden, FEED_STEP)
    loads, stores = Copies(in_sems, FEED_AHEAD), Copies(out_sems, 1)
    loads.add(heads, v_heads)
    loads.add(state, v_state)
    loads.add(w_out.at[layer], v_out)
    for at, count in chunks:
        cols = pl.ds(at, count)
        loads.add(w_both.at[layer, :, cols], v_gate_w.at[:, cols])
        loads.add(w_both.at[layer, :, pl.ds(hidden + at, count)], v_up_w.at[:, cols])
        loads.add(w_down.at[layer, cols, :], v_down_w.at[cols, :])
    loads.begin(FEED_AHEAD)
    loads.need(3)

    def store(source, target):
        stores.add(source, target)
        stores.begin(len(stores.made))

    value = v_state[...] + (dot(v_heads[...], v_out[...]) + bias[0])
    v_state[...] = value
    store(v_state, hidden_in)
    normed = (value * rms_scale(value) * gain[0]).astype(BF16)
    v_normed[...] = normed
    store(v_normed, normed_mlp)
    v_next[...] = value
    needed = 3
    for at, count in chunks:
        cols = pl.ds(at, count)
        loads.need(needed + 2)
        gate_part = dot(v_normed[...], v_gate_w[:, cols])
        up_part = dot(v_normed[...], v_up_w[:, cols])
        act_part = (gate_part * jax.nn.sigmoid(gate_part) * up_part).astype(BF16)
        v_gate[:, cols] = gate_part.astype(BF16)
        v_up[:, cols] = up_part.astype(BF16)
        v_act[:, cols] = act_part
        store(v_gate.at[:, cols], gate.at[:, cols])
        store(v_up.at[:, cols], up.at[:, cols])
        store(v_act.at[:, cols], act.at[:, cols])
        needed += 3
        loads.need(needed)
        v_next[...] += dot(act_part, v_down_w[cols, :])
    value = v_next[...]
    store(v_next, following)
    v_normed_next[...] = (value * rms_scale(value) * next_gain[0]).astype(BF16)
    store(v_normed_next, normed_next)
    stores.need(len(stores.made))


def vector_spec(at, width):
    return pl.BlockSpec((1, 1, width), lambda step: (at, 0, 0))


def feed(state, heads, layer, next_layer, weights):
    out_weight, out_bias, mlp_gain, attn_gain, gate_up_matrix, down_matrix = weights
    toks, width = state.shape
    hidden = down_matrix.shape[1]
    count = len(hidden_chunks(hidden, FEED_STEP))
    wide = lambda dtype: jax.ShapeDtypeStruct((toks, width), dtype)
    tiled = jax.ShapeDtypeStruct((toks, hidden), BF16)
    return pl.pallas_call(
        functools.partial(feed_kernel, layer=layer, hidden=hidden),
        grid=(1,),
        in_specs=[ANY] * 2
        + [vector_spec(layer, width), vector_spec(layer, width), vector_spec(next_layer, width)]
        + [ANY] * 3,
        out_specs=[ANY] * 7,
        out_shape=[wide(F32), wide(BF16), tiled, tiled, tiled, wide(F32), wide(BF16)],
        scratch_shapes=[
            pltpu.VMEM(heads.shape, BF16),
            pltpu.VMEM((toks, width), F32),
            pltpu.VMEM(out_weight.shape[1:], BF16),
            pltpu.VMEM((width, hidden), BF16),
            pltpu.VMEM((width, hidden), BF16),
            pltpu.VMEM((hidden, width), BF16),
            pltpu.VMEM((toks, width), BF16),
            pltpu.VMEM((toks, hidden), BF16),
            pltpu.VMEM((toks, hidden), BF16),
            pltpu.VMEM((toks, hidden), BF16),
            pltpu.VMEM((toks, width), F32),
            pltpu.VMEM((toks, width), BF16),
            pltpu.SemaphoreType.DMA((3 + 3 * count,)),
            pltpu.SemaphoreType.DMA((4 + 3 * count,)),
        ],
        compiler_params=pltpu.CompilerParams(
            dimension_semantics=("arbitrary",), vmem_limit_bytes=40 << 20
        ),
        cost_estimate=pl.CostEstimate(
            flops=2 * toks * width * (3 * hidden + width),
            bytes_accessed=2 * width * (3 * hidden + width) + 6 * toks * hidden,
            transcendentals=toks * hidden,
        ),
        name="feed",
    )(
        heads,
        state,
        out_bias[:, None],
        mlp_gain[:, None],
        attn_gain[:, None],
        out_weight,
        gate_up_matrix,
        down_matrix,
    )


def feed_back_kernel(
    grad,
    hidden_in,
    gain,
    gate,
    up,
    w_out,
    w_both,
    w_down,
    d_gate,
    d_up,
    d_mlp,
    d_hidden_in,
    d_attn,
    d_heads_t,
    gain_sum,
    bias_sum,
    v_grad,
    v_hidden_in,
    v_gate,
    v_up,
    v_out,
    v_gate_w,
    v_up_w,
    v_down_w,
    v_d_mlp,
    v_d_attn,
    v_d_heads,
    acc,
    in_sems,
    out_sems,
    *,
    layer,
    hidden,
    half,
):
    chunks = hidden_chunks(hidden, BACK_STEP)
    loads, stores = Copies(in_sems, BACK_AHEAD), Copies(out_sems, 1)
    loads.add(grad, v_grad)
    for at, count in chunks:
        cols = pl.ds(at, count)
        loads.add(gate.at[:, cols], v_gate.at[:, cols])
        loads.add(up.at[:, cols], v_up.at[:, cols])
        loads.add(w_down.at[layer, cols, :], v_down_w.at[cols, :])
        loads.add(w_both.at[layer, :, cols], v_gate_w.at[:, cols])
        loads.add(w_both.at[layer, :, pl.ds(hidden + at, count)], v_up_w.at[:, cols])
    loads.add(hidden_in, v_hidden_in)
    loads.add(w_out.at[layer], v_out)
    loads.begin(BACK_AHEAD)
    loads.need(1)

    def store(source, target):
        stores.add(source, target)
        stores.begin(len(stores.made))

    v_d_mlp[...] = v_grad[...].astype(BF16)
    store(v_d_mlp, d_mlp)
    needed = 1
    for at, count in chunks:
        cols = pl.ds(at, count)
        loads.need(needed + 3)
        d_act = dot_as(v_d_mlp[...], v_down_w[cols, :], NT)
        gate_part = v_gate[:, cols].astype(F32)
        up_part = v_up[:, cols].astype(F32)
        sig_gate = jax.nn.sigmoid(gate_part)
        d_gate_part = (d_act * up_part * sig_gate * (1.0 + gate_part * (1.0 - sig_gate))).astype(
            BF16
        )
        d_up_part = (d_act * gate_part * sig_gate).astype(BF16)
        v_gate[:, cols] = d_gate_part
        v_up[:, cols] = d_up_part
        store(v_gate.at[:, cols], d_gate.at[:, cols])
        store(v_up.at[:, cols], d_up.at[:, cols])
        needed += 5
        loads.need(needed)
        part = dot_as(d_gate_part, v_gate_w[:, cols], NT) + dot_as(d_up_part, v_up_w[:, cols], NT)
        if at == 0:
            acc[...] = part
        else:
            acc[...] += part
    loads.need(needed + 1)
    value = v_hidden_in[...]
    d_norm, gain_terms = norm_back(acc[...], value, rms_scale(value), gain[0])
    gain_sum[...] = gain_terms[None]
    total = v_grad[...] + d_norm
    low = total.astype(BF16)
    v_grad[...] = total
    store(v_grad, d_hidden_in)
    v_d_attn[...] = low
    store(v_d_attn, d_attn)
    bias_sum[...] = jnp.sum(low.astype(F32), axis=0, keepdims=True)
    loads.need(needed + 2)
    for piece in range(d_heads_t.shape[0]):
        v_d_heads[piece] = dot_as(v_out[...], low[piece * half : (piece + 1) * half], NT).astype(
            BF16
        )
    store(v_d_heads, d_heads_t)
    stores.need(len(stores.made))


def feed_back(grad, hidden_in, gate, up, layer, half, weights):
    out_weight, _, mlp_gain, _, gate_up_matrix, down_matrix = weights
    toks, width = grad.shape
    heads_dim = out_weight.shape[1]
    hidden = down_matrix.shape[1]
    vector_out = pl.BlockSpec((1, width), lambda step: (0, 0))
    wide = lambda dtype: jax.ShapeDtypeStruct((toks, width), dtype)
    tiled = jax.ShapeDtypeStruct((toks, hidden), BF16)
    pieces = toks // half
    count = len(hidden_chunks(hidden, BACK_STEP))
    return pl.pallas_call(
        functools.partial(feed_back_kernel, layer=layer, hidden=hidden, half=half),
        grid=(1,),
        in_specs=[ANY, ANY, vector_spec(layer, width)] + [ANY] * 5,
        out_specs=[ANY] * 6 + [vector_out] * 2,
        out_shape=[
            tiled,
            tiled,
            wide(BF16),
            wide(F32),
            wide(BF16),
            jax.ShapeDtypeStruct((pieces, heads_dim, half), BF16),
            jax.ShapeDtypeStruct((1, width), F32),
            jax.ShapeDtypeStruct((1, width), F32),
        ],
        scratch_shapes=[
            pltpu.VMEM((toks, width), F32),
            pltpu.VMEM((toks, width), F32),
            pltpu.VMEM((toks, hidden), BF16),
            pltpu.VMEM((toks, hidden), BF16),
            pltpu.VMEM(out_weight.shape[1:], BF16),
            pltpu.VMEM((width, hidden), BF16),
            pltpu.VMEM((width, hidden), BF16),
            pltpu.VMEM((hidden, width), BF16),
            pltpu.VMEM((toks, width), BF16),
            pltpu.VMEM((toks, width), BF16),
            pltpu.VMEM((pieces, heads_dim, half), BF16),
            pltpu.VMEM((toks, width), F32),
            pltpu.SemaphoreType.DMA((3 + 5 * count,)),
            pltpu.SemaphoreType.DMA((4 + 2 * count,)),
        ],
        compiler_params=pltpu.CompilerParams(
            dimension_semantics=("arbitrary",), vmem_limit_bytes=40 << 20
        ),
        cost_estimate=pl.CostEstimate(
            flops=2 * toks * width * (3 * hidden + heads_dim),
            bytes_accessed=2 * width * (3 * hidden + heads_dim) + 8 * toks * hidden,
            transcendentals=toks * hidden,
        ),
        name="feed_back",
    )(
        grad,
        hidden_in,
        mlp_gain[:, None],
        gate,
        up,
        out_weight,
        gate_up_matrix,
        down_matrix,
    )


def gated_sum_kernel(left_a, left_b, gate_a, gate_b, up_a, up_b, kept, sent):
    half_rows = kept.shape[0]

    def add(right_a, right_b):
        value = (dot(left_a[...], right_a[...]) + dot(left_b[...], right_b[...])).astype(BF16)
        kept[...] = value[:half_rows]
        sent[...] = value[half_rows:]

    first = pl.program_id(0) < pl.num_programs(0) // 2

    @pl.when(first)
    def _():
        add(gate_a, gate_b)

    @pl.when(jnp.logical_not(first))
    def _():
        add(up_a, up_b)


def gated_sum(lefts, gates, ups):
    rows, toks = lefts[0].shape
    hidden = gates[0].shape[1]
    tile = hidden // 2 if hidden % 256 == 0 else hidden
    count = hidden // tile
    whole = pl.BlockSpec((rows, toks), lambda step: (0, 0))
    gate_spec = pl.BlockSpec((toks, tile), lambda step: (0, jnp.minimum(step, count - 1)))
    up_spec_ = pl.BlockSpec((toks, tile), lambda step: (0, jnp.maximum(step - count, 0)))
    return pl.pallas_call(
        gated_sum_kernel,
        grid=(2 * count,),
        in_specs=[whole] * 2 + [gate_spec] * 2 + [up_spec_] * 2,
        out_specs=[pl.BlockSpec((rows // 2, tile), lambda step: (0, step))] * 2,
        out_shape=[jax.ShapeDtypeStruct((rows // 2, 2 * hidden), BF16)] * 2,
        compiler_params=pltpu.CompilerParams(
            dimension_semantics=("arbitrary",), vmem_limit_bytes=36 << 20
        ),
        cost_estimate=pl.CostEstimate(
            flops=8 * rows * toks * hidden,
            bytes_accessed=4 * hidden * (2 * toks + rows),
            transcendentals=0,
        ),
        name="gated_sum",
    )(*lefts, *gates, *ups)


def pair_sum_kernel(*refs, count):
    lefts, rights = refs[: 2 * count], refs[2 * count : 4 * count]
    kept, sent = refs[-2:]
    half_rows = kept.shape[0]
    at = 0
    for one in range(0, 2 * count, 2):
        cols = slice(at, at + rights[one].shape[1])
        value = (
            dot(lefts[one][...], rights[one][...]) + dot(lefts[one + 1][...], rights[one + 1][...])
        ).astype(BF16)
        kept[:, cols] = value[:half_rows]
        sent[:, cols] = value[half_rows:]
        at = cols.stop
    for extra in refs[4 * count : -2]:
        cols = slice(at, at + extra.shape[1])
        kept[:, cols] = extra[:half_rows]
        sent[:, cols] = extra[half_rows:]
        at = cols.stop


def pair_sum(terms, extras=()):
    rows, toks = terms[0][0][0].shape
    cols = sum(rights[0].shape[1] for _, rights in terms)
    total = cols + sum(value.shape[1] for value in extras)
    return pl.pallas_call(
        functools.partial(pair_sum_kernel, count=len(terms)),
        out_shape=[jax.ShapeDtypeStruct((rows // 2, total), BF16)] * 2,
        compiler_params=pltpu.CompilerParams(vmem_limit_bytes=36 << 20),
        cost_estimate=pl.CostEstimate(
            flops=4 * rows * toks * cols,
            bytes_accessed=4 * toks * cols + 2 * rows * total,
            transcendentals=0,
        ),
        name="pair_sum",
    )(*[left for lefts, _ in terms for left in lefts], *[r for _, rights in terms for r in rights], *extras)


class HalvingSum:
    def __init__(self, trade, pair, order):
        self.trade, self.order, self.step = trade, order, 1
        self.kept, self.sent = pair
        self.got = trade(self.sent, order[0])
        self.result = None

    def advance(self, gate=None):
        if self.result is not None:
            return
        kept, got = self.kept, self.got
        if gate is not None:
            (kept, got), _ = lax.optimization_barrier(((kept, got), gate))
        if self.step == len(self.order):
            self.result = kept.astype(F32) + got.astype(F32)
            return
        left = kept.shape[0] // 2
        self.sent = (kept[left:].astype(F32) + got[left:].astype(F32)).astype(BF16)
        self.kept = (kept[:left].astype(F32) + got[:left].astype(F32)).astype(BF16)
        self.got = self.trade(self.sent, self.order[self.step])
        self.step += 1

    def finish(self):
        while self.result is None:
            self.advance()
        return self.result


class SlotSum:
    result = None

    def __init__(self, trade, value, order):
        self.trade, self.value, self.order, self.step = trade, value, order, 0
        self.send()

    def send(self):
        left = self.value.shape[1] // 2
        self.kept, self.sent = self.value[:, :left], self.value[:, left:]
        self.got = self.trade(self.sent, self.order[self.step])
        self.step += 1

    def advance(self, gate):
        if self.got is None:
            return
        kept, got = self.kept, self.got
        if gate is not None:
            (kept, got), _ = lax.optimization_barrier(((kept, got), gate))
        self.value = (kept.astype(F32) + got.astype(F32)).astype(BF16)
        self.got = None
        if self.step < len(self.order):
            self.send()
        else:
            self.sent = self.value


def shards(
    tokens,
    cotangent,
    domain_ids,
    domain_counts,
    domain_weights,
    seq_cuts,
    attn_gain,
    query_weight,
    latent_weight,
    latent_up,
    out_weight,
    out_bias,
    mlp_gain,
    gate_up_matrix,
    down_matrix,
):
    seq_count = lax.axis_size("seq")
    rep_count = lax.axis_size("rep")
    place = lax.axis_index("seq").astype(jnp.int32)
    side = lax.axis_index("rep").astype(jnp.int32)
    seq_rows, loc_len, width = tokens.shape
    rows = seq_rows // rep_count
    half = loc_len // 2
    toks = rows * loc_len
    heads_dim = query_weight.shape[2]
    size = latent_up.shape[1]
    hidden = down_matrix.shape[1]
    group_cols = heads_dim // GROUPS
    bits = [1 << at for at in range(seq_count.bit_length() - 1)]
    far_late = bits[:1] + bits[2:3] + bits[1:2] + bits[3:]
    weights = (out_weight, out_bias, mlp_gain, attn_gain, gate_up_matrix, down_matrix)

    def after(value, gate):
        return lax.optimization_barrier((value, gate))[0]

    def swap_ends(value):
        moves = [(at, seq_count - 1 - at) for at in range(seq_count)]
        return lax.ppermute(value, "seq", moves)

    def across(value):
        return lax.ppermute(value, "rep", [(at, rep_count - 1 - at) for at in range(rep_count)])

    def trade(value, bit):
        return lax.ppermute(value, "seq", [(at, at ^ bit) for at in range(seq_count)])

    def rows_of(value, owner):
        return lax.dynamic_slice_in_dim(value, owner * rows, rows, 0)

    def turned(value):
        split = value.reshape((rows, 2, half) + value.shape[1:])
        return jnp.stack([split[:, 0], swap_ends(split[:, 1])], axis=1).reshape(value.shape)

    def tokens_of(value, owner):
        return rows_of(value, owner).reshape((toks,) + value.shape[2:])

    def spread(values, fill_at, fill):
        values = [value.reshape(rows, 1, loc_len, size) for value in values]
        filled = None
        for at, bit in enumerate(reversed(bits)):
            got = [trade(value, bit) for value in values]
            if at == fill_at:
                filled = fill(values)
                values, got = after((values, got), filled)
            values = [jnp.concatenate(pair, axis=1) for pair in zip(values, got)]
        return values, filled

    block = width // (seq_count * rep_count)
    kept_rows = seq_count * block
    row_at = jnp.arange(kept_rows, dtype=jnp.int32)
    col_at = jnp.arange(width, dtype=jnp.int32)

    def halving_step(order):
        distance = jnp.zeros_like(row_at)
        for level, bit in enumerate(order):
            distance = distance + (row_at // block // (seq_count // 2 >> level)) % 2 * bit
        return place ^ distance

    def picker(order, owner):
        source = (halving_step(order) * rep_count + owner) * block + row_at % block
        return (source[:, None] == col_at[None, :]).astype(BF16)

    pick, pick_late = picker(bits, side), picker(far_late, side)
    pick_other = picker(bits, rep_count - 1 - side)
    vector_at = jnp.arange(128, dtype=jnp.int32)[:, None]
    to_halving = (
        (halving_step(bits) * block + row_at % block)[:, None] == row_at[None, :]
    ).astype(BF16)

    def picked(picks, value):
        return dot_as(picks, value, NT).astype(BF16)

    domain_total = domain_counts.shape[0]
    all_tokens = seq_rows * loc_len * seq_count
    per_domain = domain_weights * (all_tokens / domain_total) / domain_counts.astype(F32)
    one_hot = (domain_ids[..., None] == jnp.arange(domain_total, dtype=jnp.int32)).astype(F32)
    row_scale = jnp.sum(one_hot * per_domain, axis=-1)
    pieces = jnp.arange(2 * seq_count, dtype=jnp.int32)

    def scalars_of(zigzag):
        source = pieces // 2
        if zigzag:
            source = jnp.where(pieces % 2 == 0, source, (2 * seq_count - 1 - pieces) // 2)
        distance = source ^ place
        slots = jnp.zeros_like(pieces)
        for level, bit in enumerate(bits):
            slots = slots + distance // bit % 2 * (seq_count // 2 >> level)
        starts = jnp.stack([place * loc_len, (2 * seq_count - 1 - 2 * place) * half])
        return jnp.concatenate([starts, slots, rows_of(seq_cuts, side)])

    def project_back(d_hidden_in, dq, d_lat, state, layer):
        d_normed = dot_as(dq, query_weight[layer], NT) + dot_as(d_lat, latent_weight[layer], NT)
        d_norm, g_gain = norm_back(d_normed, state, rms_scale(state), attn_gain[layer])
        return d_hidden_in + d_norm, g_gain

    def grad_of(owner, gate):
        value = tokens_of(cotangent, owner).astype(F32) * tokens_of(row_scale, owner)[:, None]
        split = value.reshape(rows, 2, half, width)
        swapped = swap_ends(after(split[:, 1].astype(BF16), gate))
        return jnp.stack([split[:, 0], swapped.astype(F32)], axis=1).reshape(toks, width)

    def first_normed(state):
        return (state * rms_scale(state) * attn_gain[0]).astype(BF16)

    natural_own = tokens_of(tokens, side)
    natural_normed = [first_normed(natural_own.astype(F32))]
    hidden_other = None
    saved = []
    for layer in range(LAYERS):
        last = layer == LAYERS - 1
        next_layer = min(layer + 1, LAYERS - 1)
        scalars = scalars_of(layer > 0)
        lat_input = normed_own if layer else natural_normed[0]
        lats = [
            dot(lat_input, latent_weight[layer, :, group * size : (group + 1) * size]).astype(BF16)
            for group in range(GROUPS)
        ]
        if layer == 0:
            lats, own = spread(
                lats, 2, lambda values: turned(after(natural_own, values)).astype(F32)
            )
            normed_own = first_normed(own)
        else:
            lats, hidden_other = spread(
                lats,
                0,
                lambda values: feed(
                    after(other, values), other_heads, layer - 1, next_layer, weights
                ),
            )
            saved[-1].append(hidden_other)
            other, normed_other = hidden_other[5:]
        queries_t = jnp.einsum(
            "rpid,df->rpfi",
            normed_own.reshape(rows, 2, half, width),
            query_weight[layer],
            preferred_element_type=F32,
        ).astype(BF16)
        up_t = latent_up[layer].T
        heads, attended = [], []
        for group in range(GROUPS):
            out, *rest = attend(scalars, queries_t, lats[group], up_t, group, heads)
            heads = [out]
            attended.append(rest)
            if group == 0:
                if last:
                    grad_own = grad_of(side, out)
                else:
                    natural_other = tokens_of(after(tokens, out), rep_count - 1 - side)
                    natural_normed.append(first_normed(natural_other.astype(F32)))
                    other = turned(natural_other)
        heads = heads[0].reshape(toks, heads_dim)
        other_heads = across(heads)
        if last:
            own, grad_own = after((own, grad_own), heads)
        else:
            own, other = after((own, other), heads)
            other = other.astype(F32)
        hidden_own = feed(own, heads, layer, next_layer, weights)
        saved.append([own, normed_own, heads, hidden_own, lats, queries_t, up_t, attended, scalars])
        saved[-1] += [other, normed_other if layer else None, other_heads]
        own, normed_own = hidden_own[5:]

    def placed(value, moved):
        both = jnp.stack([value, moved]).reshape(2, rows, loc_len, width)
        return jnp.where(side == 0, both, both[::-1]).reshape(seq_rows, loc_len, width)

    output = turned(own.astype(BF16))
    grad_other = None
    pending = []
    other_input = None
    layer_sums = []
    for layer in reversed(range(LAYERS)):
        last = layer == LAYERS - 1
        own, normed_own, heads, hidden_own, lats, queries_t, up_t, attended, scalars = saved[layer][:9]
        other, normed_other, other_heads = saved[layer][9:12]
        back_own = feed_back(
            grad_own, hidden_own[0], hidden_own[2], hidden_own[3], layer, half, weights
        )
        d_heads_t = back_own[5].reshape(rows, 2, heads_dim, half)
        d_in_own = back_own[3]
        d_lat, up_k, up_v, filled = [], [], [], []

        def stepped(gate):
            for late in d_lat:
                late.advance(gate)
            return [late.sent for late in d_lat]

        def sents_of(sums):
            return [one.sent if one.result is None else one.result for one in sums]

        def wide_sums(back_other, gate):
            backs = (back_own, back_other)
            hiddens = (hidden_own, hidden_other)
            gates, acts = after(([back[0] for back in backs], [hid[4] for hid in hiddens]), gate)
            gated = gated_sum(
                [picked(pick, hid[1]) for hid in hiddens], gates, [back[1] for back in backs]
            )
            plain = pair_sum(
                [
                    ([picked(pick_late, back[2]) for back in backs], acts),
                    ([picked(pick_late, back[4]) for back in backs], [heads, other_heads]),
                ]
            )
            return [HalvingSum(trade, gated, bits), HalvingSum(trade, plain, far_late)]

        def other_back(gate):
            return feed_back(
                after(grad_other, gate),
                hidden_other[0],
                hidden_other[2],
                hidden_other[3],
                layer,
                half,
                weights,
            )

        if last:
            d_heads_t = after(d_heads_t, output)
            output_moved = across(output)
        else:
            d_in_own = turned(d_in_own.astype(BF16)).astype(F32)
            hidden_other = saved[layer][12]
            grad_other, _ = project_back(*after(other_input, back_own[3]), layer + 1)
            back_other = other_back((back_own[3], pending[2].sent))
            for late in pending[:2]:
                late.advance(back_other[3])
            pending[2].advance(back_other[3])
            sums = wide_sums(back_other, (sents_of(pending), d_in_own))
            for late in pending[:2]:
                late.advance([sums[0].kept, sums[1].kept])
            for one in sums:
                one.advance(sents_of(pending[:2]))
            d_heads_t = after(d_heads_t, sents_of(sums + pending))
        for group in range(GROUPS):
            dq, d_lat_one, up_k_one, up_v_one = attend_back(
                scalars,
                queries_t,
                d_heads_t,
                attended[group][0],
                lats[group],
                up_t,
                attended[group][1:],
                group,
                filled,
            )
            up_k.append(up_k_one)
            up_v.append(up_v_one)
            for late in (pending if group == 0 else []) + d_lat:
                late.advance(up_k_one)
            d_lat.append(SlotSum(trade, d_lat_one, bits))
            sents = sents_of(pending + d_lat)
            filled = [dq]
            if group == 0:
                d_heads_t = after(d_heads_t, (sents, output_moved) if last else sents)
                if last:
                    grad_other = grad_of(rep_count - 1 - side, sents)
        dq = dq.reshape(toks, heads_dim)
        up_block = latent_up.shape[2] // (seq_count * rep_count)
        folds = up_block // block
        split = [value.reshape(-1, rep_count, up_block, size) for value in up_k + up_v]

        def up_of(owner):
            chosen = [lax.dynamic_index_in_dim(value, owner, 1, False) for value in split]
            return jnp.concatenate([value.astype(BF16) for value in chosen], axis=0)

        up_sent = up_of(rep_count - 1 - side)
        if last:
            grad_other = after(grad_other, dq)
            state, _ = after((other, grad_other), sents)
            dq_other = across(dq)
            hidden_other = feed(state, other_heads, layer, layer, weights)
            sents = stepped(hidden_other[0])
            dq_other = after(dq_other, hidden_other[0])
            up_got = across(up_sent)
            back_other = other_back(sents + [dq_other, up_sent])
            sents = stepped(back_other[3])
            up_got = after(up_got, back_other[3])
            sums = wide_sums(back_other, sents + [up_got])
            sents = stepped([sums[0].kept, sums[1].kept])
            for one in sums:
                one.advance(sents)
            stepped(sents_of(sums))
        else:
            pending[2].advance(up_k[-1])
            sents = stepped(up_k[-1])
            for one in sums:
                one.advance(sents)
            dq, up_sent = after((dq, up_sent), sents_of(sums))
            dq = turned(dq)
            up_got = across(up_sent)
            sents = stepped((sents_of(sums), dq))
            dq_other = across(dq)
            pending[2].advance(sents)
            sents = stepped(None)
            up_got = after(up_got, sents)
        while any(late.got is not None for late in d_lat):
            stepped(None)
        d_lat = jnp.concatenate([late.value.reshape(toks, size) for late in d_lat], axis=1)
        d_lat_other = across(d_lat)
        if not last:
            for one in (sums[1], sums[0]):
                one.advance(d_lat)
        state = own if layer else natural_own.astype(F32)
        grad_own, attn_gain_own = project_back(d_in_own, dq, d_lat, state, layer)
        if last:
            other_input = (back_other[3], dq_other, d_lat_other, other)
        normed = [
            picked(pick, value)
            for value in ((normed_own, normed_other) if layer else natural_normed)
        ]

        up_rows = (up_of(side).astype(F32) + up_got.astype(F32)).astype(BF16)
        up_rows = jnp.concatenate(
            [up_rows[:, at * block : (at + 1) * block] for at in range(folds)], axis=2
        ).reshape(kept_rows, folds * size)
        up_rows = dot(to_halving, up_rows).astype(BF16)
        vectors = jnp.where(
            vector_at == 0,
            back_own[6] + back_other[6],
            jnp.where(
                vector_at == 1,
                back_own[7] + back_other[7],
                jnp.where(vector_at == 2, attn_gain_own[None], 0.0),
            ),
        )
        vectors_other = jnp.where(vector_at == 3, attn_gain_own[None], 0.0)
        vectors = (
            dot_as(pick, vectors.astype(BF16), NT) + dot_as(pick_other, vectors_other.astype(BF16), NT)
        ).astype(BF16)
        terms = [(normed, [dq, dq_other]), (normed, [d_lat, d_lat_other])]
        rest = HalvingSum(trade, pair_sum(terms, [up_rows, vectors]), bits)
        if not last:
            for _ in bits[1:]:
                rest.advance(None)
            for one in (sums[1], sums[0]):
                while one.result is None:
                    one.advance(rest.sent)
        sums.append(rest)
        pending = sums
        layer_sums.insert(0, sums)
    layer_grads = []
    for sums in layer_sums:
        g_gate_up, g_plain, g_rest = [one.finish() for one in sums]
        lat_at, up_at = heads_dim, heads_dim + GROUPS * size
        vectors_at = up_at + folds * size
        g_up = jnp.concatenate(
            [g_rest[:, up_at + at * size : up_at + (at + 1) * size] for at in range(folds)]
        )
        layer_grads.append(
            (
                g_rest[:, vectors_at + 2] + across(g_rest[:, vectors_at + 3]),
                g_rest[:, :lat_at],
                g_rest[:, lat_at:up_at],
                g_up.T,
                g_plain[:, hidden:].T,
                g_rest[:, vectors_at + 1],
                g_rest[:, vectors_at],
                g_gate_up,
                g_plain[:, :hidden].T,
            )
        )
    stacked = [jnp.stack([grads[member] for grads in layer_grads]) for member in range(9)]
    input_grad = grad_own.astype(BF16)
    return (
        placed(output, output_moved),
        placed(input_grad, across(input_grad)),
        *stacked,
    )


def solution(mesh):
    rows = P(None, "seq", None)
    scattered = P(None, ("seq", "rep"))
    first = P(None, ("seq", "rep"), None)
    second = P(None, None, ("seq", "rep"))
    return jax.shard_map(
        shards,
        mesh=mesh,
        in_specs=(rows, rows, P(None, "seq")) + (P(),) * 12,
        out_specs=(
            rows,
            rows,
            scattered,
            first,
            first,
            second,
            second,
            scattered,
            scattered,
            first,
            second,
        ),
        check_vma=False,
    )
```

```python
import functools

import jax
import jax.numpy as jnp
from jax import lax
from jax.experimental import pallas as pl
from jax.experimental.pallas import tpu as pltpu
from jax.sharding import PartitionSpec as P

HD = 64
LAYERS = 2
GROUPS = 2
NEG_FILL = -1e30
LOG2E = 1.4426950408889634
ATT_SCALE = HD ** (-0.5)
NT = (((1,), (1,)), ((), ()))
TN = (((0,), (0,)), ((), ()))
F32 = jnp.float32
BF16 = jnp.bfloat16
KEY_BLOCK = 512
QUERY_BLOCK = 1024
FORWARD_QUERIES = 256
FEED_STEP, FEED_AHEAD = 768, 16
BACK_STEP, BACK_AHEAD = 1408, 6


def dot_as(left, right, dims):
    return lax.dot_general(left, right, dims, preferred_element_type=F32)


def dot(left, right):
    return jnp.dot(left, right, preferred_element_type=F32)


def order_keys(scalars, lat_ref, keys, keys_t, seq_count, half):
    for piece in range(2 * seq_count):
        slot = scalars[2 + piece]
        keys[pl.ds(piece * half, half), :] = lat_ref[0, slot, pl.ds((piece % 2) * half, half), :]
    for first in range(0, 2 * seq_count * half, 256):
        keys_t[:, first : first + 256] = keys[first : first + 256, :].T


def block_bounds(scalars, row, part, half, seq_count):
    first = scalars[part]
    cut = scalars[2 + 2 * seq_count + row]
    last = first + half - 1
    low_min = jnp.where(first >= cut, cut, 0)
    low_max = jnp.where(last >= cut, cut, 0)
    return first, cut, low_min // KEY_BLOCK, last // KEY_BLOCK + 1, low_max


def hide(scores, block_at, first, cut, half):
    lanes = lax.broadcasted_iota(jnp.int32, (1, scores.shape[1]), 1)
    query_at = first + lanes % half
    low = jnp.where(query_at >= cut, cut, 0)
    key_at = block_at * KEY_BLOCK + lax.broadcasted_iota(jnp.int32, scores.shape, 0)
    return jnp.where((key_at <= query_at) & (key_at >= low), scores, NEG_FILL)


def over_blocks(bounds, block):
    first, _, start, stop, low_max = bounds

    def body(block_at, carry):
        edge = (block_at * KEY_BLOCK + KEY_BLOCK - 1 > first) | (block_at * KEY_BLOCK < low_max)

        @pl.when(edge)
        def _():
            block(block_at, True)

        @pl.when(jnp.logical_not(edge))
        def _():
            block(block_at, False)

        return carry

    lax.fori_loop(start, stop, body, 0)


def attend_kernel(
    scalars,
    q_ref,
    lat_ref,
    up_k_ref,
    up_v_ref,
    *refs,
    seq_count,
    half,
    heads,
):
    out_ref, out_t_ref, log_ref, query_ref, mixed_ref, keys, keys_t, top, total, acc = refs[-10:]
    row, part = pl.program_id(0), pl.program_id(1)

    @pl.when(part == 0)
    def _():
        order_keys(scalars, lat_ref, keys, keys_t, seq_count, half)

    for head in range(heads):
        feats = slice(head * HD, (head + 1) * HD)
        lifted = dot_as(q_ref[0, 0, feats, :], up_k_ref[feats, :], TN)
        query_ref[0, 0, head * half : (head + 1) * half, :] = (lifted * (LOG2E * ATT_SCALE)).astype(
            BF16
        )
    top[...] = jnp.full_like(top, NEG_FILL)
    total[...] = jnp.zeros_like(total)
    acc[...] = jnp.zeros_like(acc)
    bounds = block_bounds(scalars, row, part, half, seq_count)
    columns = heads * half
    width = min(FORWARD_QUERIES, columns)

    def block(block_at, edge):
        at = pl.multiple_of(block_at * KEY_BLOCK, KEY_BLOCK)
        key_rows = keys[pl.ds(at, KEY_BLOCK), :]
        key_cols = keys_t[:, pl.ds(at, KEY_BLOCK)]
        parts = [slice(col, col + width) for col in range(0, columns, width)]
        olds = [(top[:, cols], total[:, cols]) for cols in parts]

        def scores_of(cols):
            scores = dot_as(key_rows, query_ref[0, 0, cols, :], NT)
            return hide(scores, block_at, bounds[0], bounds[1], half) if edge else scores

        all_scores = [scores_of(cols) for cols in parts]
        for cols, scores, (old_top, old_total) in zip(parts, all_scores, olds):
            new_top = jnp.maximum(old_top, jnp.max(scores, axis=0, keepdims=True))
            probs = jnp.exp2(scores - new_top)
            fade = jnp.exp2(old_top - new_top)
            total[:, cols] = old_total * fade + jnp.sum(probs, axis=0, keepdims=True)
            top[:, cols] = new_top
            acc[:, cols] = acc[:, cols] * fade + dot(key_cols, probs.astype(BF16))

    over_blocks(bounds, block)
    mixed_ref[0, 0, :, :] = (acc[...] * (1.0 / total[...])).astype(BF16)
    log_ref[0, 0, :, :] = top[...] + jnp.log2(total[...])
    for head in range(heads):
        feats = slice(head * HD, (head + 1) * HD)
        out_t = dot(
            up_v_ref[feats, :], mixed_ref[0, 0, :, head * half : (head + 1) * half]
        ).astype(BF16)
        out_t_ref[0, 0, feats, :] = out_t
        out_ref[0, 0, :, feats] = out_t.T


def attend_back_kernel(
    scalars,
    q_ref,
    d_out_ref,
    out_ref,
    lat_ref,
    up_k_ref,
    up_v_ref,
    query_ref,
    mixed_ref,
    log_ref,
    *refs,
    seq_count,
    half,
    heads,
):
    dq_ref, d_lat_ref, d_up_k_ref, d_up_v_ref = refs[-11:-7]
    keys, keys_t, d_keys, query_plain, d_mixed, delta, d_query = refs[-7:]
    row, part = pl.program_id(0), pl.program_id(1)

    @pl.when(part == 0)
    def _():
        order_keys(scalars, lat_ref, keys, keys_t, seq_count, half)
        d_keys[...] = jnp.zeros_like(d_keys)

    @pl.when((part == 0) & (row == 0))
    def _():
        d_up_k_ref[...] = jnp.zeros_like(d_up_k_ref)
        d_up_v_ref[...] = jnp.zeros_like(d_up_v_ref)

    for head in range(heads):
        feats = slice(head * HD, (head + 1) * HD)
        cols = slice(head * half, (head + 1) * half)
        d_out = d_out_ref[0, 0, feats, :]
        query_plain[cols, :] = (
            dot_as(q_ref[0, 0, feats, :], up_k_ref[feats, :], TN) * ATT_SCALE
        ).astype(BF16)
        d_mixed[cols, :] = dot_as(d_out, up_v_ref[feats, :], TN).astype(BF16)
        delta[:, cols] = jnp.sum(
            d_out.astype(F32) * out_ref[0, 0, feats, :].astype(F32), axis=0, keepdims=True
        )
    d_query[...] = jnp.zeros_like(d_query)
    bounds = block_bounds(scalars, row, part, half, seq_count)
    columns = heads * half
    width = min(QUERY_BLOCK, columns)

    def block(block_at, edge):
        at = pl.multiple_of(block_at * KEY_BLOCK, KEY_BLOCK)
        key_rows = keys[pl.ds(at, KEY_BLOCK), :]
        key_cols = keys_t[:, pl.ds(at, KEY_BLOCK)]
        key_total = d_keys[pl.ds(at, KEY_BLOCK), :]
        for col in range(0, columns, width):
            cols = slice(col, col + width)
            scores = dot_as(key_rows, query_ref[0, 0, cols, :], NT)
            if edge:
                scores = hide(scores, block_at, bounds[0], bounds[1], half)
            probs = jnp.exp2(scores - log_ref[0, 0, :, cols])
            d_probs = dot_as(key_rows, d_mixed[cols, :], NT)
            d_scores = (probs * (d_probs - delta[:, cols])).astype(BF16)
            key_total = key_total + (
                dot(d_scores, query_plain[cols, :]) + dot(probs.astype(BF16), d_mixed[cols, :])
            )
            d_query[:, cols] += dot(key_cols, d_scores)
        d_keys[pl.ds(at, KEY_BLOCK), :] = key_total

    over_blocks(bounds, block)
    for head in range(heads):
        feats = slice(head * HD, (head + 1) * HD)
        cols = slice(head * half, (head + 1) * half)
        d_lifted = (d_query[:, cols] * ATT_SCALE).astype(BF16)
        dq_ref[0, 0, :, feats] = dot(up_k_ref[feats, :], d_lifted).astype(BF16).T
        d_up_k_ref[feats, :] += dot_as(q_ref[0, 0, feats, :], d_lifted, NT)
        d_up_v_ref[feats, :] += dot_as(d_out_ref[0, 0, feats, :], mixed_ref[0, 0, :, cols], NT)

    @pl.when(part == 1)
    def _():
        for piece in range(2 * seq_count):
            slot = scalars[2 + piece]
            d_lat_ref[0, slot, pl.ds((piece % 2) * half, half), :] = d_keys[
                pl.ds(piece * half, half), :
            ].astype(BF16)


def attention_sizes(queries_t, lats):
    rows, _, feats, half = queries_t.shape
    group_feats = feats // GROUPS
    heads = group_feats // HD
    seq_count, size = lats.shape[1], lats.shape[3]
    return rows, half, group_feats, heads, heads * half, seq_count, size, seq_count * 2 * half


def head_spec(group_feats, half, group):
    return pl.BlockSpec((1, 1, group_feats, half), lambda row, part, _: (row, part, group, 0))


def token_spec(group_feats, half, group):
    return pl.BlockSpec((1, 1, half, group_feats), lambda row, part, _: (row, part, 0, group))


def lat_spec(lats):
    return pl.BlockSpec((1,) + lats.shape[1:], lambda row, part, _: (row, 0, 0, 0))


ANY = pl.BlockSpec(memory_space=pl.ANY)


def plain_spec(*block):
    return pl.BlockSpec((1, 1) + block, lambda row, part, _: (row, part, 0, 0))


def up_spec(group_feats, size, at):
    return pl.BlockSpec((group_feats, size), lambda row, part, _: (at, 0))


def in_hbm(value):
    return pltpu.with_memory_space_constraint(value, pltpu.HBM)


def attend(scalars, queries_t, lats, up_t, group, filled):
    rows, half, group_feats, heads, columns, seq_count, size, keys = attention_sizes(
        queries_t, lats
    )
    return pl.pallas_call(
        functools.partial(
            attend_kernel, seq_count=seq_count, half=half, heads=heads
        ),
        grid_spec=pltpu.PrefetchScalarGridSpec(
            num_scalar_prefetch=1,
            grid=(rows, 2),
            in_specs=[
                head_spec(group_feats, half, group),
                lat_spec(lats),
                up_spec(group_feats, size, group),
                up_spec(group_feats, size, GROUPS + group),
            ]
            + [ANY] * len(filled),
            out_specs=[
                token_spec(group_feats, half, group),
                plain_spec(group_feats, half),
                plain_spec(1, columns),
                plain_spec(columns, size),
                plain_spec(size, columns),
            ],
            scratch_shapes=[
                pltpu.VMEM((keys, size), BF16),
                pltpu.VMEM((size, keys), BF16),
                pltpu.VMEM((1, columns), F32),
                pltpu.VMEM((1, columns), F32),
                pltpu.VMEM((size, columns), F32),
            ],
        ),
        out_shape=[
            jax.ShapeDtypeStruct((rows, 2, half, GROUPS * group_feats), BF16),
            pltpu.HBM((rows, 2, group_feats, half), BF16),
            pltpu.HBM((rows, 2, 1, columns), F32),
            pltpu.HBM((rows, 2, columns, size), BF16),
            pltpu.HBM((rows, 2, size, columns), BF16),
        ],
        compiler_params=pltpu.CompilerParams(
            dimension_semantics=("arbitrary", "arbitrary"), vmem_limit_bytes=40 << 20
        ),
        cost_estimate=pl.CostEstimate(
            flops=rows * 2 * columns * keys * size * 2,
            bytes_accessed=rows * (2 * keys * size + 8 * columns * size),
            transcendentals=rows * columns * keys,
        ),
        input_output_aliases={5: 0} if filled else {},
        name="attend",
    )(scalars, queries_t, lats, up_t, up_t, *filled)


def attend_back(
    scalars, queries_t, d_heads_t, heads_t, lats, up_t, kept, group, filled
):
    rows, half, group_feats, heads, columns, seq_count, size, keys = attention_sizes(
        queries_t, lats
    )
    logs, lifted, mixed = kept
    return pl.pallas_call(
        functools.partial(
            attend_back_kernel, seq_count=seq_count, half=half, heads=heads
        ),
        grid_spec=pltpu.PrefetchScalarGridSpec(
            num_scalar_prefetch=1,
            grid=(rows, 2),
            in_specs=[
                head_spec(group_feats, half, group),
                head_spec(group_feats, half, group),
                plain_spec(group_feats, half),
                lat_spec(lats),
                up_spec(group_feats, size, group),
                up_spec(group_feats, size, GROUPS + group),
                plain_spec(columns, size),
                plain_spec(size, columns),
                plain_spec(1, columns),
            ]
            + [ANY] * len(filled),
            out_specs=[
                token_spec(group_feats, half, group),
                lat_spec(lats),
                up_spec(group_feats, size, 0),
                up_spec(group_feats, size, 0),
            ],
            scratch_shapes=[
                pltpu.VMEM((keys, size), BF16),
                pltpu.VMEM((size, keys), BF16),
                pltpu.VMEM((keys, size), F32),
                pltpu.VMEM((columns, size), BF16),
                pltpu.VMEM((columns, size), BF16),
                pltpu.VMEM((1, columns), F32),
                pltpu.VMEM((size, columns), F32),
            ],
        ),
        out_shape=[
            jax.ShapeDtypeStruct((rows, 2, half, GROUPS * group_feats), BF16),
            jax.ShapeDtypeStruct(lats.shape, BF16),
            jax.ShapeDtypeStruct((group_feats, size), F32),
            jax.ShapeDtypeStruct((group_feats, size), F32),
        ],
        compiler_params=pltpu.CompilerParams(
            dimension_semantics=("arbitrary", "arbitrary"), vmem_limit_bytes=48 << 20
        ),
        cost_estimate=pl.CostEstimate(
            flops=rows * 5 * columns * keys * size * 2,
            bytes_accessed=rows * (4 * keys * size + 12 * columns * size),
            transcendentals=rows * columns * keys,
        ),
        input_output_aliases={10: 0} if filled else {},
        name="attend_back",
    )(
        scalars,
        *map(
            in_hbm, (queries_t, d_heads_t, heads_t, lats, up_t, up_t, lifted, mixed, logs)
        ),
        *filled,
    )


def rms_scale(value_rows):
    return lax.rsqrt(jnp.mean(value_rows * value_rows, axis=-1, keepdims=True) + 1e-06)


def norm_back(grad_in, value_rows, scale_rows, gain_vec):
    normed = value_rows * scale_rows
    upstream = grad_in * gain_vec
    return (
        scale_rows * (upstream - normed * jnp.mean(upstream * normed, axis=-1, keepdims=True)),
        jnp.sum(grad_in * normed, axis=0),
    )


def hidden_chunks(hidden, step):
    return [(at, min(step, hidden - at)) for at in range(0, hidden, step)]


class Copies:
    def __init__(self, sems, ahead):
        self.sems, self.made, self.begun, self.done, self.ahead = sems, [], 0, 0, ahead

    def add(self, source, target):
        self.made.append(pltpu.make_async_copy(source, target, self.sems.at[len(self.made)]))

    def begin(self, count):
        while self.begun < min(count, len(self.made)):
            self.made[self.begun].start()
            self.begun += 1

    def need(self, count):
        while self.done < count:
            self.made[self.done].wait()
            self.done += 1
            self.begin(self.done + self.ahead)


def feed_kernel(
    heads,
    state,
    bias,
    gain,
    next_gain,
    w_out,
    w_both,
    w_down,
    hidden_in,
    normed_mlp,
    gate,
    up,
    act,
    following,
    normed_next,
    v_heads,
    v_state,
    v_out,
    v_gate_w,
    v_up_w,
    v_down_w,
    v_normed,
    v_gate,
    v_up,
    v_act,
    v_next,
    v_normed_next,
    in_sems,
    out_sems,
    *,
    layer,
    hidden,
):
    chunks = hidden_chunks(hidden, FEED_STEP)
    loads, stores = Copies(in_sems, FEED_AHEAD), Copies(out_sems, 1)
    loads.add(heads, v_heads)
    loads.add(state, v_state)
    loads.add(w_out.at[layer], v_out)
    for at, count in chunks:
        cols = pl.ds(at, count)
        loads.add(w_both.at[layer, :, cols], v_gate_w.at[:, cols])
        loads.add(w_both.at[layer, :, pl.ds(hidden + at, count)], v_up_w.at[:, cols])
        loads.add(w_down.at[layer, cols, :], v_down_w.at[cols, :])
    loads.begin(FEED_AHEAD)
    loads.need(3)

    def store(source, target):
        stores.add(source, target)
        stores.begin(len(stores.made))

    value = v_state[...] + (dot(v_heads[...], v_out[...]) + bias[0])
    v_state[...] = value
    store(v_state, hidden_in)
    normed = (value * rms_scale(value) * gain[0]).astype(BF16)
    v_normed[...] = normed
    store(v_normed, normed_mlp)
    v_next[...] = value
    needed = 3
    for at, count in chunks:
        cols = pl.ds(at, count)
        loads.need(needed + 2)
        gate_part = dot(v_normed[...], v_gate_w[:, cols])
        up_part = dot(v_normed[...], v_up_w[:, cols])
        act_part = (gate_part * jax.nn.sigmoid(gate_part) * up_part).astype(BF16)
        v_gate[:, cols] = gate_part.astype(BF16)
        v_up[:, cols] = up_part.astype(BF16)
        v_act[:, cols] = act_part
        store(v_gate.at[:, cols], gate.at[:, cols])
        store(v_up.at[:, cols], up.at[:, cols])
        store(v_act.at[:, cols], act.at[:, cols])
        needed += 3
        loads.need(needed)
        v_next[...] += dot(act_part, v_down_w[cols, :])
    value = v_next[...]
    store(v_next, following)
    v_normed_next[...] = (value * rms_scale(value) * next_gain[0]).astype(BF16)
    store(v_normed_next, normed_next)
    stores.need(len(stores.made))


def vector_spec(at, width):
    return pl.BlockSpec((1, 1, width), lambda step: (at, 0, 0))


def feed(state, heads, layer, next_layer, weights):
    out_weight, out_bias, mlp_gain, attn_gain, gate_up_matrix, down_matrix = weights
    toks, width = state.shape
    hidden = down_matrix.shape[1]
    count = len(hidden_chunks(hidden, FEED_STEP))
    wide = lambda dtype: jax.ShapeDtypeStruct((toks, width), dtype)
    tiled = jax.ShapeDtypeStruct((toks, hidden), BF16)
    return pl.pallas_call(
        functools.partial(feed_kernel, layer=layer, hidden=hidden),
        grid=(1,),
        in_specs=[ANY] * 2
        + [vector_spec(layer, width), vector_spec(layer, width), vector_spec(next_layer, width)]
        + [ANY] * 3,
        out_specs=[ANY] * 7,
        out_shape=[wide(F32), wide(BF16), tiled, tiled, tiled, wide(F32), wide(BF16)],
        scratch_shapes=[
            pltpu.VMEM(heads.shape, BF16),
            pltpu.VMEM((toks, width), F32),
            pltpu.VMEM(out_weight.shape[1:], BF16),
            pltpu.VMEM((width, hidden), BF16),
            pltpu.VMEM((width, hidden), BF16),
            pltpu.VMEM((hidden, width), BF16),
            pltpu.VMEM((toks, width), BF16),
            pltpu.VMEM((toks, hidden), BF16),
            pltpu.VMEM((toks, hidden), BF16),
            pltpu.VMEM((toks, hidden), BF16),
            pltpu.VMEM((toks, width), F32),
            pltpu.VMEM((toks, width), BF16),
            pltpu.SemaphoreType.DMA((3 + 3 * count,)),
            pltpu.SemaphoreType.DMA((4 + 3 * count,)),
        ],
        compiler_params=pltpu.CompilerParams(
            dimension_semantics=("arbitrary",), vmem_limit_bytes=40 << 20
        ),
        cost_estimate=pl.CostEstimate(
            flops=2 * toks * width * (3 * hidden + width),
            bytes_accessed=2 * width * (3 * hidden + width) + 6 * toks * hidden,
            transcendentals=toks * hidden,
        ),
        name="feed",
    )(
        heads,
        state,
        out_bias[:, None],
        mlp_gain[:, None],
        attn_gain[:, None],
        out_weight,
        gate_up_matrix,
        down_matrix,
    )


def feed_back_kernel(
    grad,
    hidden_in,
    gain,
    gate,
    up,
    w_out,
    w_both,
    w_down,
    d_gate,
    d_up,
    d_mlp,
    d_hidden_in,
    d_attn,
    d_heads_t,
    gain_sum,
    bias_sum,
    v_grad,
    v_hidden_in,
    v_gate,
    v_up,
    v_out,
    v_gate_w,
    v_up_w,
    v_down_w,
    v_d_mlp,
    v_d_attn,
    v_d_heads,
    acc,
    in_sems,
    out_sems,
    *,
    layer,
    hidden,
    half,
):
    chunks = hidden_chunks(hidden, BACK_STEP)
    loads, stores = Copies(in_sems, BACK_AHEAD), Copies(out_sems, 1)
    loads.add(grad, v_grad)
    for at, count in chunks:
        cols = pl.ds(at, count)
        loads.add(gate.at[:, cols], v_gate.at[:, cols])
        loads.add(up.at[:, cols], v_up.at[:, cols])
        loads.add(w_down.at[layer, cols, :], v_down_w.at[cols, :])
        loads.add(w_both.at[layer, :, cols], v_gate_w.at[:, cols])
        loads.add(w_both.at[layer, :, pl.ds(hidden + at, count)], v_up_w.at[:, cols])
    loads.add(hidden_in, v_hidden_in)
    loads.add(w_out.at[layer], v_out)
    loads.begin(BACK_AHEAD)
    loads.need(1)

    def store(source, target):
        stores.add(source, target)
        stores.begin(len(stores.made))

    v_d_mlp[...] = v_grad[...].astype(BF16)
    store(v_d_mlp, d_mlp)
    needed = 1
    for at, count in chunks:
        cols = pl.ds(at, count)
        loads.need(needed + 3)
        d_act = dot_as(v_d_mlp[...], v_down_w[cols, :], NT)
        gate_part = v_gate[:, cols].astype(F32)
        up_part = v_up[:, cols].astype(F32)
        sig_gate = jax.nn.sigmoid(gate_part)
        d_gate_part = (d_act * up_part * sig_gate * (1.0 + gate_part * (1.0 - sig_gate))).astype(
            BF16
        )
        d_up_part = (d_act * gate_part * sig_gate).astype(BF16)
        v_gate[:, cols] = d_gate_part
        v_up[:, cols] = d_up_part
        store(v_gate.at[:, cols], d_gate.at[:, cols])
        store(v_up.at[:, cols], d_up.at[:, cols])
        needed += 5
        loads.need(needed)
        part = dot_as(d_gate_part, v_gate_w[:, cols], NT) + dot_as(d_up_part, v_up_w[:, cols], NT)
        if at == 0:
            acc[...] = part
        else:
            acc[...] += part
    loads.need(needed + 1)
    value = v_hidden_in[...]
    d_norm, gain_terms = norm_back(acc[...], value, rms_scale(value), gain[0])
    gain_sum[...] = gain_terms[None]
    total = v_grad[...] + d_norm
    low = total.astype(BF16)
    v_grad[...] = total
    store(v_grad, d_hidden_in)
    v_d_attn[...] = low
    store(v_d_attn, d_attn)
    bias_sum[...] = jnp.sum(low.astype(F32), axis=0, keepdims=True)
    loads.need(needed + 2)
    for piece in range(d_heads_t.shape[0]):
        v_d_heads[piece] = dot_as(v_out[...], low[piece * half : (piece + 1) * half], NT).astype(
            BF16
        )
    store(v_d_heads, d_heads_t)
    stores.need(len(stores.made))


def feed_back(grad, hidden_in, gate, up, layer, half, weights):
    out_weight, _, mlp_gain, _, gate_up_matrix, down_matrix = weights
    toks, width = grad.shape
    heads_dim = out_weight.shape[1]
    hidden = down_matrix.shape[1]
    vector_out = pl.BlockSpec((1, width), lambda step: (0, 0))
    wide = lambda dtype: jax.ShapeDtypeStruct((toks, width), dtype)
    tiled = jax.ShapeDtypeStruct((toks, hidden), BF16)
    pieces = toks // half
    count = len(hidden_chunks(hidden, BACK_STEP))
    return pl.pallas_call(
        functools.partial(feed_back_kernel, layer=layer, hidden=hidden, half=half),
        grid=(1,),
        in_specs=[ANY, ANY, vector_spec(layer, width)] + [ANY] * 5,
        out_specs=[ANY] * 6 + [vector_out] * 2,
        out_shape=[
            tiled,
            tiled,
            wide(BF16),
            wide(F32),
            wide(BF16),
            jax.ShapeDtypeStruct((pieces, heads_dim, half), BF16),
            jax.ShapeDtypeStruct((1, width), F32),
            jax.ShapeDtypeStruct((1, width), F32),
        ],
        scratch_shapes=[
            pltpu.VMEM((toks, width), F32),
            pltpu.VMEM((toks, width), F32),
            pltpu.VMEM((toks, hidden), BF16),
            pltpu.VMEM((toks, hidden), BF16),
            pltpu.VMEM(out_weight.shape[1:], BF16),
            pltpu.VMEM((width, hidden), BF16),
            pltpu.VMEM((width, hidden), BF16),
            pltpu.VMEM((hidden, width), BF16),
            pltpu.VMEM((toks, width), BF16),
            pltpu.VMEM((toks, width), BF16),
            pltpu.VMEM((pieces, heads_dim, half), BF16),
            pltpu.VMEM((toks, width), F32),
            pltpu.SemaphoreType.DMA((3 + 5 * count,)),
            pltpu.SemaphoreType.DMA((4 + 2 * count,)),
        ],
        compiler_params=pltpu.CompilerParams(
            dimension_semantics=("arbitrary",), vmem_limit_bytes=40 << 20
        ),
        cost_estimate=pl.CostEstimate(
            flops=2 * toks * width * (3 * hidden + heads_dim),
            bytes_accessed=2 * width * (3 * hidden + heads_dim) + 8 * toks * hidden,
            transcendentals=toks * hidden,
        ),
        name="feed_back",
    )(
        grad,
        hidden_in,
        mlp_gain[:, None],
        gate,
        up,
        out_weight,
        gate_up_matrix,
        down_matrix,
    )


def gated_sum_kernel(left_a, left_b, gate_a, gate_b, up_a, up_b, kept, sent):
    half_rows = kept.shape[0]

    def add(right_a, right_b):
        value = (dot(left_a[...], right_a[...]) + dot(left_b[...], right_b[...])).astype(BF16)
        kept[...] = value[:half_rows]
        sent[...] = value[half_rows:]

    first = pl.program_id(0) < pl.num_programs(0) // 2

    @pl.when(first)
    def _():
        add(gate_a, gate_b)

    @pl.when(jnp.logical_not(first))
    def _():
        add(up_a, up_b)


def gated_sum(lefts, gates, ups):
    rows, toks = lefts[0].shape
    hidden = gates[0].shape[1]
    tile = hidden // 2 if hidden % 256 == 0 else hidden
    count = hidden // tile
    whole = pl.BlockSpec((rows, toks), lambda step: (0, 0))
    gate_spec = pl.BlockSpec((toks, tile), lambda step: (0, jnp.minimum(step, count - 1)))
    up_spec_ = pl.BlockSpec((toks, tile), lambda step: (0, jnp.maximum(step - count, 0)))
    return pl.pallas_call(
        gated_sum_kernel,
        grid=(2 * count,),
        in_specs=[whole] * 2 + [gate_spec] * 2 + [up_spec_] * 2,
        out_specs=[pl.BlockSpec((rows // 2, tile), lambda step: (0, step))] * 2,
        out_shape=[jax.ShapeDtypeStruct((rows // 2, 2 * hidden), BF16)] * 2,
        compiler_params=pltpu.CompilerParams(
            dimension_semantics=("arbitrary",), vmem_limit_bytes=36 << 20
        ),
        cost_estimate=pl.CostEstimate(
            flops=8 * rows * toks * hidden,
            bytes_accessed=4 * hidden * (2 * toks + rows),
            transcendentals=0,
        ),
        name="gated_sum",
    )(*lefts, *gates, *ups)


def pair_sum_kernel(*refs, count):
    lefts, rights = refs[: 2 * count], refs[2 * count : 4 * count]
    kept, sent = refs[-2:]
    half_rows = kept.shape[0]
    at = 0
    for one in range(0, 2 * count, 2):
        cols = slice(at, at + rights[one].shape[1])
        value = (
            dot(lefts[one][...], rights[one][...]) + dot(lefts[one + 1][...], rights[one + 1][...])
        ).astype(BF16)
        kept[:, cols] = value[:half_rows]
        sent[:, cols] = value[half_rows:]
        at = cols.stop
    for extra in refs[4 * count : -2]:
        cols = slice(at, at + extra.shape[1])
        kept[:, cols] = extra[:half_rows]
        sent[:, cols] = extra[half_rows:]
        at = cols.stop


def pair_sum(terms, extras=()):
    rows, toks = terms[0][0][0].shape
    cols = sum(rights[0].shape[1] for _, rights in terms)
    total = cols + sum(value.shape[1] for value in extras)
    return pl.pallas_call(
        functools.partial(pair_sum_kernel, count=len(terms)),
        out_shape=[jax.ShapeDtypeStruct((rows // 2, total), BF16)] * 2,
        compiler_params=pltpu.CompilerParams(vmem_limit_bytes=36 << 20),
        cost_estimate=pl.CostEstimate(
            flops=4 * rows * toks * cols,
            bytes_accessed=4 * toks * cols + 2 * rows * total,
            transcendentals=0,
        ),
        name="pair_sum",
    )(*[left for lefts, _ in terms for left in lefts], *[r for _, rights in terms for r in rights], *extras)


class HalvingSum:
    def __init__(self, trade, pair, order):
        self.trade, self.order, self.step = trade, order, 1
        self.kept, self.sent = pair
        self.got = trade(self.sent, order[0])
        self.result = None

    def advance(self, gate=None):
        if self.result is not None:
            return
        kept, got = self.kept, self.got
        if gate is not None:
            (kept, got), _ = lax.optimization_barrier(((kept, got), gate))
        if self.step == len(self.order):
            self.result = kept.astype(F32) + got.astype(F32)
            return
        left = kept.shape[0] // 2
        self.sent = (kept[left:].astype(F32) + got[left:].astype(F32)).astype(BF16)
        self.kept = (kept[:left].astype(F32) + got[:left].astype(F32)).astype(BF16)
        self.got = self.trade(self.sent, self.order[self.step])
        self.step += 1

    def finish(self):
        while self.result is None:
            self.advance()
        return self.result


class SlotSum:
    result = None

    def __init__(self, trade, value, order):
        self.trade, self.value, self.order, self.step = trade, value, order, 0
        self.send()

    def send(self):
        left = self.value.shape[1] // 2
        self.kept, self.sent = self.value[:, :left], self.value[:, left:]
        self.got = self.trade(self.sent, self.order[self.step])
        self.step += 1

    def advance(self, gate):
        if self.got is None:
            return
        kept, got = self.kept, self.got
        if gate is not None:
            (kept, got), _ = lax.optimization_barrier(((kept, got), gate))
        self.value = (kept.astype(F32) + got.astype(F32)).astype(BF16)
        self.got = None
        if self.step < len(self.order):
            self.send()
        else:
            self.sent = self.value


def shards(
    tokens,
    cotangent,
    domain_ids,
    domain_counts,
    domain_weights,
    seq_cuts,
    attn_gain,
    query_weight,
    latent_weight,
    latent_up,
    out_weight,
    out_bias,
    mlp_gain,
    gate_up_matrix,
    down_matrix,
):
    seq_count = lax.axis_size("seq")
    rep_count = lax.axis_size("rep")
    place = lax.axis_index("seq").astype(jnp.int32)
    side = lax.axis_index("rep").astype(jnp.int32)
    seq_rows, loc_len, width = tokens.shape
    rows = seq_rows // rep_count
    half = loc_len // 2
    toks = rows * loc_len
    heads_dim = query_weight.shape[2]
    size = latent_up.shape[1]
    hidden = down_matrix.shape[1]
    group_cols = heads_dim // GROUPS
    bits = [1 << at for at in range(seq_count.bit_length() - 1)]
    far_late = bits[:1] + bits[2:3] + bits[1:2] + bits[3:]
    weights = (out_weight, out_bias, mlp_gain, attn_gain, gate_up_matrix, down_matrix)

    def after(value, gate):
        return lax.optimization_barrier((value, gate))[0]

    def swap_ends(value):
        moves = [(at, seq_count - 1 - at) for at in range(seq_count)]
        return lax.ppermute(value, "seq", moves)

    def across(value):
        return lax.ppermute(value, "rep", [(at, rep_count - 1 - at) for at in range(rep_count)])

    def trade(value, bit):
        return lax.ppermute(value, "seq", [(at, at ^ bit) for at in range(seq_count)])

    def rows_of(value, owner):
        return lax.dynamic_slice_in_dim(value, owner * rows, rows, 0)

    def turned(value):
        split = value.reshape((rows, 2, half) + value.shape[1:])
        return jnp.stack([split[:, 0], swap_ends(split[:, 1])], axis=1).reshape(value.shape)

    def tokens_of(value, owner):
        return rows_of(value, owner).reshape((toks,) + value.shape[2:])

    def spread(values, fill_at, fill):
        values = [value.reshape(rows, 1, loc_len, size) for value in values]
        filled = None
        for at, bit in enumerate(reversed(bits)):
            got = [trade(value, bit) for value in values]
            if at == fill_at:
                filled = fill(values)
                values, got = after((values, got), filled)
            values = [jnp.concatenate(pair, axis=1) for pair in zip(values, got)]
        return values, filled

    block = width // (seq_count * rep_count)
    kept_rows = seq_count * block
    row_at = jnp.arange(kept_rows, dtype=jnp.int32)
    col_at = jnp.arange(width, dtype=jnp.int32)

    def halving_step(order):
        distance = jnp.zeros_like(row_at)
        for level, bit in enumerate(order):
            distance = distance + (row_at // block // (seq_count // 2 >> level)) % 2 * bit
        return place ^ distance

    def picker(order, owner):
        source = (halving_step(order) * rep_count + owner) * block + row_at % block
        return (source[:, None] == col_at[None, :]).astype(BF16)

    pick, pick_late = picker(bits, side), picker(far_late, side)
    pick_other = picker(bits, rep_count - 1 - side)
    vector_at = jnp.arange(128, dtype=jnp.int32)[:, None]
    to_halving = (
        (halving_step(bits) * block + row_at % block)[:, None] == row_at[None, :]
    ).astype(BF16)

    def picked(picks, value):
        return dot_as(picks, value, NT).astype(BF16)

    domain_total = domain_counts.shape[0]
    all_tokens = seq_rows * loc_len * seq_count
    per_domain = domain_weights * (all_tokens / domain_total) / domain_counts.astype(F32)
    one_hot = (domain_ids[..., None] == jnp.arange(domain_total, dtype=jnp.int32)).astype(F32)
    row_scale = jnp.sum(one_hot * per_domain, axis=-1)
    pieces = jnp.arange(2 * seq_count, dtype=jnp.int32)

    def scalars_of(zigzag):
        source = pieces // 2
        if zigzag:
            source = jnp.where(pieces % 2 == 0, source, (2 * seq_count - 1 - pieces) // 2)
        distance = source ^ place
        slots = jnp.zeros_like(pieces)
        for level, bit in enumerate(bits):
            slots = slots + distance // bit % 2 * (seq_count // 2 >> level)
        starts = jnp.stack([place * loc_len, (2 * seq_count - 1 - 2 * place) * half])
        return jnp.concatenate([starts, slots, rows_of(seq_cuts, side)])

    def project_back(d_hidden_in, dq, d_lat, state, layer):
        d_normed = dot_as(dq, query_weight[layer], NT) + dot_as(d_lat, latent_weight[layer], NT)
        d_norm, g_gain = norm_back(d_normed, state, rms_scale(state), attn_gain[layer])
        return d_hidden_in + d_norm, g_gain

    def grad_of(owner, gate):
        value = tokens_of(cotangent, owner).astype(F32) * tokens_of(row_scale, owner)[:, None]
        split = value.reshape(rows, 2, half, width)
        swapped = swap_ends(after(split[:, 1].astype(BF16), gate))
        return jnp.stack([split[:, 0], swapped.astype(F32)], axis=1).reshape(toks, width)

    def first_normed(state):
        return (state * rms_scale(state) * attn_gain[0]).astype(BF16)

    natural_own = tokens_of(tokens, side)
    natural_normed = [first_normed(natural_own.astype(F32))]
    hidden_other = None
    saved = []
    for layer in range(LAYERS):
        last = layer == LAYERS - 1
        next_layer = min(layer + 1, LAYERS - 1)
        scalars = scalars_of(layer > 0)
        lat_input = normed_own if layer else natural_normed[0]
        lats = [
            dot(lat_input, latent_weight[layer, :, group * size : (group + 1) * size]).astype(BF16)
            for group in range(GROUPS)
        ]
        if layer == 0:
            lats, own = spread(
                lats, 2, lambda values: turned(after(natural_own, values)).astype(F32)
            )
            normed_own = first_normed(own)
        else:
            lats, hidden_other = spread(
                lats,
                0,
                lambda values: feed(
                    after(other, values), other_heads, layer - 1, next_layer, weights
                ),
            )
            saved[-1].append(hidden_other)
            other, normed_other = hidden_other[5:]
        queries_t = jnp.einsum(
            "rpid,df->rpfi",
            normed_own.reshape(rows, 2, half, width),
            query_weight[layer],
            preferred_element_type=F32,
        ).astype(BF16)
        up_t = latent_up[layer].T
        heads, attended = [], []
        for group in range(GROUPS):
            out, *rest = attend(scalars, queries_t, lats[group], up_t, group, heads)
            heads = [out]
            attended.append(rest)
            if group == 0:
                if last:
                    grad_own = grad_of(side, out)
                else:
                    natural_other = tokens_of(after(tokens, out), rep_count - 1 - side)
                    natural_normed.append(first_normed(natural_other.astype(F32)))
                    other = turned(natural_other)
        heads = heads[0].reshape(toks, heads_dim)
        other_heads = across(heads)
        if last:
            own, grad_own = after((own, grad_own), heads)
        else:
            own, other = after((own, other), heads)
            other = other.astype(F32)
        hidden_own = feed(own, heads, layer, next_layer, weights)
        saved.append([own, normed_own, heads, hidden_own, lats, queries_t, up_t, attended, scalars])
        saved[-1] += [other, normed_other if layer else None, other_heads]
        own, normed_own = hidden_own[5:]

    def placed(value, moved):
        both = jnp.stack([value, moved]).reshape(2, rows, loc_len, width)
        return jnp.where(side == 0, both, both[::-1]).reshape(seq_rows, loc_len, width)

    output = turned(own.astype(BF16))
    grad_other = None
    pending = []
    other_input = None
    layer_sums = []
    for layer in reversed(range(LAYERS)):
        last = layer == LAYERS - 1
        own, normed_own, heads, hidden_own, lats, queries_t, up_t, attended, scalars = saved[layer][:9]
        other, normed_other, other_heads = saved[layer][9:12]
        back_own = feed_back(
            grad_own, hidden_own[0], hidden_own[2], hidden_own[3], layer, half, weights
        )
        d_heads_t = back_own[5].reshape(rows, 2, heads_dim, half)
        d_in_own = back_own[3]
        d_lat, up_k, up_v, filled = [], [], [], []

        def stepped(gate):
            for late in d_lat:
                late.advance(gate)
            return [late.sent for late in d_lat]

        def sents_of(sums):
            return [one.sent if one.result is None else one.result for one in sums]

        def wide_sums(back_other, gate):
            backs = (back_own, back_other)
            hiddens = (hidden_own, hidden_other)
            gates, acts = after(([back[0] for back in backs], [hid[4] for hid in hiddens]), gate)
            gated = gated_sum(
                [picked(pick, hid[1]) for hid in hiddens], gates, [back[1] for back in backs]
            )
            plain = pair_sum(
                [
                    ([picked(pick_late, back[2]) for back in backs], acts),
                    ([picked(pick_late, back[4]) for back in backs], [heads, other_heads]),
                ]
            )
            return [HalvingSum(trade, gated, bits), HalvingSum(trade, plain, far_late)]

        def other_back(gate):
            return feed_back(
                after(grad_other, gate),
                hidden_other[0],
                hidden_other[2],
                hidden_other[3],
                layer,
                half,
                weights,
            )

        if last:
            d_heads_t = after(d_heads_t, output)
            output_moved = across(output)
        else:
            d_in_own = turned(d_in_own.astype(BF16)).astype(F32)
            hidden_other = saved[layer][12]
            grad_other, _ = project_back(*after(other_input, back_own[3]), layer + 1)
            back_other = other_back((back_own[3], pending[2].sent))
            for late in pending[:2]:
                late.advance(back_other[3])
            pending[2].advance(back_other[3])
            sums = wide_sums(back_other, (sents_of(pending), d_in_own))
            for late in pending[:2]:
                late.advance([sums[0].kept, sums[1].kept])
            for one in sums:
                one.advance(sents_of(pending[:2]))
            d_heads_t = after(d_heads_t, sents_of(sums + pending))
        for group in range(GROUPS):
            dq, d_lat_one, up_k_one, up_v_one = attend_back(
                scalars,
                queries_t,
                d_heads_t,
                attended[group][0],
                lats[group],
                up_t,
                attended[group][1:],
                group,
                filled,
            )
            up_k.append(up_k_one)
            up_v.append(up_v_one)
            for late in (pending if group == 0 else []) + d_lat:
                late.advance(up_k_one)
            d_lat.append(SlotSum(trade, d_lat_one, bits))
            sents = sents_of(pending + d_lat)
            filled = [dq]
            if group == 0:
                d_heads_t = after(d_heads_t, (sents, output_moved) if last else sents)
                if last:
                    grad_other = grad_of(rep_count - 1 - side, sents)
        dq = dq.reshape(toks, heads_dim)
        up_block = latent_up.shape[2] // (seq_count * rep_count)
        folds = up_block // block
        split = [value.reshape(-1, rep_count, up_block, size) for value in up_k + up_v]

        def up_of(owner):
            chosen = [lax.dynamic_index_in_dim(value, owner, 1, False) for value in split]
            return jnp.concatenate([value.astype(BF16) for value in chosen], axis=0)

        up_sent = up_of(rep_count - 1 - side)
        if last:
            grad_other = after(grad_other, dq)
            state, _ = after((other, grad_other), sents)
            dq_other = across(dq)
            hidden_other = feed(state, other_heads, layer, layer, weights)
            sents = stepped(hidden_other[0])
            dq_other = after(dq_other, hidden_other[0])
            up_got = across(up_sent)
            back_other = other_back(sents + [dq_other, up_sent])
            sents = stepped(back_other[3])
            up_got = after(up_got, back_other[3])
            sums = wide_sums(back_other, sents + [up_got])
            sents = stepped([sums[0].kept, sums[1].kept])
            for one in sums:
                one.advance(sents)
            stepped(sents_of(sums))
        else:
            pending[2].advance(up_k[-1])
            sents = stepped(up_k[-1])
            sums[1].advance(sents)
            dq, up_sent = after((dq, up_sent), sums[1].sent)
            dq = turned(dq)
            up_got = across(up_sent)
            sents = stepped((sums[1].sent, dq))
            sums[0].advance(sents)
            dq_other = across(dq)
            pending[2].advance(sents)
            sents = stepped(sums[0].sent)
            up_got = after(up_got, sents)
        while any(late.got is not None for late in d_lat):
            stepped(None)
        d_lat = jnp.concatenate([late.value.reshape(toks, size) for late in d_lat], axis=1)
        d_lat_other = across(d_lat)
        if not last:
            for one in (sums[1], sums[0]):
                one.advance(d_lat)
        state = own if layer else natural_own.astype(F32)
        grad_own, attn_gain_own = project_back(d_in_own, dq, d_lat, state, layer)
        if last:
            other_input = (back_other[3], dq_other, d_lat_other, other)
        normed = [
            picked(pick, value)
            for value in ((normed_own, normed_other) if layer else natural_normed)
        ]

        up_rows = (up_of(side).astype(F32) + up_got.astype(F32)).astype(BF16)
        up_rows = jnp.concatenate(
            [up_rows[:, at * block : (at + 1) * block] for at in range(folds)], axis=2
        ).reshape(kept_rows, folds * size)
        up_rows = dot(to_halving, up_rows).astype(BF16)
        vectors = jnp.where(
            vector_at == 0,
            back_own[6] + back_other[6],
            jnp.where(
                vector_at == 1,
                back_own[7] + back_other[7],
                jnp.where(vector_at == 2, attn_gain_own[None], 0.0),
            ),
        )
        vectors_other = jnp.where(vector_at == 3, attn_gain_own[None], 0.0)
        vectors = (
            dot_as(pick, vectors.astype(BF16), NT) + dot_as(pick_other, vectors_other.astype(BF16), NT)
        ).astype(BF16)
        terms = [(normed, [dq, dq_other]), (normed, [d_lat, d_lat_other])]
        rest = HalvingSum(trade, pair_sum(terms, [up_rows, vectors]), bits)
        if not last:
            for _ in bits[1:]:
                rest.advance(None)
            for one in (sums[1], sums[0]):
                while one.result is None:
                    one.advance(rest.sent)
        sums.append(rest)
        pending = sums
        layer_sums.insert(0, sums)
    layer_grads, other_gains = [], []
    for sums in layer_sums:
        g_gate_up, g_plain, g_rest = [one.finish() for one in sums]
        lat_at, up_at = heads_dim, heads_dim + GROUPS * size
        vectors_at = up_at + folds * size
        g_up = jnp.concatenate(
            [g_rest[:, up_at + at * size : up_at + (at + 1) * size] for at in range(folds)]
        )
        other_gains.append(g_rest[:, vectors_at + 3])
        layer_grads.append(
            (
                g_rest[:, vectors_at + 2],
                g_rest[:, :lat_at],
                g_rest[:, lat_at:up_at],
                g_up.T,
                g_plain[:, hidden:].T,
                g_rest[:, vectors_at + 1],
                g_rest[:, vectors_at],
                g_gate_up,
                g_plain[:, :hidden].T,
            )
        )
    stacked = [jnp.stack([grads[member] for grads in layer_grads]) for member in range(9)]
    stacked[0] = stacked[0] + across(jnp.stack(other_gains))
    input_grad = grad_own.astype(BF16)
    return (
        placed(output, output_moved),
        placed(input_grad, across(input_grad)),
        *stacked,
    )


def solution(mesh):
    rows = P(None, "seq", None)
    scattered = P(None, ("seq", "rep"))
    first = P(None, ("seq", "rep"), None)
    second = P(None, None, ("seq", "rep"))
    return jax.shard_map(
        shards,
        mesh=mesh,
        in_specs=(rows, rows, P(None, "seq")) + (P(),) * 12,
        out_specs=(
            rows,
            rows,
            scattered,
            first,
            first,
            second,
            second,
            scattered,
            scattered,
            first,
            second,
        ),
        check_vma=False,
    )
```
